128 devices in a mesh: seq: 8 (over x, core), grp: 16 (over z, y).
Axes of the slice: x: 4, y: 4, z: 4, core: 2. Of those that a mesh axis runs over, the one named last changes fastest.
Arguments:
- tokens: bfloat16 [16, 1024, 1536], P('grp', 'seq'), may hold values from -15 to 15
- lengths: int32 [16, 3], P('grp'), may hold values from 1 to 512, 1024 in all within a row
- prompt_adapter: int32 [16, 3], P('grp'), may hold values from 0 to 15
- routes: int32 [16, 1024, 8], P('grp', 'seq'), may hold values from 0 to 39, all different within a row; in each aligned block of 128 rows (0 to 127, 128 to 255, ..., all dimensions but the last counted through in order) at most 40 rows name the same one
- routing_weight: float32 [16, 1024, 8], P('grp', 'seq'), may hold values from 0.1 to 1
- attention_gain: float32 [1536], replicated, may hold values from 0.5 to 1.5
- query_weight: bfloat16 [1536, 1536], replicated, may hold values from -25 to 25
- key_weight: bfloat16 [1536, 512], replicated, may hold values from -0.15625 to 0.15625
- value_weight: bfloat16 [1536, 512], replicated, may hold values from -0.15625 to 0.15625
- output_weight: bfloat16 [1536, 1536], replicated, may hold values from -0.15625 to 0.15625
- adapter_down_maps: bfloat16 [4, 16, 1536, 16], P(None, 'grp'), may hold values from -0.15625 to 0.15625
- adapter_up_query_output: bfloat16 [2, 16, 16, 1536], P(None, 'grp'), may hold values from -1.5 to 1.5
- adapter_up_key_value: bfloat16 [2, 16, 16, 512], P(None, 'grp'), may hold values from -1.5 to 1.5
- expert_gain: float32 [1536], replicated, may hold values from 0.5 to 1.5
- gate_weight: bfloat16 [80, 1536, 256], P('grp'), may hold values from -0.15625 to 0.15625
- up_weight: bfloat16 [80, 1536, 256], P('grp'), may hold values from -0.15625 to 0.15625
- down_weight: bfloat16 [80, 256, 1536], P('grp'), may hold values from -0.25 to 0.25
- closing_gain: float32 [1536], replicated, may hold values from 0.5 to 1.5
- vocab_projection: bfloat16 [1536, 49152], P(None, ('seq', 'grp')), may hold values from -10 to 10
Outputs:
- hidden_out: bfloat16 [16, 1024, 1536], P('grp', 'seq')
- log_probs: float32 [48, 49152], P(None, ('seq', 'grp'))
The draws below stay inside these ranges and needn't reach their ends.
Inputs may be any that keep to these rules, and one draw needn't show every extreme that they name: The 3 lengths of a group sum to 1024; the longest is exactly 512. `routes`: A token names 8 different experts. Within the 128 tokens of one device no expert is named by more than 40 of them, and in every draw some expert is named by exactly 40 tokens of some device.
All inputs are finite; a program needn't handle non-finite values.
Results may differ from the reference program's by a relative error of at most 0.017.
The reference program's roundings to bfloat16 on the way count: a program that leaves them out, or rounds other values in their place, can miss the bound.
Values may be sent and summed in bfloat16 or wider, within the bound.
No kernel may reach another device: no remote copies, remote signals or barrier semaphores. Data moves between devices by JAX's collectives and lax.ppermute only.
A program may use at most 192 MiB of HBM per device.

```python
import math
import jax
import jax.numpy as jnp
import numpy as np
from jax import lax

MODEL_DIM = 1536
HEADS = 24
KV_HEADS = 8
HEAD = 64
EXPERTS = 40
EXPERT_FF = 512
TOP = 8
VOCAB = 49152
ADAPTER_RANK = 16
SEQS = 3
TOK_DEV = 128
GROUPS = 16
GROUP_TOK = 1024
ADAPTER_COUNT = 16
KEY_WIDTH = 512
HALF = 256
SLICES = 80
CAP = 40
ENDS = 48
N_SEQ = 8
N_GRP = 16


def draw_tokens(key, part):
    key_values, key_matrix = jax.random.split(key, 2)
    shape = (GROUPS, GROUP_TOK, MODEL_DIM)
    row_scale = jnp.exp(jax.random.uniform(key_matrix, (GROUPS, GROUP_TOK, 1), jnp.float32, jnp.log(0.3), jnp.log(3.0)))
    features = jnp.clip(jax.random.normal(key_values, shape, jnp.float32), -5.0, 5.0)
    return (features * row_scale).astype(jnp.bfloat16)


def draw_query_weight(key, part):
    key_values = jax.random.fold_in(key, 0)
    shape = (MODEL_DIM, HEADS * HEAD)
    features = jnp.clip(jax.random.normal(key_values, shape, jnp.float32), -5.0, 5.0)
    return (features * MODEL_DIM ** (-0.5)).astype(jnp.bfloat16)


def draw_vocab_projection(key, part):
    columns = 0.5 + jnp.arange(VOCAB, dtype=jnp.float32)[None, :] / VOCAB
    features = jnp.clip(jax.random.normal(key, (MODEL_DIM, VOCAB), jnp.float32), -5.0, 5.0) * 4.0
    return (features * columns * MODEL_DIM ** (-0.5)).astype(jnp.bfloat16)


def plant(entries, rng, least, largest):
    longest = entries.shape.index(max(entries.shape))
    spots = []
    for shift in (0, 1):
        where = [jax.random.randint(jax.random.fold_in(rng, axis), (), 0, length) for axis, length in enumerate(entries.shape)]
        where[longest] = (where[longest] + shift) % entries.shape[longest]
        spots.append(tuple(where))
    return entries.at[spots[0]].set(least).at[spots[1]].set(largest)


def block_levels(stream_key, shape, cuts, low, high):
    factor_of, own = 1.0, jax.random.fold_in(stream_key, 6)
    for position, blocks in cuts:
        draws = jnp.exp(jax.random.uniform(jax.random.fold_in(own, position), (blocks,), jnp.float32, low / len(cuts), high / len(cuts)))
        factor_of = factor_of * jnp.repeat(draws, shape[position] // blocks).reshape([-1 if axis == position else 1 for axis in range(len(shape))])
    return factor_of


def split_up(number_of, total, bound, slope):
    weights = [(1 << 20) // math.isqrt(standing ** slope) + 1 for standing in range(2, number_of + 1)]
    spare, given = total - bound - (number_of - 1), [1] * (number_of - 1)
    while spare > 0:
        candidates = [i for i in range(number_of - 1) if given[i] < bound]
        mass, budget = sum([weights[i] for i in candidates]), spare
        for i in candidates:
            addition = min(bound - given[i], max(1, budget * weights[i] // mass), spare)
            given[i] = given[i] + addition
            spare = spare - addition
    return np.array([bound] + given)


def uneven(key, amount, total, most, slope):
    if amount == 2:
        one = jax.random.randint(key, (), max(1, total - most), min(most, total - 1) + 1)
        return jnp.stack([one, total - one])
    sizes = jnp.asarray(split_up(amount, total, most, slope), jnp.int32)
    twos = (amount - 1) // 2
    giver, receiver = sizes[1:1 + 2 * twos:2], sizes[2:2 + 2 * twos:2]
    room = jnp.minimum(giver - 1, most - receiver)
    shifted = jax.random.randint(jax.random.fold_in(key, 1), (twos,), 0, 1 << 20) % (room + 1)
    sizes = sizes.at[1:1 + 2 * twos:2].set(giver - shifted).at[2:2 + 2 * twos:2].set(receiver + shifted)
    return sizes[jax.random.permutation(jax.random.fold_in(key, 2), amount)]


def routed_block(key, own, number, rows, number_of, top, bound, lean):
    sequence = jax.random.permutation(key, number_of)
    crowded, usual = portions_of(number_of, rows * top, bound, lean, True), portions_of(number_of, rows * top, bound, lean, False)
    places = jnp.arange(number_of)

    def named(tallies, offset_by):
        used = int((tallies > 0).sum())
        fixed = max(1, used // 4)
        passed = fixed + (places - fixed + offset_by * (used - fixed)) % max(1, number_of - fixed)
        return jnp.zeros((number_of,), jnp.int32).at[sequence[jnp.where(places < fixed, places, passed)]].set(jnp.asarray(tallies, jnp.int32))

    tallies = jnp.where(number % 4 == 0, named(crowded, number // 4), named(usual, number - number // 4 - 1))
    mixed = jax.random.permutation(jax.random.fold_in(own, 3), number_of)
    giver, sink = mixed[0:number_of // 2 * 2:2], mixed[1:number_of // 2 * 2:2]
    margin = jnp.minimum(tallies[giver] - 1, bound - tallies[sink]) // 2
    margin = jnp.where((giver == sequence[0]) | (sink == sequence[0]) | (tallies[sink] == 0), 0, jnp.maximum(margin, 0))
    passed = jax.random.randint(jax.random.fold_in(own, 4), (number_of // 2,), 0, 1 << 20) % (margin + 1)
    tallies = tallies.at[giver].add(-passed).at[sink].add(passed)
    items = jnp.searchsorted(jnp.cumsum(tallies), jnp.arange(rows * top), side="right").astype(jnp.int32)
    listing = items.reshape(top, rows).T
    listing = listing[jax.random.permutation(jax.random.fold_in(own, 1), rows)]
    offset_by = jax.random.randint(jax.random.fold_in(own, 2), (rows, 1), 0, top)
    return jnp.take_along_axis(listing, (jnp.arange(top)[None, :] + offset_by) % top, axis=1)


def portions_of(amount, total, reach, skew, full):
    weights = [(1 << 20) // math.isqrt(standing ** skew) + 1 for standing in range(1, amount + 1)]
    largest = reach if full else min(reach, max(-(-total // amount), total * weights[0] // sum(weights)))
    least = 1 if total - largest >= amount - 1 else 0
    holding, rest = [largest] + [least] * (amount - 1), total - largest - least * (amount - 1)
    while rest > 0:
        movable = [i for i in range(1, amount) if holding[i] < largest] or [i for i in range(1, amount) if holding[i] < reach]
        whole, left = sum([weights[i] for i in movable]), rest
        for i in movable:
            extra = min(reach - holding[i], max(1, left * weights[i] // whole), rest)
            holding[i] = holding[i] + extra
            rest = rest - extra
    return np.array(holding)


def centred(rng, dims, scale, reach, cuts=(), kind=jnp.bfloat16):
    values = jax.random.normal(rng, dims, jnp.float32) * scale
    if len(cuts) > 0:
        values = block_levels(rng, dims, cuts, -0.22, 0.18) * values
    return jnp.clip(values, min=-reach, max=reach).astype(kind)


def setup_inputs(seed: int = 0) -> dict:
    splits = jax.random.split(jax.random.key(seed), 20)
    tokens = draw_tokens(jax.random.fold_in(splits[19], 71), 0)
    lengths = jax.vmap(lambda own: uneven(own, SEQS, GROUP_TOK, GROUP_TOK // 2, 2))(jax.random.split(splits[1], GROUPS)).reshape((GROUPS, SEQS)).astype(jnp.int32)
    prompt_adapter = plant(jax.random.randint(splits[2], (GROUPS, SEQS), 0, ADAPTER_COUNT), jax.random.fold_in(splits[2], 1), 0, ADAPTER_COUNT - 1).astype(jnp.int32)
    routes_keys = jax.random.split(jax.random.fold_in(splits[3], 1), GROUPS * GROUP_TOK // TOK_DEV)
    routes_turns = jax.random.permutation(jax.random.fold_in(splits[3], 3), GROUPS * GROUP_TOK // TOK_DEV)
    routes = jax.vmap(lambda own, number: routed_block(jax.random.fold_in(splits[3], 2), own, number, TOK_DEV, EXPERTS, TOP, CAP, 1))(routes_keys, routes_turns).reshape((GROUPS, GROUP_TOK, TOP))
    routing_weight = jnp.clip(jnp.exp(math.log(1.0) - 2.3025851 * jax.random.uniform(splits[4], (GROUPS, GROUP_TOK, TOP), jnp.float32) ** block_levels(splits[4], (GROUPS, GROUP_TOK, TOP), ((0, 16), (1, 8)), -0.2, 0.2)), 0.1, 1.0)
    attention_gain = jnp.clip(1.0 + 0.1 * jax.random.normal(splits[5], (MODEL_DIM,), jnp.float32), 0.5, 1.5)
    query_weight = draw_query_weight(jax.random.fold_in(splits[19], 71), 0)
    key_weight = centred(splits[7], (MODEL_DIM, KEY_WIDTH), MODEL_DIM ** -0.5, 0.15625)
    value_weight = centred(splits[8], (MODEL_DIM, KEY_WIDTH), MODEL_DIM ** -0.5, 0.15625)
    output_weight = centred(splits[9], (HEADS * HEAD, MODEL_DIM), (HEADS * HEAD) ** -0.5, 0.15625)
    adapter_down_maps = centred(splits[10], (4, ADAPTER_COUNT, MODEL_DIM, ADAPTER_RANK), MODEL_DIM ** -0.5, 0.15625, ((1, 16),))
    adapter_up_query_output = centred(splits[11], (2, ADAPTER_COUNT, ADAPTER_RANK, MODEL_DIM), ADAPTER_RANK ** -0.5, 1.5, ((1, 16),))
    adapter_up_key_value = centred(splits[12], (2, ADAPTER_COUNT, ADAPTER_RANK, KEY_WIDTH), ADAPTER_RANK ** -0.5, 1.5, ((1, 16),))
    expert_gain = jnp.clip(1.0 + 0.1 * jax.random.normal(splits[13], (MODEL_DIM,), jnp.float32), 0.5, 1.5)
    gate_weight = centred(splits[14], (SLICES, MODEL_DIM, HALF), MODEL_DIM ** -0.5, 0.15625, ((0, 16),))
    up_weight = centred(splits[15], (SLICES, MODEL_DIM, HALF), MODEL_DIM ** -0.5, 0.15625, ((0, 16),))
    down_weight = centred(splits[16], (SLICES, HALF, MODEL_DIM), EXPERT_FF ** -0.5, 0.25, ((0, 16),))
    closing_gain = jnp.clip(1.0 + 0.1 * jax.random.normal(splits[17], (MODEL_DIM,), jnp.float32), 0.5, 1.5)
    vocab_projection = draw_vocab_projection(jax.random.fold_in(splits[19], 71), 0)
    return {"tokens": tokens, "lengths": lengths, "prompt_adapter": prompt_adapter, "routes": routes, "routing_weight": routing_weight, "attention_gain": attention_gain, "query_weight": query_weight, "key_weight": key_weight, "value_weight": value_weight, "output_weight": output_weight, "adapter_down_maps": adapter_down_maps, "adapter_up_query_output": adapter_up_query_output, "adapter_up_key_value": adapter_up_key_value, "expert_gain": expert_gain, "gate_weight": gate_weight, "up_weight": up_weight, "down_weight": down_weight, "closing_gain": closing_gain, "vocab_projection": vocab_projection}


EPSILON = 1e-05
ROPE_BASE = 10000.0
MASKED = -1e+30

def rms_scaled(features, scales):
    features = features.astype(jnp.float32)
    inverse = lax.rsqrt(lax.optimization_barrier(jnp.mean(features * features, axis=-1, keepdims=True)) + EPSILON)
    return (features * inverse * scales).astype(jnp.bfloat16)

def rotate(features, offsets):
    half_size = features.shape[-1] // 2
    frequency = ROPE_BASE ** (-jnp.arange(half_size, dtype=jnp.float32) / half_size)
    angles = offsets.astype(jnp.float32)[:, None, None] * frequency[None, None, :]
    cosine = jnp.cos(angles)
    sines = jnp.sin(angles)
    first_half = features[..., :half_size]
    second = features[..., half_size:]
    return jnp.concatenate([first_half * cosine - second * sines, second * cosine + first_half * sines], axis=-1)

def doc_layout(prompt_lens, row_index):
    doc_ends = jnp.cumsum(prompt_lens).astype(jnp.int32)
    starts = (doc_ends - prompt_lens).astype(jnp.int32)
    document = lax.optimization_barrier(jnp.sum((row_index[:, None] >= doc_ends[None, :]).astype(jnp.int32), axis=1)).astype(jnp.int32)
    member = document[:, None] == jnp.arange(prompt_lens.shape[0], dtype=jnp.int32)[None, :]
    doc_start = lax.optimization_barrier(jnp.sum(jnp.where(member, starts[None, :], 0), axis=1)).astype(jnp.int32)
    return (document, (row_index - doc_start).astype(jnp.int32), member)

def adapter_delta(normalized_rows, selected_experts, down_proj, up_weights):
    low_rank = jnp.einsum('td,adr->tar', normalized_rows.astype(jnp.float32), down_proj.astype(jnp.float32))
    low_rank = (low_rank * selected_experts[:, :, None]).astype(jnp.bfloat16)
    low_rank = lax.optimization_barrier(low_rank).astype(jnp.float32)
    return jnp.einsum('tar,are->te', low_rank, up_weights.astype(jnp.float32))

def reference(tokens, lengths, prompt_adapter, routes, routing_weight, attention_gain, query_weight, key_weight, value_weight, output_weight, adapter_down_maps, adapter_up_query_output, adapter_up_key_value, expert_gain, gate_weight, up_weight, down_weight, closing_gain, vocab_projection):
    ratio = HEADS // KV_HEADS
    logit_scale = HEAD ** (-0.5)

    def group_layer(group_args):
        rows_in, prompt_lens, owners = group_args
        row_index = jnp.arange(GROUP_TOK, dtype=jnp.int32)
        document, offsets, member = doc_layout(prompt_lens, row_index)
        adapter = owners[document]
        selected_experts = (adapter[:, None] == jnp.arange(ADAPTER_COUNT, dtype=jnp.int32)[None, :]).astype(jnp.float32)
        normalized_rows = rms_scaled(rows_in, attention_gain)
        query_matrix = jnp.dot(normalized_rows, query_weight, preferred_element_type=jnp.float32) + adapter_delta(normalized_rows, selected_experts, adapter_down_maps[0], adapter_up_query_output[0])
        query_matrix = rotate(query_matrix.reshape(GROUP_TOK, HEADS, HEAD), offsets).astype(jnp.bfloat16)
        key_matrix = jnp.dot(normalized_rows, key_weight, preferred_element_type=jnp.float32) + adapter_delta(normalized_rows, selected_experts, adapter_down_maps[1], adapter_up_key_value[0])
        key_matrix = rotate(key_matrix.reshape(GROUP_TOK, KV_HEADS, HEAD), offsets).astype(jnp.bfloat16)
        value_matrix = (jnp.dot(normalized_rows, value_weight, preferred_element_type=jnp.float32) + adapter_delta(normalized_rows, selected_experts, adapter_down_maps[2], adapter_up_key_value[1])).astype(jnp.bfloat16)
        grouped_queries = query_matrix.reshape(GROUP_TOK, KV_HEADS, ratio, HEAD).astype(jnp.float32)
        attention_logits = jnp.einsum('jhlv,phv->hljp', grouped_queries, key_matrix.astype(jnp.float32)) * logit_scale
        allowed = (document[:, None] == document[None, :]) & (row_index[None, :] <= row_index[:, None])
        attention_logits = jnp.where(allowed[None, None], attention_logits, MASKED)
        running_max = lax.optimization_barrier(jnp.max(attention_logits, axis=-1, keepdims=True))
        weights = jnp.where(allowed[None, None], jnp.exp(attention_logits - running_max), 0.0)
        running_totals = lax.optimization_barrier(jnp.sum(weights, axis=-1))
        attention_weights = lax.optimization_barrier(weights.astype(jnp.bfloat16)).astype(jnp.float32)
        head_values = value_matrix.reshape(GROUP_TOK, KV_HEADS, HEAD).astype(jnp.float32)
        weighted_values = jnp.einsum('ukoe,euh->ukoh', attention_weights, head_values) / running_totals[..., None]
        attention_output = weighted_values.transpose(2, 0, 1, 3).reshape(GROUP_TOK, HEADS * HEAD).astype(jnp.bfloat16)
        outside_mask = jnp.dot(attention_output, output_weight, preferred_element_type=jnp.float32) + adapter_delta(attention_output, selected_experts, adapter_down_maps[3], adapter_up_query_output[1])
        return (rows_in.astype(jnp.float32) + outside_mask).astype(jnp.bfloat16)
    mixed_rows = lax.map(group_layer, (tokens, lengths, prompt_adapter))
    blocks = GROUPS * N_SEQ
    per_holder = SLICES // N_GRP
    moe_in = rms_scaled(mixed_rows, expert_gain).reshape(blocks, TOK_DEV, MODEL_DIM)
    gate_all = gate_weight.astype(jnp.float32).reshape(EXPERTS, 2, MODEL_DIM, HALF)
    up_all = up_weight.astype(jnp.float32).reshape(EXPERTS, 2, MODEL_DIM, HALF)
    down_all = down_weight.astype(jnp.float32).reshape(EXPERTS, 2, HALF, MODEL_DIM)

    def expert_block(block_args):
        normalized_rows, expert_route, route_weight = block_args
        expert_ids = expert_route.reshape(-1)
        onehot = (expert_ids[:, None] == jnp.arange(EXPERTS, dtype=jnp.int32)[None, :]).astype(jnp.int32)
        slot_index = lax.optimization_barrier(jnp.sum((jnp.cumsum(onehot, axis=0) - onehot) * onehot, axis=1)).astype(jnp.int32)
        source_row = (jnp.arange(TOK_DEV * TOP, dtype=jnp.int32) // TOP).astype(jnp.int32)
        slot_table = jnp.full((EXPERTS * CAP,), TOK_DEV, jnp.int32).at[expert_ids * CAP + slot_index].set(source_row)
        padded = jnp.concatenate([normalized_rows, jnp.zeros((1, MODEL_DIM), jnp.bfloat16)], axis=0)
        expert_rows = padded[slot_table].reshape(EXPERTS, CAP, MODEL_DIM).astype(jnp.float32)
        gate_proj = jnp.einsum('ecd,ehdf->ehcf', expert_rows, gate_all)
        up_proj = jnp.einsum('ecd,ehdf->ehcf', expert_rows, up_all)
        hidden = (jax.nn.silu(gate_proj) * up_proj).astype(jnp.bfloat16)
        hidden = lax.optimization_barrier(hidden).astype(jnp.float32)
        halves = jnp.einsum('ehcf,ehfd->ehcd', hidden, down_all).astype(jnp.bfloat16)
        halves = halves.reshape(EXPERTS * 2 * CAP, MODEL_DIM)
        slice_ids = (2 * expert_ids[:, None] + jnp.arange(2, dtype=jnp.int32)[None, :]).astype(jnp.int32)
        pick_index = (slice_ids * CAP + slot_index[:, None]).astype(jnp.int32)
        picked = halves[pick_index].astype(jnp.float32).reshape(TOK_DEV, TOP * 2, MODEL_DIM)
        holder = slice_ids // per_holder
        holder_hot = (holder[:, :, None] == jnp.arange(N_GRP, dtype=jnp.int32)[None, None, :]).astype(jnp.float32)
        holder_hot = (holder_hot * route_weight.reshape(-1)[:, None, None]).reshape(TOK_DEV, TOP * 2, N_GRP)
        partial_value = jnp.einsum('tkg,tkd->tgd', holder_hot, picked, precision=lax.Precision.HIGHEST).astype(jnp.bfloat16)
        partial_value = lax.optimization_barrier(partial_value).astype(jnp.float32)
        return lax.optimization_barrier(jnp.sum(partial_value, axis=1))
    combined = lax.map(expert_block, (moe_in, routes.reshape(blocks, TOK_DEV, TOP), routing_weight.reshape(blocks, TOK_DEV, TOP)))
    hidden_out = (mixed_rows.astype(jnp.float32) + combined.reshape(GROUPS, GROUP_TOK, MODEL_DIM)).astype(jnp.bfloat16)
    last_index = (jnp.cumsum(lengths, axis=1) - 1).astype(jnp.int32)
    last_rows = jnp.take_along_axis(hidden_out, jnp.broadcast_to(last_index[:, :, None], (GROUPS, SEQS, MODEL_DIM)), axis=1)
    final_rows = rms_scaled(last_rows.reshape(ENDS, MODEL_DIM), closing_gain)
    logits = jnp.dot(final_rows, vocab_projection, preferred_element_type=jnp.float32)
    running_max = lax.optimization_barrier(jnp.max(logits, axis=1, keepdims=True))
    log_probs = logits - (running_max + jnp.log(lax.optimization_barrier(jnp.sum(jnp.exp(logits - running_max), axis=1, keepdims=True))))
    return (hidden_out, log_probs)
```

```python
import jax
import jax.numpy as jnp
from jax import lax
from jax.experimental import pallas as pl
from jax.experimental.pallas import tpu as pltpu
from jax.sharding import PartitionSpec as P

HEADS = 24
KV_HEADS = 8
HEAD = 64
EXPERTS = 40
TOP = 8
SLOTS = 48
EPSILON = 1e-05
ROPE_BASE = 10000.0
MASKED = -1e30
SIDE = 4
BF = jnp.bfloat16
F32 = jnp.float32
WHOLE = ("seq", "grp")


def shift(rows, axis, step):
    if axis == "z":
        pairs = [(i, (i // SIDE + step) % SIDE * SIDE + i % SIDE) for i in range(16)]
    else:
        pairs = [(i, i // SIDE * SIDE + (i % SIDE + step) % SIDE) for i in range(16)]
    return lax.ppermute(rows, "grp", pairs)


def partner(rows):
    return lax.ppermute(rows, "seq", [(s, s ^ 1) for s in range(8)])


def gather_tokens(first, second):
    near = [shift(first, "y", 1), shift(second, "z", 1), shift(first, "y", -1),
            shift(second, "z", -1), shift(first, "y", 2), shift(second, "z", 2)]
    near = lax.optimization_barrier(near)
    plane_a = jnp.stack([first, near[0], near[2], near[4]])
    plane_b = jnp.stack([second, near[1], near[3], near[5]])
    far = [shift(plane_a, "z", 1), shift(plane_b, "y", 1), shift(plane_a, "z", -1),
           shift(plane_b, "y", -1)]
    far = lax.optimization_barrier(far)
    last = [shift(far[0][:2], "z", 1), shift(far[1][:2], "y", 1),
            shift(far[2][2:], "z", -1), shift(far[3][2:], "y", -1)]
    return ([plane_a, far[0], far[2], last[0], last[2]],
            [plane_b, far[1], far[3], last[1], last[3]])


def reduce_tokens(parts_a, parts_b):
    def wide(v):
        return v.astype(F32)

    far = [shift(parts_a[3][:2], "z", 1), shift(parts_b[3][:2], "y", 1),
           shift(parts_a[3][2:], "z", -1), shift(parts_b[3][2:], "y", -1)]
    far = lax.optimization_barrier(far)

    def relay(parts, down, up):
        plus = jnp.concatenate([(wide(parts[2][:2]) + wide(down)).astype(BF), parts[2][2:]])
        minus = jnp.concatenate([parts[1][:2], (wide(parts[1][2:]) + wide(up)).astype(BF)])
        return plus, minus

    plus_a, minus_a = relay(parts_a, far[0], far[2])
    plus_b, minus_b = relay(parts_b, far[1], far[3])
    near = [shift(plus_a, "z", 1), shift(plus_b, "y", 1), shift(minus_a, "z", -1),
            shift(minus_b, "y", -1)]
    near = lax.optimization_barrier(near)
    sum_a = wide(parts_a[0]) + wide(near[0]) + wide(near[2])
    sum_b = wide(parts_b[0]) + wide(near[1]) + wide(near[3])
    low_a, low_b = sum_a[1:].astype(BF), sum_b[1:].astype(BF)
    final = [shift(low_a[1], "y", 1), shift(low_b[1], "z", 1), shift(low_a[0], "y", -1),
             shift(low_b[0], "z", -1), shift(low_a[2], "y", 2), shift(low_b[2], "z", 2)]
    total_a = sum_a[0] + wide(final[0]) + wide(final[2]) + wide(final[4])
    total_b = sum_b[0] + wide(final[1]) + wide(final[3]) + wide(final[5])
    return jnp.concatenate([total_a, total_b])


def dot_t(lhs, rhs):
    return lax.dot_general(lhs, rhs, (((1,), (1,)), ((), ())), preferred_element_type=F32)


def attention_kernel(*refs):
    tok = refs[0:6]
    adapt = refs[6:14]
    (gain, gain_moe, cosine, sine, bias, doc, colp, colr, wq_hbm, wk_hbm, wv_hbm, wo_hbm,
     mixed_out, moe_a, moe_b,
     wq, wk, wv, wo, xn, ad, qbuf, kbuf, vbuf, att, sems) = refs[14:]
    copies = [pltpu.make_async_copy(src, dst, sems.at[i]) for i, (src, dst) in enumerate(
        [(wk_hbm, wk), (wv_hbm, wv), (wq_hbm, wq), (wo_hbm, wo)])]
    for copy in copies:
        copy.start()
    count = tok[0].shape[0]
    for j in range(8):
        ad[48 * j:48 * j + 48, :] = adapt[j][...]

    def norm(rows, scale):
        inverse = lax.rsqrt(jnp.mean(rows * rows, axis=-1, keepdims=True) + EPSILON)
        return (rows * inverse * scale).astype(BF)

    for b in range(6):
        xn[b * count:(b + 1) * count, :] = norm(tok[b][...].astype(F32), gain[...])
    copies[0].wait()
    copies[1].wait()
    col_prompt = colp[...]
    col_row = colr[...]

    def low(z, roll, first, docs):
        moved = pltpu.roll(z, roll, 1)
        keep = (docs == col_prompt) & (col_row >= first) & (col_row < first + 2)
        return jnp.where(keep, moved, 0.0).astype(BF)

    lane = lax.broadcasted_iota(jnp.int32, (count, 128), 1)
    lower = (lane & 63) < 32

    def rope(u, cos_t, sin_t):
        turned = jnp.where(lower, pltpu.roll(u, 96, 1), pltpu.roll(u, 32, 1))
        return (u * cos_t + turned * sin_t).astype(BF)

    def key_block(b, carry):
        at = pl.multiple_of(b * count, count)
        rows = xn[pl.ds(at, count), :]
        docs = doc[pl.ds(at, count), :]
        z = dot_t(rows, ad[...])
        keys = jnp.dot(rows, wk[...], preferred_element_type=F32) + jnp.dot(
            low(z, 10, 12, docs), ad[:, :512], preferred_element_type=F32)
        values = jnp.dot(rows, wv[...], preferred_element_type=F32) + jnp.dot(
            low(z, 8, 12, docs), ad[:, 512:1024], preferred_element_type=F32)
        vbuf[pl.ds(at, count), :] = values.astype(BF)
        cos_t = cosine[pl.ds(at, count), :]
        sin_t = sine[pl.ds(at, count), :]
        for c in range(4):
            kbuf[pl.ds(at, count), 128 * c:128 * c + 128] = rope(
                keys[:, 128 * c:128 * c + 128], cos_t, sin_t)
        return carry

    lax.fori_loop(0, 6, key_block, 0)
    copies[2].wait()
    own = xn[0:count, :]
    docs = doc[0:count, :]
    z = dot_t(own, ad[...])
    zq = low(z, 8, 8, docs)
    cos_t = cosine[0:count, :]
    sin_t = sine[0:count, :]
    low_half = lane < 64

    def query_block(c, carry):
        at = pl.multiple_of(c * 384, 128)
        u = jnp.dot(own, wq[:, pl.ds(at, 384)], preferred_element_type=F32) + jnp.dot(
            zq, ad[:, pl.ds(at, 384)], preferred_element_type=F32)
        for t in range(3):
            qbuf[:, pl.ds(pl.multiple_of(at + 128 * t, 128), 128)] = rope(
                u[:, 128 * t:128 * t + 128], cos_t, sin_t)
        return carry

    lax.fori_loop(0, 4, query_block, 0)

    def pair(j, carry):
        kv = pl.ds(pl.multiple_of(j * 128, 128), 128)
        keys = kbuf[:, kv]
        values = vbuf[:, kv]
        tiles = [qbuf[:, pl.ds(pl.multiple_of(j * 384 + 128 * t, 128), 128)] for t in range(3)]
        results = []
        for h in range(6):
            own_low, kv_low = h % 2 == 0, h < 3
            q = tiles[h // 2].astype(F32)
            if own_low != kv_low:
                q = pltpu.roll(q, 64, 1)
            q = jnp.where(low_half if kv_low else ~low_half, q, 0.0).astype(BF)
            s = dot_t(q, keys) * (HEAD ** -0.5) + bias[...]
            top = jnp.max(s, axis=-1, keepdims=True)
            w = jnp.exp(s - top)
            total = jnp.sum(w, axis=-1, keepdims=True)
            o = jnp.dot(w.astype(BF), values, preferred_element_type=F32) / total
            if own_low != kv_low:
                o = pltpu.roll(o, 64, 1)
            results.append(o)
        for t in range(3):
            att[:, pl.ds(pl.multiple_of(j * 384 + 128 * t, 128), 128)] = jnp.where(
                low_half, results[2 * t], results[2 * t + 1]).astype(BF)
        return carry

    lax.fori_loop(0, 4, pair, 0)
    copies[3].wait()
    attended = att[...]
    zo = low(dot_t(attended, ad[...]), 4, 10, docs)
    mixed = (tok[0][...].astype(F32) + jnp.dot(attended, wo[...], preferred_element_type=F32)
             + jnp.dot(zo, ad[...], preferred_element_type=F32)).astype(BF)
    mixed_out[...] = mixed
    moe = norm(mixed.astype(F32), gain_moe[...])
    moe_a[...] = moe[:count // 2]
    moe_b[...] = moe[count // 2:]


def attention(tok, adapt, gain, gain_moe, cosine, sine, bias, doc, colp, colr, wq, wk, wv, wo):
    count, width = tok[0].shape
    vm = pl.BlockSpec(memory_space=pltpu.VMEM)
    anywhere = pl.BlockSpec(memory_space=pl.ANY)
    half = jax.ShapeDtypeStruct((count // 2, width), BF)
    return pl.pallas_call(
        attention_kernel,
        out_shape=(jax.ShapeDtypeStruct((count, width), BF), half, half),
        in_specs=[vm] * 22 + [anywhere] * 4,
        out_specs=(vm, vm, vm),
        scratch_shapes=[
            pltpu.VMEM(wq.shape, BF), pltpu.VMEM(wk.shape, BF), pltpu.VMEM(wv.shape, BF),
            pltpu.VMEM(wo.shape, BF), pltpu.VMEM((6 * count, width), BF),
            pltpu.VMEM((384, width), BF), pltpu.VMEM((count, width), BF),
            pltpu.VMEM((6 * count, 512), BF), pltpu.VMEM((6 * count, 512), BF),
            pltpu.VMEM((count, width), BF), pltpu.SemaphoreType.DMA((4,)),
        ],
        compiler_params=pltpu.CompilerParams(vmem_limit_bytes=48 << 20),
        name="attention_block",
    )(*tok, *adapt, gain, gain_moe, cosine, sine, bias, doc, colp, colr, wq, wk, wv, wo)


def expert_kernel(*refs):
    pieces_a, pieces_b = refs[0:5], refs[5:10]
    high, low, gate_hbm, up_hbm, down_hbm = refs[10:15]
    out_a, out_b = refs[15:19], refs[19:23]
    x, xe, ho, gate, up, down, sem_x, sem_w, sem_o = refs[23:]
    loads = []
    where_a = [x.at[0, :, 0:64], x.at[1, :, 0:64], x.at[2, :, 0:64], x.at[3, 0:2, 0:64],
               x.at[3, 2:4, 0:64]]
    where_b = [x.at[:, 0, 64:128], x.at[:, 1, 64:128], x.at[:, 2, 64:128],
               x.at[0:2, 3, 64:128], x.at[2:4, 3, 64:128]]
    for k in range(5):
        loads.append(pltpu.make_async_copy(pieces_a[k], where_a[k], sem_x.at[k]))
        loads.append(pltpu.make_async_copy(pieces_b[k], where_b[k], sem_x.at[5 + k]))
    for copy in loads:
        copy.start()
    weights = []
    for s in range(5):
        weights.append([pltpu.make_async_copy(src.at[s], dst.at[s], sem_w.at[3 * s + k])
                        for k, (src, dst) in enumerate(
                            [(gate_hbm, gate), (up_hbm, up), (down_hbm, down)])])
        for copy in weights[-1]:
            copy.start()
    for copy in loads:
        copy.wait()
    before = (lax.broadcasted_iota(jnp.int32, (128, 128), 0)
              < lax.broadcasted_iota(jnp.int32, (128, 128), 1)).astype(BF)
    slot = lax.broadcasted_iota(jnp.int32, (SLOTS, 128), 0).astype(F32)

    def places(i):
        named = (high[i] > 0.0).astype(F32)
        rank = jnp.dot(named.astype(BF), before, preferred_element_type=F32)
        rank = jnp.where(named > 0.0, rank, -1.0)
        return [slot == rank[s:s + 1, :] for s in range(5)]

    def take(i, carry):
        block = x[i // 4, lax.rem(i, 4)]
        hot = jnp.concatenate([jnp.where(p, 1.0, 0.0) for p in places(i)]).astype(BF)
        rows = jnp.dot(hot, block, preferred_element_type=F32).astype(BF)
        for s in range(5):
            xe[s, pl.ds(pl.multiple_of(i * SLOTS, SLOTS), SLOTS), :] = rows[
                s * SLOTS:(s + 1) * SLOTS]
        return carry

    lax.fori_loop(0, 16, take, 0)
    size = 8 * SLOTS
    for s in range(5):
        for copy in weights[s]:
            copy.wait()

        def run(c, carry, s=s):
            at = pl.ds(pl.multiple_of(c * size, size), size)
            rows = xe[s, at, :]
            g = jnp.dot(rows, gate[s], preferred_element_type=F32)
            u = jnp.dot(rows, up[s], preferred_element_type=F32)
            hidden = (g / (1.0 + jnp.exp(-g)) * u).astype(BF)
            ho[s, at, :] = jnp.dot(hidden, down[s], preferred_element_type=F32).astype(BF)
            return carry

        lax.fori_loop(0, 2, run, 0)

    def combine(i, carry):
        spots = places(i)
        high_i, low_i = high[i], low[i]
        hot_high = jnp.concatenate(
            [jnp.where(p, high_i[s:s + 1, :], 0.0) for s, p in enumerate(spots)]).astype(BF)
        hot_low = jnp.concatenate(
            [jnp.where(p, low_i[s:s + 1, :], 0.0) for s, p in enumerate(spots)]).astype(BF)
        at = pl.ds(pl.multiple_of(i * SLOTS, SLOTS), SLOTS)
        rows = jnp.concatenate([ho[s, at, :] for s in range(5)])
        dims = (((0,), (0,)), ((), ()))
        total = lax.dot_general(hot_high, rows, dims, preferred_element_type=F32)
        total = total + lax.dot_general(hot_low, rows, dims, preferred_element_type=F32)
        x[i // 4, lax.rem(i, 4)] = total.astype(BF)
        return carry

    lax.fori_loop(0, 16, combine, 0)
    stores = [pltpu.make_async_copy(x.at[k, :, 0:64], out_a[k], sem_o.at[k]) for k in range(4)]
    stores += [pltpu.make_async_copy(x.at[:, k, 64:128], out_b[k], sem_o.at[4 + k])
               for k in range(4)]
    for copy in stores:
        copy.start()
    for copy in stores:
        copy.wait()


def experts(pieces_a, pieces_b, high, low, gate, up, down):
    width = gate.shape[1]
    anywhere = pl.BlockSpec(memory_space=pl.ANY)
    vm = pl.BlockSpec(memory_space=pltpu.VMEM)
    quarter = jax.ShapeDtypeStruct((4, 64, width), BF)
    outs = pl.pallas_call(
        expert_kernel,
        out_shape=(quarter,) * 8,
        in_specs=[anywhere] * 10 + [vm] * 2 + [anywhere] * 3,
        out_specs=(anywhere,) * 8,
        scratch_shapes=[
            pltpu.VMEM((4, 4, 128, width), BF), pltpu.VMEM((5, 16 * SLOTS, width), BF),
            pltpu.VMEM((5, 16 * SLOTS, width), BF), pltpu.VMEM(gate.shape, BF),
            pltpu.VMEM(up.shape, BF), pltpu.VMEM(down.shape, BF),
            pltpu.SemaphoreType.DMA((10,)), pltpu.SemaphoreType.DMA((15,)),
            pltpu.SemaphoreType.DMA((8,)),
        ],
        compiler_params=pltpu.CompilerParams(vmem_limit_bytes=58 << 20),
        name="expert_block",
    )(*pieces_a, *pieces_b, high, low, gate, up, down)
    return outs[:4], outs[4:]


def rms_scaled(features, scales):
    features = features.astype(F32)
    inverse = lax.rsqrt(jnp.mean(features * features, axis=-1, keepdims=True) + EPSILON)
    return (features * inverse * scales).astype(BF)


def body(tokens, lengths, prompt_adapter, routes, routing_weight, attention_gain, query_weight,
         key_weight, value_weight, output_weight, adapter_down_maps, adapter_up_query_output,
         adapter_up_key_value, expert_gain, gate_weight, up_weight, down_weight, closing_gain,
         vocab_projection):
    own = tokens[0]
    count, width = own.shape
    me, grp = lax.axis_index("seq"), lax.axis_index("grp")
    back1 = lax.ppermute(own, "seq", [(s, s + 2) for s in range(6)])
    back2 = lax.ppermute(own, "seq", [(s, s + 4) for s in range(4)])

    ids, given = routes[0], routing_weight[0]
    table = jnp.sum(jnp.where(
        ids[:, None, :] == jnp.arange(EXPERTS, dtype=jnp.int32)[None, :, None],
        given[:, None, :], 0.0), axis=2).T
    table = jnp.repeat(table, 2, axis=0).reshape(16, 5 * count)
    high = lax.reduce_precision(table, 8, 7)
    low = table - high
    route_rows = jnp.concatenate(
        [high, low, jnp.zeros((16, width - 10 * count), F32)], axis=1).astype(BF)

    ranks = (jnp.arange(16, dtype=jnp.int32)[:, None]
             == 2 * me + jnp.arange(2, dtype=jnp.int32)[None, :]).astype(BF)
    downs = jnp.einsum("rk,pdr->pkd", ranks, adapter_down_maps[:, 0],
                       preferred_element_type=F32).astype(BF).reshape(8, width)
    ups = lax.dynamic_slice_in_dim(adapter_up_query_output[:, 0], 2 * me, 2, 1).reshape(4, width)
    thin = lax.dynamic_slice_in_dim(adapter_up_key_value[:, 0], 2 * me, 2, 1)
    thin = jnp.concatenate([thin[0], thin[1], jnp.zeros((2, width - 1024), BF)], axis=1)
    maps = jnp.concatenate([downs, ups, thin], axis=0)
    payload = jnp.concatenate(
        [jnp.broadcast_to(maps[None], (16, 14, width)), route_rows[:, None, :],
         jnp.zeros((16, 1, width), BF)], axis=1)
    held = lax.all_to_all(payload, "grp", 0, 0, tiled=True)
    row_kind = jnp.arange(16, dtype=jnp.int32)[None, :, None]
    picked = jnp.stack([lax.dynamic_index_in_dim(held, prompt_adapter[0, p], 0, False)
                        for p in range(3)])
    picked = jnp.where(row_kind < 14, picked, 0).reshape(48, width)
    turn = [picked] + [lax.ppermute(picked, "seq", [(s, (s + d) % 8) for s in range(8)])
                       for d in (2, 6, 4)]
    adapt = turn + [partner(piece) for piece in turn]
    tok = [own, back1, back2]
    tok = tok + [partner(rows) for rows in tok]

    rel = jnp.array([0, 3, 1, 2], jnp.int32)
    source = ((grp // 4 + rel[:, None]) % 4 * 4 + (grp % 4 + rel[None, :]) % 4).reshape(16)
    order = (source[:, None] == jnp.arange(16, dtype=jnp.int32)[None, :]).astype(F32)
    route_in = jnp.dot(order, held[:, 14, :].astype(F32), precision=lax.Precision.HIGHEST)
    pad = jnp.zeros((16, 3, count), F32)
    high_in = jnp.concatenate([route_in[:, :5 * count].reshape(16, 5, count), pad], axis=1)
    low_in = jnp.concatenate(
        [route_in[:, 5 * count:10 * count].reshape(16, 5, count), pad], axis=1)

    lens = lengths[0]
    ends = jnp.cumsum(lens)
    starts = ends - lens
    other = me ^ 1
    blocks = jnp.stack([me, me - 2, me - 4, other, other - 2, other - 4])
    index = (blocks[:, None] * count + jnp.arange(count, dtype=jnp.int32)[None, :]).reshape(-1)
    document = jnp.sum((index[:, None] >= ends[None, :]).astype(jnp.int32), axis=1)
    start = jnp.where(document == 0, starts[0], jnp.where(document == 1, starts[1], starts[2]))
    half = HEAD // 2
    frequency = ROPE_BASE ** (-jnp.arange(half, dtype=F32) / half)
    angles = (index - start).astype(F32)[:, None] * frequency[None, :]
    cosine, sine = jnp.cos(angles), jnp.sin(angles)
    cosine = jnp.concatenate([cosine] * 4, axis=1)
    sine = jnp.concatenate([-sine, sine, -sine, sine], axis=1)
    row_index = index[:count]
    allowed = ((document[None, :] == document[:count, None]) & (index[None, :] >= 0)
               & (index[None, :] <= row_index[:, None]))
    bias = jnp.where(allowed, 0.0, MASKED).astype(F32)
    columns = jnp.arange(384, dtype=jnp.int32)[None, :]

    mixed, moe_a, moe_b = attention(
        tok, adapt, attention_gain[None], expert_gain[None], cosine, sine, bias,
        document[:, None], columns // 16 % 3, columns % 16, query_weight, key_weight,
        value_weight, output_weight)

    pieces_a, pieces_b = gather_tokens(moe_a, moe_b)
    parts_a, parts_b = experts(pieces_a, pieces_b, high_in, low_in, gate_weight, up_weight,
                               down_weight)
    combined = reduce_tokens(parts_a, parts_b)
    hidden_out = (mixed.astype(F32) + combined).astype(BF)

    selector = (ends[:, None] - 1 == row_index[None, :]).astype(BF)
    last = jnp.dot(selector, hidden_out, preferred_element_type=F32)
    last = rms_scaled(last, closing_gain)
    part = width // 8
    split = last.reshape(3, 8, part).transpose(1, 0, 2)
    mine = lax.all_to_all(split, "seq", 0, 0, tiled=True)
    mine = jnp.sum(mine.astype(F32), axis=0).astype(BF)
    everyone = lax.all_to_all(jnp.broadcast_to(mine[None], (128, 3, part)), WHOLE, 0, 0,
                              tiled=True)
    final_rows = everyone.reshape(8, 48, part).transpose(1, 0, 2).reshape(48, width)
    logits = jnp.dot(final_rows, vocab_projection, preferred_element_type=F32)
    top = jnp.max(logits, axis=1)
    mass = jnp.sum(jnp.exp(logits - top[:, None]), axis=1)
    stats = jnp.concatenate([top, mass, jnp.zeros((32,), F32)])
    stats = lax.all_to_all(jnp.broadcast_to(stats[None], (128, 128)), WHOLE, 0, 0, tiled=True)
    tops = stats[:, :48]
    peak = jnp.max(tops, axis=0)
    total = jnp.sum(stats[:, 48:96] * jnp.exp(tops - peak[None]), axis=0)
    log_probs = logits - (peak + jnp.log(total))[:, None]
    return hidden_out[None], log_probs


def solution(mesh):
    placed = (
        P("grp", "seq", None), P("grp", None), P("grp", None), P("grp", "seq", None),
        P("grp", "seq", None), P(), P(), P(), P(), P(), P(None, "grp", None, None),
        P(None, "grp", None, None), P(None, "grp", None, None), P(), P("grp", None, None),
        P("grp", None, None), P("grp", None, None), P(), P(None, WHOLE),
    )
    return jax.shard_map(
        body,
        mesh=mesh,
        in_specs=placed,
        out_specs=(P("grp", "seq", None), P(None, WHOLE)),
        check_vma=False,
    )
```

```python
import functools

import jax
import jax.numpy as jnp
import numpy as np
from jax import lax
from jax.experimental import pallas as pl
from jax.experimental.pallas import tpu as pltpu
from jax.sharding import PartitionSpec as P

HEADS = 24
KV_HEADS = 8
HEAD = 64
EXPERTS = 40
TOP = 8
CAP = 40
EPSILON = 1e-05
ROPE_BASE = 10000.0
MASKED = -1e30
SIDE = 4
BF = jnp.bfloat16
F32 = jnp.float32
WHOLE = ("seq", "grp")


def shift(rows, phase, step):
    pairs = []
    for s in range(8):
        for i in range(16):
            if s % 2 == phase:
                to = i // SIDE * SIDE + (i % SIDE + step) % SIDE
            else:
                to = (i // SIDE + step) % SIDE * SIDE + i % SIDE
            pairs.append((s * 16 + i, s * 16 + to))
    return lax.ppermute(rows, WHOLE, pairs)


def partner(rows):
    return lax.ppermute(rows, "seq", [(s, s ^ 1) for s in range(8)])


def wide(v):
    return v.astype(F32)


def dot_t(lhs, rhs):
    return lax.dot_general(lhs, rhs, (((1,), (1,)), ((), ())), preferred_element_type=F32)


def attention_kernel(*refs):
    tok = refs[0:6]
    adapt = refs[6:14]
    (gain, gain_moe, cosine, sine, key_doc, key_index, doc, index, colp, colr, wq_hbm, wk_hbm,
     wv_hbm, wo_hbm, mixed_out, moe_out,
     wq, wk, wv, wo, xn, ad, qbuf, kbuf, vbuf, att, sems) = refs[14:]
    copies = [pltpu.make_async_copy(src, dst, sems.at[i]) for i, (src, dst) in enumerate(
        [(wk_hbm, wk), (wv_hbm, wv), (wq_hbm, wq), (wo_hbm, wo)])]
    for copy in copies:
        copy.start()
    count = tok[0].shape[0]
    for j in range(8):
        ad[48 * j:48 * j + 48, :] = adapt[j][...]

    def norm(rows, scale):
        inverse = lax.rsqrt(jnp.mean(rows * rows, axis=-1, keepdims=True) + EPSILON)
        return (rows * inverse * scale).astype(BF)

    for b in range(6):
        xn[b * count:(b + 1) * count, :] = norm(tok[b][...].astype(F32), gain[...])
    copies[0].wait()
    copies[1].wait()
    col_prompt = colp[...]
    col_row = colr[...]

    def low(z, roll, first, docs):
        moved = pltpu.roll(z, roll, 1)
        keep = (docs == col_prompt) & (col_row >= first) & (col_row < first + 2)
        return jnp.where(keep, moved, 0.0).astype(BF)

    lane = lax.broadcasted_iota(jnp.int32, (count, 128), 1)
    lower = (lane & 63) < 32

    def rope(u, cos_t, sin_t):
        turned = jnp.where(lower, pltpu.roll(u, 96, 1), pltpu.roll(u, 32, 1))
        return (u * cos_t + turned * sin_t).astype(BF)

    def key_block(b, carry):
        at = pl.multiple_of(b * count, count)
        rows = xn[pl.ds(at, count), :]
        docs = doc[pl.ds(at, count), :]
        z = dot_t(rows, ad[...])
        keys = jnp.dot(rows, wk[...], preferred_element_type=F32) + jnp.dot(
            low(z, 10, 12, docs), ad[:, :512], preferred_element_type=F32)
        values = jnp.dot(rows, wv[...], preferred_element_type=F32) + jnp.dot(
            low(z, 8, 12, docs), ad[:, 512:1024], preferred_element_type=F32)
        vbuf[pl.ds(at, count), :] = values.astype(BF)
        cos_t = cosine[pl.ds(at, count), :]
        sin_t = sine[pl.ds(at, count), :]
        for c in range(4):
            kbuf[pl.ds(at, count), 128 * c:128 * c + 128] = rope(
                keys[:, 128 * c:128 * c + 128], cos_t, sin_t)
        return carry

    lax.fori_loop(0, 6, key_block, 0)
    copies[2].wait()
    own = xn[0:count, :]
    docs = doc[0:count, :]
    z = dot_t(own, ad[...])
    zq = low(z, 8, 8, docs)
    cos_t = cosine[0:count, :]
    sin_t = sine[0:count, :]
    low_half = lane < 64
    allowed = (docs == key_doc[...]) & (key_index[...] <= index[...])
    bias = jnp.where(allowed, 0.0, MASKED)

    def query_block(c, carry):
        at = pl.multiple_of(c * 384, 128)
        u = jnp.dot(own, wq[:, pl.ds(at, 384)], preferred_element_type=F32) + jnp.dot(
            zq, ad[:, pl.ds(at, 384)], preferred_element_type=F32)
        for t in range(3):
            qbuf[:, pl.ds(pl.multiple_of(at + 128 * t, 128), 128)] = rope(
                u[:, 128 * t:128 * t + 128], cos_t, sin_t)
        return carry

    lax.fori_loop(0, 4, query_block, 0)

    def pair(j, carry):
        kv = pl.ds(pl.multiple_of(j * 128, 128), 128)
        keys = kbuf[:, kv]
        values = vbuf[:, kv]
        tiles = [qbuf[:, pl.ds(pl.multiple_of(j * 384 + 128 * t, 128), 128)] for t in range(3)]
        results = []
        for h in range(6):
            own_low, kv_low = h % 2 == 0, h < 3
            q = tiles[h // 2].astype(F32)
            if own_low != kv_low:
                q = pltpu.roll(q, 64, 1)
            q = jnp.where(low_half if kv_low else ~low_half, q, 0.0).astype(BF)
            s = dot_t(q, keys) * (HEAD ** -0.5) + bias
            top = jnp.max(s, axis=-1, keepdims=True)
            w = jnp.exp(s - top)
            total = jnp.sum(w, axis=-1, keepdims=True)
            o = jnp.dot(w.astype(BF), values, preferred_element_type=F32) / total
            if own_low != kv_low:
                o = pltpu.roll(o, 64, 1)
            results.append(o)
        for t in range(3):
            att[:, pl.ds(pl.multiple_of(j * 384 + 128 * t, 128), 128)] = jnp.where(
                low_half, results[2 * t], results[2 * t + 1]).astype(BF)
        return carry

    lax.fori_loop(0, 4, pair, 0)
    copies[3].wait()
    attended = att[...]
    zo = low(dot_t(attended, ad[...]), 4, 10, docs)
    mixed = (tok[0][...].astype(F32) + jnp.dot(attended, wo[...], preferred_element_type=F32)
             + jnp.dot(zo, ad[...], preferred_element_type=F32)).astype(BF)
    mixed_out[...] = mixed
    moe_out[...] = norm(mixed.astype(F32), gain_moe[...])


def attention(tok, adapt, *others):
    count, width = tok[0].shape
    wq, wk, wv, wo = others[-4:]
    vm = pl.BlockSpec(memory_space=pltpu.VMEM)
    anywhere = pl.BlockSpec(memory_space=pl.ANY)
    rows = jax.ShapeDtypeStruct((count, width), BF)
    return pl.pallas_call(
        attention_kernel,
        out_shape=(rows, rows),
        in_specs=[vm] * (10 + len(others)) + [anywhere] * 4,
        out_specs=(vm, vm),
        scratch_shapes=[
            pltpu.VMEM(wq.shape, BF), pltpu.VMEM(wk.shape, BF), pltpu.VMEM(wv.shape, BF),
            pltpu.VMEM(wo.shape, BF), pltpu.VMEM((6 * count, width), BF),
            pltpu.VMEM((384, width), BF), pltpu.VMEM((count, width), BF),
            pltpu.VMEM((6 * count, 512), BF), pltpu.VMEM((6 * count, 512), BF),
            pltpu.VMEM((count, width), BF), pltpu.SemaphoreType.DMA((4,)),
        ],
        compiler_params=pltpu.CompilerParams(vmem_limit_bytes=48 << 20),
        cost_estimate=pl.CostEstimate(flops=6 << 30, transcendentals=0,
                                      bytes_accessed=16 << 20),
        name="attention_block",
    )(*tok, *adapt, *others)


def expert_kernel(sizes, *refs):
    n = len(sizes)
    pieces, (first, table, gate_hbm, up_hbm, down_hbm) = refs[:n], refs[n:n + 5]
    outs = refs[n + 5:2 * n + 5]
    x, xe, ho, scale, gate, up, down, sem_x, sem_w, sem_o = refs[2 * n + 5:]
    pairs = sum(sizes) // 2
    rows_all = pairs * 2 * CAP
    starts = [sum(sizes[:k]) for k in range(n)]
    loads = [pltpu.make_async_copy(pieces[k], x.at[pl.ds(starts[k], sizes[k])], sem_x.at[k])
             for k in range(n)]
    for copy in loads:
        copy.start()
    odd = first[0]
    order = [odd, odd + 1, odd + 2, odd + 3, 4 - 4 * odd]
    weights = []
    for s in range(5):
        weights.append([pltpu.make_async_copy(src.at[order[s]], dst, sem_w.at[3 * s + k])
                        for k, (src, dst) in enumerate(
                            [(gate_hbm, gate.at[s]), (up_hbm, up.at[s]),
                             (down_hbm, down.at[pl.ds(256 * s, 256)])])])
        for copy in weights[-1]:
            copy.start()
    row = lax.broadcasted_iota(jnp.int32, (256, 256), 0)
    col = lax.broadcasted_iota(jnp.int32, (256, 256), 1)
    before = ((row < col) & ((row < 128) == (col < 128))).astype(BF)
    slot = lax.broadcasted_iota(jnp.int32, (2 * CAP, 256), 0).astype(F32)
    base = jnp.where(lax.broadcasted_iota(jnp.int32, (8, 256), 1) < 128, 0.0, float(CAP))
    for copy in loads:
        copy.wait()

    def places(i):
        named = table[i] > 0.0
        rank = jnp.dot(named.astype(F32).astype(BF), before, preferred_element_type=F32) + base
        rank = jnp.where(named, rank, -1.0)
        return [slot == rank[e:e + 1, :] for e in range(3)]

    def take(i, carry):
        spots = places(i)
        block = jnp.concatenate([x[2 * i], x[2 * i + 1]])
        hot = jnp.concatenate([jnp.where(p, 1.0, 0.0) for p in spots]).astype(BF)
        rows = jnp.dot(hot, block, preferred_element_type=F32).astype(BF)
        at = pl.ds(pl.multiple_of(i * 2 * CAP, 16), 2 * CAP)
        given = table[i]
        for e in range(3):
            xe[e, at, :] = rows[e * 2 * CAP:(e + 1) * 2 * CAP]
            scale[e, at, :] = jnp.sum(jnp.where(spots[e], given[e:e + 1, :], 0.0), axis=1,
                                      keepdims=True)
        return carry

    lax.fori_loop(0, pairs, take, 0)
    size = min(rows_all, 320)
    for e in range(3):
        halves = [2 * e, 2 * e + 1] if e < 2 else [4]
        for s in halves:
            for copy in weights[s]:
                copy.wait()

        def run(c, carry, e=e, halves=halves):
            at = pl.ds(pl.multiple_of(c * size, 16), size)
            rows = xe[e, at, :]
            hidden = []
            for s in halves:
                g = jnp.dot(rows, gate[s], preferred_element_type=F32)
                u = jnp.dot(rows, up[s], preferred_element_type=F32)
                hidden.append((g / (1.0 + jnp.exp(-g)) * u).astype(BF))
            hidden = jnp.concatenate(hidden, axis=1)
            maps = down[512 * e:512 * e + 256 * len(halves), :]
            out = jnp.dot(hidden, maps, preferred_element_type=F32)
            ho[e, at, :] = (out * scale[e, at, :]).astype(BF)
            return carry

        lax.fori_loop(0, rows_all // size, run, 0)

    def combine(i, carry):
        hot = jnp.concatenate([jnp.where(p, 1.0, 0.0) for p in places(i)]).astype(BF)
        at = pl.ds(pl.multiple_of(i * 2 * CAP, 16), 2 * CAP)
        rows = jnp.concatenate([ho[e, at, :] for e in range(3)])
        total = lax.dot_general(hot, rows, (((0,), (0,)), ((), ())),
                                preferred_element_type=F32).astype(BF)
        x[2 * i] = total[:128]
        x[2 * i + 1] = total[128:]
        return carry

    lax.fori_loop(0, pairs, combine, 0)
    stores = [pltpu.make_async_copy(x.at[pl.ds(starts[k], sizes[k])], outs[k], sem_o.at[k])
              for k in range(n)]
    for copy in stores:
        copy.start()
    for copy in stores:
        copy.wait()


def experts(pieces, first, table, gate, up, down):
    sizes = [piece.shape[0] for piece in pieces]
    total, width = sum(sizes), gate.shape[1]
    rows = total * CAP
    anywhere = pl.BlockSpec(memory_space=pl.ANY)
    vm = pl.BlockSpec(memory_space=pltpu.VMEM)
    return pl.pallas_call(
        functools.partial(expert_kernel, sizes),
        out_shape=tuple(jax.ShapeDtypeStruct(piece.shape, BF) for piece in pieces),
        in_specs=[anywhere] * len(sizes) + [pl.BlockSpec(memory_space=pltpu.SMEM), vm]
        + [anywhere] * 3,
        out_specs=(anywhere,) * len(sizes),
        scratch_shapes=[
            pltpu.VMEM((total, 128, width), BF), pltpu.VMEM((3, rows, width), BF),
            pltpu.VMEM((3, rows, width), BF), pltpu.VMEM((3, rows, 1), F32),
            pltpu.VMEM(gate.shape, BF), pltpu.VMEM(up.shape, BF),
            pltpu.VMEM((5 * 256, width), BF),
            pltpu.SemaphoreType.DMA((len(sizes),)), pltpu.SemaphoreType.DMA((15,)),
            pltpu.SemaphoreType.DMA((len(sizes),)),
        ],
        compiler_params=pltpu.CompilerParams(vmem_limit_bytes=44 << 20),
        cost_estimate=pl.CostEstimate(flops=rows * 6 * 1536 * 256 * 5, transcendentals=0,
                                      bytes_accessed=12 << 20),
        name="expert_block",
    )(*pieces, first, table, gate, up, down)


def rms_scaled(features, scales):
    features = features.astype(F32)
    inverse = lax.rsqrt(jnp.mean(features * features, axis=-1, keepdims=True) + EPSILON)
    return (features * inverse * scales).astype(BF)


def body(tokens, lengths, prompt_adapter, routes, routing_weight, attention_gain, query_weight,
         key_weight, value_weight, output_weight, adapter_down_maps, adapter_up_query_output,
         adapter_up_key_value, expert_gain, gate_weight, up_weight, down_weight, closing_gain,
         vocab_projection):
    own = tokens[0]
    count, width = own.shape
    me, grp = lax.axis_index("seq"), lax.axis_index("grp")

    listing = np.concatenate([np.array([0, 1, 2] if g % 2 == 0 else [1, 2, 0]) + 5 * g // 2
                              for g in range(16)]).astype(np.int32)
    ids, given = routes[0], routing_weight[0]
    table = jnp.sum(jnp.where(ids.T[None] == jnp.asarray(listing)[:, None, None],
                              given.T[None], 0.0), axis=1).reshape(16, 3 * count)
    high = lax.reduce_precision(table, 8, 7)
    low = table - high
    route_rows = jnp.concatenate(
        [high, low, jnp.zeros((16, width - 6 * count), F32)], axis=1).astype(BF)

    ranks = (jnp.arange(16, dtype=jnp.int32)[:, None]
             == 2 * me + jnp.arange(2, dtype=jnp.int32)[None, :]).astype(BF)
    downs = jnp.einsum("rk,pdr->pkd", ranks, adapter_down_maps[:, 0],
                       preferred_element_type=F32).astype(BF).reshape(8, width)
    ups = lax.dynamic_slice_in_dim(adapter_up_query_output[:, 0], 2 * me, 2, 1).reshape(4, width)
    thin = lax.dynamic_slice_in_dim(adapter_up_key_value[:, 0], 2 * me, 2, 1)
    thin = jnp.concatenate([thin[0], thin[1], jnp.zeros((2, width - 1024), BF)], axis=1)
    maps = jnp.concatenate([downs, ups, thin], axis=0)
    payload = jnp.concatenate(
        [jnp.broadcast_to(maps[None], (16, 14, width)), route_rows[:, None, :],
         jnp.zeros((16, 1, width), BF)], axis=1)
    payload, own = lax.optimization_barrier((payload, own))
    held = lax.all_to_all(payload, "grp", 0, 0, tiled=True)
    back1 = lax.ppermute(own, "seq", [(s, s + 2) for s in range(6)])
    back2 = lax.ppermute(own, "seq", [(s, s + 4) for s in range(4)])
    picked = jnp.stack([lax.dynamic_index_in_dim(held, prompt_adapter[0, p], 0, False)
                        for p in range(3)]).reshape(48, width)
    turn = [picked] + [lax.ppermute(picked, "seq", [(s, (s + d) % 8) for s in range(8)])
                       for d in (2, 6, 4)]
    adapt = turn + [partner(piece) for piece in turn]
    tok = [own, back1, back2]
    tok = tok + [partner(rows) for rows in tok]

    lens = lengths[0]
    ends = jnp.cumsum(lens)
    starts = ends - lens
    other = me ^ 1
    blocks = jnp.stack([me, me - 2, me - 4, other, other - 2, other - 4])
    row = jnp.arange(count, dtype=jnp.int32)
    index = (blocks[:, None] * count + row[None, :]).reshape(-1)
    document = jnp.sum((index[:, None] >= ends[None, :]).astype(jnp.int32), axis=1)
    half = HEAD // 2
    frequency = ROPE_BASE ** (-(jnp.arange(128, dtype=jnp.int32) % half).astype(F32) / half)
    sign = jnp.where(jnp.arange(128) % HEAD < half, -1.0, 1.0).astype(F32)
    near = row.astype(F32)[:, None] * frequency[None, :]
    far = (blocks[:, None] * count - starts[None, :]).astype(F32)[:, :, None] * frequency
    near_cos, near_sin = jnp.cos(near)[None], jnp.sin(near)[None]
    far_cos, far_sin = jnp.cos(far), jnp.sin(far)

    def by_document(values):
        docs = document.reshape(6, count, 1)
        return jnp.where(docs == 0, values[:, None, 0], jnp.where(
            docs == 1, values[:, None, 1], values[:, None, 2]))

    far_cos, far_sin = by_document(far_cos), by_document(far_sin)
    cosine = (far_cos * near_cos - far_sin * near_sin).reshape(6 * count, 128)
    sine = ((far_sin * near_cos + far_cos * near_sin) * sign).reshape(6 * count, 128)
    row_index = index[:count]
    columns = jnp.arange(384, dtype=jnp.int32)[None, :]
    key_document = jnp.where(index >= 0, document, -1)

    mixed, moe_in = attention(
        tok, adapt, attention_gain[None], expert_gain[None], cosine, sine, key_document[None],
        index[None], document[:, None], row_index[:, None], columns // 16 % 3, columns % 16,
        query_weight, key_weight, value_weight, output_weight)

    rel = jnp.array([0, 3, 1, 2], jnp.int32)
    first, second = jnp.where(me % 2 == 0, grp % 4, grp // 4), jnp.where(
        me % 2 == 0, grp // 4, grp % 4)
    first, second = (first + rel[None, :]) % 4, (second + rel[:, None]) % 4
    source = jnp.where(me % 2 == 0, second * 4 + first, first * 4 + second).reshape(16)
    order = (source[:, None] == jnp.arange(16, dtype=jnp.int32)[None, :]).astype(F32)
    route_in = jnp.dot(order, held[:, 14, :].astype(F32), precision=lax.Precision.HIGHEST)
    route_in = (route_in[:, :3 * count] + route_in[:, 3 * count:6 * count]).reshape(8, 2, 3, count)
    route_in = jnp.concatenate([route_in, jnp.zeros((8, 2, 5, count), F32)], axis=2)
    route_in = route_in.transpose(0, 2, 1, 3).reshape(8, 8, 2 * count)
    odd = (grp % 2).astype(jnp.int32)[None]
    weights = (gate_weight, up_weight, down_weight)

    line = lax.optimization_barrier(
        [shift(moe_in, 0, 1), shift(moe_in, 0, -1), shift(moe_in, 0, 2)])
    plane = jnp.stack([moe_in] + line)
    minus, plus = shift(plane, 1, 1), shift(plane, 1, -1)
    (done_own,) = experts([plane], odd, route_in[:2], *weights)
    minus, plus, done_own = lax.optimization_barrier((minus, plus, done_own))
    ahead, behind = shift(minus[:2], 1, 1), shift(plus[2:], 1, -1)
    done_minus, done_plus = experts([minus, plus], odd, route_in[2:6], *weights)
    ahead, behind, done_minus, done_plus = lax.optimization_barrier(
        (ahead, behind, done_minus, done_plus))
    done_ahead, done_behind = experts([ahead, behind], odd, route_in[6:], *weights)

    ahead, behind = lax.optimization_barrier(
        (shift(done_ahead, 1, 1), shift(done_behind, 1, -1)))
    plus = jnp.concatenate([(wide(done_plus[:2]) + wide(ahead)).astype(BF), done_plus[2:]])
    minus = jnp.concatenate([done_minus[:2], (wide(done_minus[2:]) + wide(behind)).astype(BF)])
    plus, minus = lax.optimization_barrier((shift(plus, 1, 1), shift(minus, 1, -1)))
    plane = wide(done_own) + wide(plus) + wide(minus)
    low = plane[1:].astype(BF)
    line = lax.optimization_barrier(
        [shift(low[1], 0, 1), shift(low[0], 0, -1), shift(low[2], 0, 2)])
    combined = plane[0] + wide(line[0]) + wide(line[1]) + wide(line[2])
    hidden_out = (mixed.astype(F32) + combined).astype(BF)

    selector = (ends[:, None] - 1 == row_index[None, :]).astype(BF)
    last = jnp.dot(selector, hidden_out, preferred_element_type=F32)
    last = rms_scaled(last, closing_gain)
    part = width // 8
    split = last.reshape(3, 8, part).transpose(1, 0, 2)
    mine = lax.all_to_all(split, "seq", 0, 0, tiled=True)
    mine = jnp.sum(mine.astype(F32), axis=0).astype(BF)
    everyone = lax.all_to_all(jnp.broadcast_to(mine[None], (128, 3, part)), WHOLE, 0, 0,
                              tiled=True)
    final_rows = everyone.reshape(8, 48, part).transpose(1, 0, 2).reshape(48, width)
    logits = jnp.dot(final_rows, vocab_projection, preferred_element_type=F32)
    top = jnp.max(logits, axis=1)
    mass = jnp.sum(jnp.exp(logits - top[:, None]), axis=1)
    stats = jnp.concatenate([top, mass, jnp.zeros((32,), F32)])
    stats = lax.all_to_all(jnp.broadcast_to(stats[None], (128, 128)), WHOLE, 0, 0, tiled=True)
    tops = stats[:, :48]
    peak = jnp.max(tops, axis=0)
    total = jnp.sum(stats[:, 48:96] * jnp.exp(tops - peak[None]), axis=0)
    log_probs = logits - (peak + jnp.log(total))[:, None]
    return hidden_out[None], log_probs


def solution(mesh):
    placed = (
        P("grp", "seq", None), P("grp", None), P("grp", None), P("grp", "seq", None),
        P("grp", "seq", None), P(), P(), P(), P(), P(), P(None, "grp", None, None),
        P(None, "grp", None, None), P(None, "grp", None, None), P(), P("grp", None, None),
        P("grp", None, None), P("grp", None, None), P(), P(None, WHOLE),
    )
    return jax.shard_map(
        body,
        mesh=mesh,
        in_specs=placed,
        out_specs=(P("grp", "seq", None), P(None, WHOLE)),
        check_vma=False,
    )
```

```python
import functools

import jax
import jax.numpy as jnp
import numpy as np
from jax import lax
from jax.experimental import pallas as pl
from jax.experimental.pallas import tpu as pltpu
from jax.sharding import PartitionSpec as P

HEADS = 24
KV_HEADS = 8
HEAD = 64
EXPERTS = 40
TOP = 8
CAP = 40
EPSILON = 1e-05
ROPE_BASE = 10000.0
MASKED = -1e30
SIDE = 4
BF = jnp.bfloat16
F32 = jnp.float32
WHOLE = ("seq", "grp")


def shift(rows, phase, step):
    pairs = []
    for s in range(8):
        for i in range(16):
            if s % 2 == phase:
                to = i // SIDE * SIDE + (i % SIDE + step) % SIDE
            else:
                to = (i // SIDE + step) % SIDE * SIDE + i % SIDE
            pairs.append((s * 16 + i, s * 16 + to))
    return lax.ppermute(rows, WHOLE, pairs)


def partner(rows):
    return lax.ppermute(rows, "seq", [(s, s ^ 1) for s in range(8)])


def wide(v):
    return v.astype(F32)


def dot_t(lhs, rhs):
    return lax.dot_general(lhs, rhs, (((1,), (1,)), ((), ())), preferred_element_type=F32)


def norm(rows, scale):
    inverse = lax.rsqrt(jnp.mean(rows * rows, axis=-1, keepdims=True) + EPSILON)
    return (rows * inverse * scale).astype(BF)


def base_kernel(t0, t1, t2, t3, t4, gain, wq_hbm, wk_hbm, wv_hbm, xn, base_q, base_k, base_v,
                wq, wk, wv, sems):
    copies = [pltpu.make_async_copy(src, dst, sems.at[i]) for i, (src, dst) in enumerate(
        [(wk_hbm, wk), (wv_hbm, wv), (wq_hbm, wq)])]
    for copy in copies:
        copy.start()
    count = t0.shape[0]
    for b, rows in enumerate((t0, t1, t2, t3, t4)):
        xn[b * count:(b + 1) * count, :] = norm(rows[...].astype(F32), gain[...])
    copies[0].wait()
    copies[1].wait()

    def key_block(b, carry):
        at = pl.ds(pl.multiple_of(b * 320, 320), 320)
        rows = xn[at, :]
        base_k[at, :] = jnp.dot(rows, wk[...], preferred_element_type=F32)
        base_v[at, :] = jnp.dot(rows, wv[...], preferred_element_type=F32)
        return carry

    lax.fori_loop(0, 2, key_block, 0)
    copies[2].wait()
    own = xn[0:count, :]

    def query_block(c, carry):
        at = pl.ds(pl.multiple_of(c * 512, 512), 512)
        base_q[:, at] = jnp.dot(own, wq[:, at], preferred_element_type=F32)
        return carry

    lax.fori_loop(0, 3, query_block, 0)


def base_projections(tok, gain, wq, wk, wv):
    count, width = tok[0].shape
    vm = pl.BlockSpec(memory_space=pltpu.VMEM)
    anywhere = pl.BlockSpec(memory_space=pl.ANY)
    return pl.pallas_call(
        base_kernel,
        out_shape=(jax.ShapeDtypeStruct((5 * count, width), BF),
                   jax.ShapeDtypeStruct((count, width), F32),
                   jax.ShapeDtypeStruct((5 * count, 512), F32),
                   jax.ShapeDtypeStruct((5 * count, 512), F32)),
        in_specs=[vm] * 6 + [anywhere] * 3,
        out_specs=(vm,) * 4,
        scratch_shapes=[
            pltpu.VMEM(wq.shape, BF), pltpu.VMEM(wk.shape, BF), pltpu.VMEM(wv.shape, BF),
            pltpu.SemaphoreType.DMA((3,)),
        ],
        compiler_params=pltpu.CompilerParams(vmem_limit_bytes=32 << 20),
        cost_estimate=pl.CostEstimate(flops=5 << 30, transcendentals=0,
                                      bytes_accessed=14 << 20),
        name="base_block",
    )(*tok, gain, wq, wk, wv)


def attention_kernel(*refs):
    adapt = refs[0:8]
    (tok, xn, base_q, base_k, base_v, gain_moe, cosine, sine, key_doc, key_index, doc, index,
     colp, colr, wo_hbm, mixed_out, moe_out, wo, ad, qbuf, kbuf, vbuf, att, score, prob,
     sem) = refs[8:]
    load = pltpu.make_async_copy(wo_hbm, wo, sem)
    load.start()
    count = tok.shape[0]
    for j in range(8):
        ad[48 * j:48 * j + 48, :] = adapt[j][...]
    col_prompt = colp[...]
    col_row = colr[...]

    def low(z, roll, first, docs):
        moved = pltpu.roll(z, roll, 1)
        keep = (docs == col_prompt) & (col_row >= first) & (col_row < first + 2)
        return jnp.where(keep, moved, 0.0).astype(BF)

    lane = lax.broadcasted_iota(jnp.int32, (count, 128), 1)
    lower = (lane & 63) < 32

    def rope(u, cos_t, sin_t):
        turned = jnp.where(lower, pltpu.roll(u, 96, 1), pltpu.roll(u, 32, 1))
        return u * cos_t + turned * sin_t

    def key_block(b, carry):
        at = pl.ds(pl.multiple_of(b * count, count), count)
        docs = doc[at, :]
        z = dot_t(xn[at, :], ad[...])
        keys = base_k[at, :] + jnp.dot(
            low(z, 10, 12, docs), ad[:, :512], preferred_element_type=F32)
        values = base_v[at, :] + jnp.dot(
            low(z, 8, 12, docs), ad[:, 512:1024], preferred_element_type=F32)
        vbuf[at, :] = values.astype(BF)
        cos_t = cosine[at, :]
        sin_t = sine[at, :]
        for c in range(4):
            kbuf[at, 128 * c:128 * c + 128] = rope(
                keys[:, 128 * c:128 * c + 128], cos_t, sin_t).astype(BF)
        return carry

    lax.fori_loop(0, 5, key_block, 0)
    docs = doc[0:count, :]
    zq = low(dot_t(xn[0:count, :], ad[...]), 8, 8, docs)
    cos_t = cosine[0:count, :]
    sin_t = sine[0:count, :]
    low_half = lane < 64
    allowed = (docs == key_doc[...]) & (key_index[...] <= index[...])
    bias = jnp.where(allowed, 0.0, MASKED)

    def query_block(c, carry):
        at = pl.multiple_of(c * 384, 128)
        u = base_q[:, pl.ds(at, 384)] + jnp.dot(
            zq, ad[:, pl.ds(at, 384)], preferred_element_type=F32)
        for t in range(3):
            q = rope(u[:, 128 * t:128 * t + 128], cos_t, sin_t).astype(BF).astype(F32)
            q = q * (HEAD ** -0.5)
            turned = pltpu.roll(q, 64, 1)
            for own_low in (True, False):
                h = 2 * t + (0 if own_low else 1)
                kv_low = h < 3
                rows = q if own_low == kv_low else turned
                keep = low_half if kv_low else ~low_half
                qbuf[c, count * h:count * h + count, :] = jnp.where(keep, rows, 0.0).astype(BF)
        return carry

    lax.fori_loop(0, 4, query_block, 0)

    def pair(j, carry):
        kv = pl.ds(pl.multiple_of(j * 128, 128), 128)
        score[...] = dot_t(qbuf[j], kbuf[:, kv])
        totals = []
        for h in range(6):
            at = slice(count * h, count * h + count)
            s = score[at, :] + bias
            top = jnp.max(s, axis=-1, keepdims=True)
            w = jnp.exp(s - top)
            totals.append(jnp.sum(w, axis=-1, keepdims=True))
            prob[at, :] = w.astype(BF)
        out = jnp.dot(prob[...], vbuf[:, kv], preferred_element_type=F32)
        results = []
        for h in range(6):
            o = out[count * h:count * h + count] / totals[h]
            results.append(pltpu.roll(o, 64, 1) if (h % 2 == 0) != (h < 3) else o)
        for t in range(3):
            att[:, pl.ds(pl.multiple_of(j * 384 + 128 * t, 128), 128)] = jnp.where(
                low_half, results[2 * t], results[2 * t + 1]).astype(BF)
        return carry

    lax.fori_loop(0, 4, pair, 0)
    load.wait()
    attended = att[...]
    zo = low(dot_t(attended, ad[...]), 4, 10, docs)
    mixed = (tok[...].astype(F32) + jnp.dot(attended, wo[...], preferred_element_type=F32)
             + jnp.dot(zo, ad[...], preferred_element_type=F32)).astype(BF)
    mixed_out[...] = mixed
    moe_out[...] = norm(mixed.astype(F32), gain_moe[...])


def attention(adapt, own, *others):
    count, width = own.shape
    wo = others[-1]
    vm = pl.BlockSpec(memory_space=pltpu.VMEM)
    anywhere = pl.BlockSpec(memory_space=pl.ANY)
    rows = jax.ShapeDtypeStruct((count, width), BF)
    return pl.pallas_call(
        attention_kernel,
        out_shape=(rows, rows),
        in_specs=[vm] * (8 + len(others)) + [anywhere],
        out_specs=(vm, vm),
        scratch_shapes=[
            pltpu.VMEM(wo.shape, BF), pltpu.VMEM((384, width), BF),
            pltpu.VMEM((4, 6 * count, 128), BF), pltpu.VMEM((5 * count, 512), BF),
            pltpu.VMEM((5 * count, 512), BF), pltpu.VMEM((count, width), BF),
            pltpu.VMEM((6 * count, 5 * count), F32), pltpu.VMEM((6 * count, 5 * count), BF),
            pltpu.SemaphoreType.DMA,
        ],
        compiler_params=pltpu.CompilerParams(vmem_limit_bytes=40 << 20),
        cost_estimate=pl.CostEstimate(flops=6 << 30, transcendentals=0,
                                      bytes_accessed=16 << 20),
        name="attention_block",
    )(*adapt, own, *others)


def expert_kernel(sizes, *refs):
    n = len(sizes)
    pieces, (first, table, gate_hbm, up_hbm, down_hbm) = refs[:n], refs[n:n + 5]
    outs = refs[n + 5:2 * n + 5]
    x, xe, ho, scale, gate, up, down, sem_x, sem_w, sem_o = refs[2 * n + 5:]
    pairs = sum(sizes) // 2
    rows_all = pairs * 2 * CAP
    starts = [sum(sizes[:k]) for k in range(n)]
    loads = [pltpu.make_async_copy(pieces[k], x.at[pl.ds(starts[k], sizes[k])], sem_x.at[k])
             for k in range(n)]
    for copy in loads:
        copy.start()
    odd = first[0]
    order = [odd, odd + 1, odd + 2, odd + 3, 4 - 4 * odd]
    weights = []
    for s in range(5):
        weights.append([pltpu.make_async_copy(src.at[order[s]], dst, sem_w.at[3 * s + k])
                        for k, (src, dst) in enumerate(
                            [(gate_hbm, gate.at[s]), (up_hbm, up.at[s]),
                             (down_hbm, down.at[pl.ds(256 * s, 256)])])])
        for copy in weights[-1]:
            copy.start()
    row = lax.broadcasted_iota(jnp.int32, (256, 256), 0)
    col = lax.broadcasted_iota(jnp.int32, (256, 256), 1)
    before = ((row < col) & ((row < 128) == (col < 128))).astype(BF)
    slot = lax.broadcasted_iota(jnp.int32, (2 * CAP, 256), 0).astype(F32)
    base = jnp.where(lax.broadcasted_iota(jnp.int32, (8, 256), 1) < 128, 0.0, float(CAP))
    for copy in loads:
        copy.wait()

    def places(i):
        named = table[i] > 0.0
        rank = jnp.dot(named.astype(F32).astype(BF), before, preferred_element_type=F32) + base
        rank = jnp.where(named, rank, -1.0)
        return [slot == rank[e:e + 1, :] for e in range(3)]

    def take(i, carry):
        spots = places(i)
        block = jnp.concatenate([x[2 * i], x[2 * i + 1]])
        hot = jnp.concatenate([jnp.where(p, 1.0, 0.0) for p in spots]).astype(BF)
        rows = jnp.dot(hot, block, preferred_element_type=F32).astype(BF)
        at = pl.ds(pl.multiple_of(i * 2 * CAP, 16), 2 * CAP)
        given = table[i]
        for e in range(3):
            xe[e, at, :] = rows[e * 2 * CAP:(e + 1) * 2 * CAP]
            scale[e, at, :] = jnp.sum(jnp.where(spots[e], given[e:e + 1, :], 0.0), axis=1,
                                      keepdims=True)
        return carry

    lax.fori_loop(0, pairs, take, 0)
    size = min(rows_all, 320)

    def ffn(e, count):
        for h in range(count):
            for k, (src, dst) in enumerate([(gate_hbm, gate), (up_hbm, up)]):
                pltpu.make_async_copy(src.at[0], dst.at[0], sem_w.at[6 * e + 3 * h + k]).wait()
            pltpu.make_async_copy(down_hbm.at[0], down.at[pl.ds(0, 256)],
                                  sem_w.at[6 * e + 3 * h + 2]).wait()

        def run(c, carry):
            at = pl.ds(pl.multiple_of(c * size, 16), size)
            rows = xe[e, at, :]
            hidden = []
            for h in range(count):
                g = jnp.dot(rows, gate[2 * e + h], preferred_element_type=F32)
                u = jnp.dot(rows, up[2 * e + h], preferred_element_type=F32)
                hidden.append((g / (1.0 + jnp.exp(-g)) * u).astype(BF))
            hidden = jnp.concatenate(hidden, axis=1)
            maps = down[pl.ds(pl.multiple_of(512 * e, 256), 256 * count), :]
            out = jnp.dot(hidden, maps, preferred_element_type=F32)
            ho[e, at, :] = (out * scale[e, at, :]).astype(BF)
            return carry

        lax.fori_loop(0, rows_all // size, run, 0)

    def whole(e, carry):
        ffn(e, 2)
        return carry

    lax.fori_loop(0, 2, whole, 0)
    ffn(2, 1)

    def combine(i, carry):
        hot = jnp.concatenate([jnp.where(p, 1.0, 0.0) for p in places(i)]).astype(BF)
        at = pl.ds(pl.multiple_of(i * 2 * CAP, 16), 2 * CAP)
        rows = jnp.concatenate([ho[e, at, :] for e in range(3)])
        total = lax.dot_general(hot, rows, (((0,), (0,)), ((), ())),
                                preferred_element_type=F32).astype(BF)
        x[2 * i] = total[:128]
        x[2 * i + 1] = total[128:]
        return carry

    lax.fori_loop(0, pairs, combine, 0)
    stores = [pltpu.make_async_copy(x.at[pl.ds(starts[k], sizes[k])], outs[k], sem_o.at[k])
              for k in range(n)]
    for copy in stores:
        copy.start()
    for copy in stores:
        copy.wait()


def experts(pieces, first, table, gate, up, down):
    sizes = [piece.shape[0] for piece in pieces]
    total, width = sum(sizes), gate.shape[1]
    rows = total * CAP
    anywhere = pl.BlockSpec(memory_space=pl.ANY)
    vm = pl.BlockSpec(memory_space=pltpu.VMEM)
    return pl.pallas_call(
        functools.partial(expert_kernel, sizes),
        out_shape=tuple(jax.ShapeDtypeStruct(piece.shape, BF) for piece in pieces),
        in_specs=[anywhere] * len(sizes) + [pl.BlockSpec(memory_space=pltpu.SMEM), vm]
        + [anywhere] * 3,
        out_specs=(anywhere,) * len(sizes),
        scratch_shapes=[
            pltpu.VMEM((total, 128, width), BF), pltpu.VMEM((3, rows, width), BF),
            pltpu.VMEM((3, rows, width), BF), pltpu.VMEM((3, rows, 1), F32),
            pltpu.VMEM(gate.shape, BF), pltpu.VMEM(up.shape, BF),
            pltpu.VMEM((5 * 256, width), BF),
            pltpu.SemaphoreType.DMA((len(sizes),)), pltpu.SemaphoreType.DMA((15,)),
            pltpu.SemaphoreType.DMA((len(sizes),)),
        ],
        compiler_params=pltpu.CompilerParams(vmem_limit_bytes=44 << 20),
        cost_estimate=pl.CostEstimate(flops=rows * 6 * 1536 * 256 * 5, transcendentals=0,
                                      bytes_accessed=12 << 20),
        name="expert_block",
    )(*pieces, first, table, gate, up, down)


def rms_scaled(features, scales):
    features = features.astype(F32)
    inverse = lax.rsqrt(jnp.mean(features * features, axis=-1, keepdims=True) + EPSILON)
    return (features * inverse * scales).astype(BF)


def body(tokens, lengths, prompt_adapter, routes, routing_weight, attention_gain, query_weight,
         key_weight, value_weight, output_weight, adapter_down_maps, adapter_up_query_output,
         adapter_up_key_value, expert_gain, gate_weight, up_weight, down_weight, closing_gain,
         vocab_projection):
    own = tokens[0]
    count, width = own.shape
    me, grp = lax.axis_index("seq"), lax.axis_index("grp")

    listing = np.concatenate([np.array([0, 1, 2] if g % 2 == 0 else [1, 2, 0]) + 5 * g // 2
                              for g in range(16)]).astype(np.int32)
    ids, given = routes[0], routing_weight[0]
    table = jnp.sum(jnp.where(ids.T[None] == jnp.asarray(listing)[:, None, None],
                              given.T[None], 0.0), axis=1).reshape(16, 3 * count)
    high = lax.reduce_precision(table, 8, 7)
    low = table - high
    route_rows = jnp.concatenate(
        [high, low, jnp.zeros((16, width - 6 * count), F32)], axis=1).astype(BF)

    ranks = (jnp.arange(16, dtype=jnp.int32)[:, None]
             == 2 * me + jnp.arange(2, dtype=jnp.int32)[None, :]).astype(BF)
    downs = jnp.einsum("rk,pdr->pkd", ranks, adapter_down_maps[:, 0],
                       preferred_element_type=F32).astype(BF).reshape(8, width)
    ups = lax.dynamic_slice_in_dim(adapter_up_query_output[:, 0], 2 * me, 2, 1).reshape(4, width)
    thin = lax.dynamic_slice_in_dim(adapter_up_key_value[:, 0], 2 * me, 2, 1)
    thin = jnp.concatenate([thin[0], thin[1], jnp.zeros((2, width - 1024), BF)], axis=1)
    maps = jnp.concatenate([downs, ups, thin], axis=0)
    payload = jnp.concatenate(
        [jnp.broadcast_to(maps[None], (16, 14, width)), route_rows[:, None, :],
         jnp.zeros((16, 1, width), BF)], axis=1)
    payload, own = lax.optimization_barrier((payload, own))
    held = lax.all_to_all(payload, "grp", 0, 0, tiled=True)
    back1 = lax.ppermute(own, "seq", [(s, s + 2) for s in range(6)])
    back2 = lax.ppermute(own, "seq", [(s, s + 4) for s in range(4)])
    lens = lengths[0]
    ends = jnp.cumsum(lens)
    starts = ends - lens
    blocks = me - jnp.array([0, 2, 4, 1, 3], jnp.int32)
    row = jnp.arange(count, dtype=jnp.int32)
    index = (blocks[:, None] * count + row[None, :]).reshape(-1)
    document = jnp.sum((index[:, None] >= ends[None, :]).astype(jnp.int32), axis=1)
    half = HEAD // 2
    frequency = ROPE_BASE ** (-(jnp.arange(128, dtype=jnp.int32) % half).astype(F32) / half)
    sign = jnp.where(jnp.arange(128) % HEAD < half, -1.0, 1.0).astype(F32)
    near = row.astype(F32)[:, None] * frequency[None, :]
    far = (blocks[:, None] * count - starts[None, :]).astype(F32)[:, :, None] * frequency
    near_cos, near_sin = jnp.cos(near)[None], jnp.sin(near)[None]
    far_cos, far_sin = jnp.cos(far), jnp.sin(far)

    def by_document(values):
        docs = document.reshape(5, count, 1)
        return jnp.where(docs == 0, values[:, None, 0], jnp.where(
            docs == 1, values[:, None, 1], values[:, None, 2]))

    far_cos, far_sin = by_document(far_cos), by_document(far_sin)
    cosine = (far_cos * near_cos - far_sin * near_sin).reshape(5 * count, 128)
    sine = ((far_sin * near_cos + far_cos * near_sin) * sign).reshape(5 * count, 128)
    row_index = index[:count]
    columns = jnp.arange(384, dtype=jnp.int32)[None, :]
    key_document = jnp.where(index >= 0, document, -1)

    held, cosine, sine, document, index, key_document, row_index = lax.optimization_barrier(
        (held, cosine, sine, document, index, key_document, row_index))
    picked = jnp.stack([lax.dynamic_index_in_dim(held, prompt_adapter[0, p], 0, False)
                        for p in range(3)]).reshape(48, width)
    turn = [picked] + [lax.ppermute(picked, "seq", [(s, (s + d) % 8) for s in range(8)])
                       for d in (2, 6, 4)]
    adapt = turn + [partner(piece) for piece in turn]
    odd_core = me % 2 == 1
    tok = [own, back1, back2, partner(jnp.where(odd_core, back1, own)),
           partner(jnp.where(odd_core, back2, back1))]
    base = base_projections(tok, attention_gain[None], query_weight, key_weight, value_weight)

    mixed, moe_in = attention(
        adapt, own, *base, expert_gain[None], cosine, sine, key_document[None], index[None],
        document[:, None], row_index[:, None], columns // 16 % 3, columns % 16, output_weight)

    rel = jnp.array([0, 3, 1, 2], jnp.int32)
    first, second = jnp.where(me % 2 == 0, grp % 4, grp // 4), jnp.where(
        me % 2 == 0, grp // 4, grp % 4)
    first, second = (first + rel[None, :]) % 4, (second + rel[:, None]) % 4
    source = jnp.where(me % 2 == 0, second * 4 + first, first * 4 + second).reshape(16)
    order = (source[:, None] == jnp.arange(16, dtype=jnp.int32)[None, :]).astype(F32)
    route_in = jnp.dot(order, held[:, 14, :].astype(F32), precision=lax.Precision.HIGHEST)
    route_in = (route_in[:, :3 * count] + route_in[:, 3 * count:6 * count]).reshape(8, 2, 3, count)
    route_in = jnp.concatenate([route_in, jnp.zeros((8, 2, 5, count), F32)], axis=2)
    route_in = route_in.transpose(0, 2, 1, 3).reshape(8, 8, 2 * count)
    odd = (grp % 2).astype(jnp.int32)[None]
    weights = (gate_weight, up_weight, down_weight)

    def share(pieces, which):
        return experts(pieces, odd, jnp.stack([route_in[k] for k in which]), *weights)

    line = lax.optimization_barrier(
        [shift(moe_in, 0, 1), shift(moe_in, 0, -1), shift(moe_in, 0, 2)])
    own_lo, own_hi = jnp.stack([moe_in, line[0]]), jnp.stack([line[1], line[2]])
    minus_lo, plus_hi = shift(own_lo, 1, 1), shift(own_hi, 1, -1)
    minus_hi, plus_lo = shift(own_hi, 1, 1), shift(own_lo, 1, -1)
    own_lo, own_hi = share([own_lo, own_hi], (0, 1))
    minus_lo, plus_hi, own_lo, own_hi = lax.optimization_barrier(
        (minus_lo, plus_hi, own_lo, own_hi))
    first_lo, first_hi = share([minus_lo, plus_hi], (2, 5))
    minus_lo, plus_hi, minus_hi, plus_lo, first_lo, first_hi = lax.optimization_barrier(
        (minus_lo, plus_hi, minus_hi, plus_lo, first_lo, first_hi))
    far_lo, far_hi = shift(minus_lo, 1, 1), shift(plus_hi, 1, -1)
    minus_hi, plus_lo = share([minus_hi, plus_lo], (3, 4))
    minus_lo, plus_hi, minus_hi, plus_lo, far_lo, far_hi = lax.optimization_barrier(
        (first_lo, first_hi, minus_hi, plus_lo, far_lo, far_hi))

    minus_lo, plus_hi = shift(minus_lo, 1, -1), shift(plus_hi, 1, 1)
    far_lo, far_hi = share([far_lo, far_hi], (6, 7))
    minus_lo, plus_hi, far_lo, far_hi = lax.optimization_barrier(
        (minus_lo, plus_hi, far_lo, far_hi))
    far_lo, far_hi = lax.optimization_barrier((shift(far_lo, 1, 1), shift(far_hi, 1, -1)))
    plus_lo = shift((wide(plus_lo) + wide(far_lo)).astype(BF), 1, 1)
    minus_hi = shift((wide(minus_hi) + wide(far_hi)).astype(BF), 1, -1)
    minus_lo, plus_hi, minus_hi, plus_lo = lax.optimization_barrier(
        (minus_lo, plus_hi, minus_hi, plus_lo))
    own_lo = wide(own_lo) + wide(plus_lo) + wide(minus_lo)
    own_hi = wide(own_hi) + wide(plus_hi) + wide(minus_hi)
    line = lax.optimization_barrier(
        [shift(own_hi[0].astype(BF), 0, 1), shift(own_lo[1].astype(BF), 0, -1),
         shift(own_hi[1].astype(BF), 0, 2)])
    combined = own_lo[0] + wide(line[0]) + wide(line[1]) + wide(line[2])
    hidden_out = (mixed.astype(F32) + combined).astype(BF)

    selector = (ends[:, None] - 1 == row_index[None, :]).astype(BF)
    last = jnp.dot(selector, hidden_out, preferred_element_type=F32)
    last = rms_scaled(last, closing_gain)
    part = width // 8
    split = last.reshape(3, 8, part).transpose(1, 0, 2)
    mine = lax.all_to_all(split, "seq", 0, 0, tiled=True)
    mine = jnp.sum(mine.astype(F32), axis=0).astype(BF)
    everyone = lax.all_to_all(jnp.broadcast_to(mine[None], (128, 3, part)), WHOLE, 0, 0,
                              tiled=True)
    final_rows = everyone.reshape(8, 48, part).transpose(1, 0, 2).reshape(48, width)
    logits = jnp.dot(final_rows, vocab_projection, preferred_element_type=F32)
    top = jnp.max(logits, axis=1)
    mass = jnp.sum(jnp.exp(logits - top[:, None]), axis=1)
    stats = jnp.concatenate([top, mass, jnp.zeros((32,), F32)])
    stats = lax.all_to_all(jnp.broadcast_to(stats[None], (128, 128)), WHOLE, 0, 0, tiled=True)
    tops = stats[:, :48]
    peak = jnp.max(tops, axis=0)
    total = jnp.sum(stats[:, 48:96] * jnp.exp(tops - peak[None]), axis=0)
    log_probs = logits - (peak + jnp.log(total))[:, None]
    return hidden_out[None], log_probs


def solution(mesh):
    placed = (
        P("grp", "seq", None), P("grp", None), P("grp", None), P("grp", "seq", None),
        P("grp", "seq", None), P(), P(), P(), P(), P(), P(None, "grp", None, None),
        P(None, "grp", None, None), P(None, "grp", None, None), P(), P("grp", None, None),
        P("grp", None, None), P("grp", None, None), P(), P(None, WHOLE),
    )
    return jax.shard_map(
        body,
        mesh=mesh,
        in_specs=placed,
        out_specs=(P("grp", "seq", None), P(None, WHOLE)),
        check_vma=False,
    )
```

```python
import functools

import jax
import jax.numpy as jnp
import numpy as np
from jax import lax
from jax.experimental import pallas as pl
from jax.experimental.pallas import tpu as pltpu
from jax.sharding import PartitionSpec as P

HEADS = 24
KV_HEADS = 8
HEAD = 64
EXPERTS = 40
TOP = 8
CAP = 40
KERNEL_VMEM = 63 << 20
EPSILON = 1e-05
ROPE_BASE = 10000.0
MASKED = -1e30
SIDE = 4
BF = jnp.bfloat16
F32 = jnp.float32
WHOLE = ("seq", "grp")


def shift(rows, phase, step):
    pairs = []
    for s in range(8):
        for i in range(16):
            if s % 2 == phase:
                to = i // SIDE * SIDE + (i % SIDE + step) % SIDE
            else:
                to = (i // SIDE + step) % SIDE * SIDE + i % SIDE
            pairs.append((s * 16 + i, s * 16 + to))
    return lax.ppermute(rows, WHOLE, pairs)


def partner(rows):
    return lax.ppermute(rows, "seq", [(s, s ^ 1) for s in range(8)])


def wide(v):
    return v.astype(F32)


def dot_t(lhs, rhs):
    return lax.dot_general(lhs, rhs, (((1,), (1,)), ((), ())), preferred_element_type=F32)


def norm(rows, scale):
    inverse = lax.rsqrt(jnp.mean(rows * rows, axis=-1, keepdims=True) + EPSILON)
    return (rows * inverse * scale).astype(BF)


def base_kernel(t0, t1, t2, t3, t4, gain, wq_hbm, wk_hbm, wv_hbm, xn, base_q, base_k, base_v,
                wq, wk, wv, sems):
    copies = [pltpu.make_async_copy(src, dst, sems.at[i]) for i, (src, dst) in enumerate(
        [(wk_hbm, wk), (wv_hbm, wv), (wq_hbm, wq)])]
    for copy in copies:
        copy.start()
    count = t0.shape[0]
    for b, rows in enumerate((t0, t1, t2, t3, t4)):
        xn[b * count:(b + 1) * count, :] = norm(rows[...].astype(F32), gain[...])
    copies[0].wait()
    copies[1].wait()

    def key_block(b, carry):
        at = pl.ds(pl.multiple_of(b * 320, 320), 320)
        rows = xn[at, :]
        base_k[at, :] = jnp.dot(rows, wk[...], preferred_element_type=F32)
        base_v[at, :] = jnp.dot(rows, wv[...], preferred_element_type=F32)
        return carry

    lax.fori_loop(0, 2, key_block, 0)
    copies[2].wait()
    own = xn[0:count, :]

    def query_block(c, carry):
        at = pl.ds(pl.multiple_of(c * 512, 512), 512)
        base_q[:, at] = jnp.dot(own, wq[:, at], preferred_element_type=F32)
        return carry

    lax.fori_loop(0, 3, query_block, 0)


def base_projections(tok, gain, wq, wk, wv):
    count, width = tok[0].shape
    vm = pl.BlockSpec(memory_space=pltpu.VMEM)
    anywhere = pl.BlockSpec(memory_space=pl.ANY)
    return pl.pallas_call(
        base_kernel,
        out_shape=(jax.ShapeDtypeStruct((5 * count, width), BF),
                   jax.ShapeDtypeStruct((count, width), F32),
                   jax.ShapeDtypeStruct((5 * count, 512), F32),
                   jax.ShapeDtypeStruct((5 * count, 512), F32)),
        in_specs=[vm] * 6 + [anywhere] * 3,
        out_specs=(vm,) * 4,
        scratch_shapes=[
            pltpu.VMEM(wq.shape, BF), pltpu.VMEM(wk.shape, BF), pltpu.VMEM(wv.shape, BF),
            pltpu.SemaphoreType.DMA((3,)),
        ],
        compiler_params=pltpu.CompilerParams(vmem_limit_bytes=KERNEL_VMEM),
        cost_estimate=pl.CostEstimate(flops=5 << 30, transcendentals=0,
                                      bytes_accessed=14 << 20),
        name="base_block",
    )(*tok, gain, wq, wk, wv)


def attention_kernel(*refs):
    adapt = refs[0:8]
    (tok, gain_moe, cosine, sine, key_doc, key_index, doc, index, colp, colr, xn_hbm, q_hbm,
     k_hbm, v_hbm, wo_hbm, mixed_out, moe_out, wo, xn, base_q, base_k, base_v, ad, qbuf, kbuf,
     vbuf, att, score, prob, sems) = refs[8:]
    loads = [pltpu.make_async_copy(src, dst, sems.at[i]) for i, (src, dst) in enumerate(
        [(xn_hbm, xn), (k_hbm, base_k), (v_hbm, base_v), (q_hbm, base_q), (wo_hbm, wo)])]
    for load in loads:
        load.start()
    count = tok.shape[0]
    for j in range(8):
        ad[48 * j:48 * j + 48, :] = adapt[j][...]
    col_prompt = colp[...]
    col_row = colr[...]

    def low(z, roll, first, docs):
        moved = pltpu.roll(z, roll, 1)
        keep = (docs == col_prompt) & (col_row >= first) & (col_row < first + 2)
        return jnp.where(keep, moved, 0.0).astype(BF)

    lane = lax.broadcasted_iota(jnp.int32, (count, 128), 1)
    lower = (lane & 63) < 32

    def rope(u, cos_t, sin_t):
        turned = jnp.where(lower, pltpu.roll(u, 96, 1), pltpu.roll(u, 32, 1))
        return u * cos_t + turned * sin_t

    def key_block(b, carry):
        at = pl.ds(pl.multiple_of(b * count, count), count)
        docs = doc[at, :]
        z = dot_t(xn[at, :], ad[...])
        keys = base_k[at, :] + jnp.dot(
            low(z, 10, 12, docs), ad[:, :512], preferred_element_type=F32)
        values = base_v[at, :] + jnp.dot(
            low(z, 8, 12, docs), ad[:, 512:1024], preferred_element_type=F32)
        vbuf[at, :] = values.astype(BF)
        cos_t = cosine[at, :]
        sin_t = sine[at, :]
        for c in range(4):
            kbuf[at, 128 * c:128 * c + 128] = rope(
                keys[:, 128 * c:128 * c + 128], cos_t, sin_t).astype(BF)
        return carry

    for load in loads[:3]:
        load.wait()
    lax.fori_loop(0, 5, key_block, 0)
    docs = doc[0:count, :]
    zq = low(dot_t(xn[0:count, :], ad[...]), 8, 8, docs)
    cos_t = cosine[0:count, :]
    sin_t = sine[0:count, :]
    low_half = lane < 64
    allowed = (docs == key_doc[...]) & (key_index[...] <= index[...])
    bias = jnp.where(allowed, 0.0, MASKED)

    def query_block(c, carry):
        at = pl.multiple_of(c * 384, 128)
        u = base_q[:, pl.ds(at, 384)] + jnp.dot(
            zq, ad[:, pl.ds(at, 384)], preferred_element_type=F32)
        for t in range(3):
            q = rope(u[:, 128 * t:128 * t + 128], cos_t, sin_t).astype(BF).astype(F32)
            q = q * (HEAD ** -0.5)
            turned = pltpu.roll(q, 64, 1)
            for own_low in (True, False):
                h = 2 * t + (0 if own_low else 1)
                kv_low = h < 3
                rows = q if own_low == kv_low else turned
                keep = low_half if kv_low else ~low_half
                qbuf[c, count * h:count * h + count, :] = jnp.where(keep, rows, 0.0).astype(BF)
        return carry

    loads[3].wait()
    lax.fori_loop(0, 4, query_block, 0)

    def pair(j, carry):
        kv = pl.ds(pl.multiple_of(j * 128, 128), 128)
        score[...] = dot_t(qbuf[j], kbuf[:, kv])
        totals = []
        for h in range(6):
            at = slice(count * h, count * h + count)
            s = score[at, :] + bias
            top = jnp.max(s, axis=-1, keepdims=True)
            w = jnp.exp(s - top)
            totals.append(jnp.sum(w, axis=-1, keepdims=True))
            prob[at, :] = w.astype(BF)
        out = jnp.dot(prob[...], vbuf[:, kv], preferred_element_type=F32)
        results = []
        for h in range(6):
            o = out[count * h:count * h + count] / totals[h]
            results.append(pltpu.roll(o, 64, 1) if (h % 2 == 0) != (h < 3) else o)
        for t in range(3):
            att[:, pl.ds(pl.multiple_of(j * 384 + 128 * t, 128), 128)] = jnp.where(
                low_half, results[2 * t], results[2 * t + 1]).astype(BF)
        return carry

    lax.fori_loop(0, 4, pair, 0)
    loads[4].wait()
    attended = att[...]
    zo = low(dot_t(attended, ad[...]), 4, 10, docs)
    mixed = (tok[...].astype(F32) + jnp.dot(attended, wo[...], preferred_element_type=F32)
             + jnp.dot(zo, ad[...], preferred_element_type=F32)).astype(BF)
    mixed_out[...] = mixed
    moe_out[...] = norm(mixed.astype(F32), gain_moe[...])


def attention(adapt, own, tables, base, wo):
    count, width = own.shape
    vm = pl.BlockSpec(memory_space=pltpu.VMEM)
    anywhere = pl.BlockSpec(memory_space=pl.ANY)
    rows = jax.ShapeDtypeStruct((count, width), BF)
    return pl.pallas_call(
        attention_kernel,
        out_shape=(rows, rows),
        in_specs=[vm] * (9 + len(tables)) + [anywhere] * 5,
        out_specs=(vm, vm),
        scratch_shapes=[
            pltpu.VMEM(wo.shape, BF), pltpu.VMEM(base[0].shape, BF),
            pltpu.VMEM(base[1].shape, F32), pltpu.VMEM(base[2].shape, F32),
            pltpu.VMEM(base[3].shape, F32), pltpu.VMEM((384, width), BF),
            pltpu.VMEM((4, 6 * count, 128), BF), pltpu.VMEM((5 * count, 512), BF),
            pltpu.VMEM((5 * count, 512), BF), pltpu.VMEM((count, width), BF),
            pltpu.VMEM((6 * count, 5 * count), F32), pltpu.VMEM((6 * count, 5 * count), BF),
            pltpu.SemaphoreType.DMA((5,)),
        ],
        compiler_params=pltpu.CompilerParams(vmem_limit_bytes=KERNEL_VMEM),
        cost_estimate=pl.CostEstimate(flops=6 << 30, transcendentals=0,
                                      bytes_accessed=16 << 20),
        name="attention_block",
    )(*adapt, own, *tables, *base, wo)


def expert_kernel(sizes, *refs):
    n = len(sizes)
    pieces, (first, table, gate_hbm, up_hbm, down_hbm) = refs[:n], refs[n:n + 5]
    outs = refs[n + 5:2 * n + 5]
    x, xe, ho, scale, gate, up, down, sem_x, sem_w, sem_o = refs[2 * n + 5:]
    pairs = sum(sizes) // 2
    rows_all = pairs * 2 * CAP
    starts = [sum(sizes[:k]) for k in range(n)]
    loads = [pltpu.make_async_copy(pieces[k], x.at[pl.ds(starts[k], sizes[k])], sem_x.at[k])
             for k in range(n)]
    for copy in loads:
        copy.start()
    odd = first[0]
    order = [odd, odd + 1, odd + 2, odd + 3, 4 - 4 * odd]
    weights = []
    for s in range(5):
        weights.append([pltpu.make_async_copy(src.at[order[s]], dst, sem_w.at[3 * s + k])
                        for k, (src, dst) in enumerate(
                            [(gate_hbm, gate.at[s]), (up_hbm, up.at[s]),
                             (down_hbm, down.at[pl.ds(256 * s, 256)])])])
        for copy in weights[-1]:
            copy.start()
    row = lax.broadcasted_iota(jnp.int32, (256, 256), 0)
    col = lax.broadcasted_iota(jnp.int32, (256, 256), 1)
    before = ((row < col) & ((row < 128) == (col < 128))).astype(BF)
    slot = lax.broadcasted_iota(jnp.int32, (2 * CAP, 256), 0).astype(F32)
    base = jnp.where(lax.broadcasted_iota(jnp.int32, (8, 256), 1) < 128, 0.0, float(CAP))
    for copy in loads:
        copy.wait()

    def places(i):
        named = table[i] > 0.0
        rank = jnp.dot(named.astype(F32).astype(BF), before, preferred_element_type=F32) + base
        rank = jnp.where(named, rank, -1.0)
        return [slot == rank[e:e + 1, :] for e in range(3)]

    def take(i, carry):
        spots = places(i)
        block = jnp.concatenate([x[2 * i], x[2 * i + 1]])
        hot = jnp.concatenate([jnp.where(p, 1.0, 0.0) for p in spots]).astype(BF)
        rows = jnp.dot(hot, block, preferred_element_type=F32).astype(BF)
        at = pl.ds(pl.multiple_of(i * 2 * CAP, 16), 2 * CAP)
        given = table[i]
        for e in range(3):
            xe[e, at, :] = rows[e * 2 * CAP:(e + 1) * 2 * CAP]
            scale[e, at, :] = jnp.sum(jnp.where(spots[e], given[e:e + 1, :], 0.0), axis=1,
                                      keepdims=True)
        return carry

    lax.fori_loop(0, pairs, take, 0)
    size = min(rows_all, 320)

    def ffn(e, count):
        for h in range(count):
            for k, (src, dst) in enumerate([(gate_hbm, gate), (up_hbm, up)]):
                pltpu.make_async_copy(src.at[0], dst.at[0], sem_w.at[6 * e + 3 * h + k]).wait()
            pltpu.make_async_copy(down_hbm.at[0], down.at[pl.ds(0, 256)],
                                  sem_w.at[6 * e + 3 * h + 2]).wait()

        def run(c, carry):
            at = pl.ds(pl.multiple_of(c * size, 16), size)
            rows = xe[e, at, :]
            hidden = []
            for h in range(count):
                g = jnp.dot(rows, gate[2 * e + h], preferred_element_type=F32)
                u = jnp.dot(rows, up[2 * e + h], preferred_element_type=F32)
                hidden.append((g / (1.0 + jnp.exp(-g)) * u).astype(BF))
            hidden = jnp.concatenate(hidden, axis=1)
            maps = down[pl.ds(pl.multiple_of(512 * e, 256), 256 * count), :]
            out = jnp.dot(hidden, maps, preferred_element_type=F32)
            ho[e, at, :] = (out * scale[e, at, :]).astype(BF)
            return carry

        lax.fori_loop(0, rows_all // size, run, 0)

    def whole(e, carry):
        ffn(e, 2)
        return carry

    lax.fori_loop(0, 2, whole, 0)
    ffn(2, 1)

    def combine(i, carry):
        hot = jnp.concatenate([jnp.where(p, 1.0, 0.0) for p in places(i)]).astype(BF)
        at = pl.ds(pl.multiple_of(i * 2 * CAP, 16), 2 * CAP)
        rows = jnp.concatenate([ho[e, at, :] for e in range(3)])
        total = lax.dot_general(hot, rows, (((0,), (0,)), ((), ())),
                                preferred_element_type=F32).astype(BF)
        x[2 * i] = total[:128]
        x[2 * i + 1] = total[128:]
        return carry

    lax.fori_loop(0, pairs, combine, 0)
    stores = [pltpu.make_async_copy(x.at[pl.ds(starts[k], sizes[k])], outs[k], sem_o.at[k])
              for k in range(n)]
    for copy in stores:
        copy.start()
    for copy in stores:
        copy.wait()


def experts(pieces, first, table, gate, up, down):
    sizes = [piece.shape[0] for piece in pieces]
    total, width = sum(sizes), gate.shape[1]
    rows = total * CAP
    anywhere = pl.BlockSpec(memory_space=pl.ANY)
    vm = pl.BlockSpec(memory_space=pltpu.VMEM)
    return pl.pallas_call(
        functools.partial(expert_kernel, sizes),
        out_shape=tuple(jax.ShapeDtypeStruct(piece.shape, BF) for piece in pieces),
        in_specs=[anywhere] * len(sizes) + [pl.BlockSpec(memory_space=pltpu.SMEM), vm]
        + [anywhere] * 3,
        out_specs=(anywhere,) * len(sizes),
        scratch_shapes=[
            pltpu.VMEM((total, 128, width), BF), pltpu.VMEM((3, rows, width), BF),
            pltpu.VMEM((3, rows, width), BF), pltpu.VMEM((3, rows, 1), F32),
            pltpu.VMEM(gate.shape, BF), pltpu.VMEM(up.shape, BF),
            pltpu.VMEM((5 * 256, width), BF),
            pltpu.SemaphoreType.DMA((len(sizes),)), pltpu.SemaphoreType.DMA((15,)),
            pltpu.SemaphoreType.DMA((len(sizes),)),
        ],
        compiler_params=pltpu.CompilerParams(vmem_limit_bytes=KERNEL_VMEM),
        cost_estimate=pl.CostEstimate(flops=rows * 6 * 1536 * 256 * 5, transcendentals=0,
                                      bytes_accessed=12 << 20),
        name="expert_block",
    )(*pieces, first, table, gate, up, down)


def rms_scaled(features, scales):
    features = features.astype(F32)
    inverse = lax.rsqrt(jnp.mean(features * features, axis=-1, keepdims=True) + EPSILON)
    return (features * inverse * scales).astype(BF)


def body(tokens, lengths, prompt_adapter, routes, routing_weight, attention_gain, query_weight,
         key_weight, value_weight, output_weight, adapter_down_maps, adapter_up_query_output,
         adapter_up_key_value, expert_gain, gate_weight, up_weight, down_weight, closing_gain,
         vocab_projection):
    own = tokens[0]
    count, width = own.shape
    me, grp = lax.axis_index("seq"), lax.axis_index("grp")

    listing = np.concatenate([np.array([0, 1, 2] if g % 2 == 0 else [1, 2, 0]) + 5 * g // 2
                              for g in range(16)]).astype(np.int32)
    ids, given = routes[0], routing_weight[0]
    table = jnp.sum(jnp.where(ids.T[None] == jnp.asarray(listing)[:, None, None],
                              given.T[None], 0.0), axis=1).reshape(16, 3 * count)
    high = lax.reduce_precision(table, 8, 7)
    low = table - high
    route_rows = jnp.concatenate(
        [high, low, jnp.zeros((16, width - 6 * count), F32)], axis=1).astype(BF)

    ranks = (jnp.arange(16, dtype=jnp.int32)[:, None]
             == 2 * me + jnp.arange(2, dtype=jnp.int32)[None, :]).astype(BF)
    downs = jnp.einsum("rk,pdr->pkd", ranks, adapter_down_maps[:, 0],
                       preferred_element_type=F32).astype(BF).reshape(8, width)
    ups = lax.dynamic_slice_in_dim(adapter_up_query_output[:, 0], 2 * me, 2, 1).reshape(4, width)
    thin = lax.dynamic_slice_in_dim(adapter_up_key_value[:, 0], 2 * me, 2, 1)
    thin = jnp.concatenate([thin[0], thin[1], jnp.zeros((2, width - 1024), BF)], axis=1)
    maps = jnp.concatenate([downs, ups, thin], axis=0)
    payload = jnp.concatenate(
        [jnp.broadcast_to(maps[None], (16, 14, width)), route_rows[:, None, :],
         jnp.zeros((16, 1, width), BF)], axis=1)
    payload, own = lax.optimization_barrier((payload, own))
    held = lax.all_to_all(payload, "grp", 0, 0, tiled=True)
    back1 = lax.ppermute(own, "seq", [(s, s + 2) for s in range(6)])
    back2 = lax.ppermute(own, "seq", [(s, s + 4) for s in range(4)])
    odd_core = me % 2 == 1
    tok = [own, back1, back2, partner(jnp.where(odd_core, back1, own)),
           partner(jnp.where(odd_core, back2, back1))]

    lens = lengths[0]
    ends = jnp.cumsum(lens)
    starts = ends - lens
    blocks = me - jnp.array([0, 2, 4, 1, 3], jnp.int32)
    row = jnp.arange(count, dtype=jnp.int32)
    index = (blocks[:, None] * count + row[None, :]).reshape(-1)
    document = jnp.sum((index[:, None] >= ends[None, :]).astype(jnp.int32), axis=1)
    half = HEAD // 2
    frequency = ROPE_BASE ** (-(jnp.arange(128, dtype=jnp.int32) % half).astype(F32) / half)
    sign = jnp.where(jnp.arange(128) % HEAD < half, -1.0, 1.0).astype(F32)
    near = row.astype(F32)[:, None] * frequency[None, :]
    far = (blocks[:, None] * count - starts[None, :]).astype(F32)[:, :, None] * frequency
    near_cos, near_sin = jnp.cos(near)[None], jnp.sin(near)[None]
    far_cos, far_sin = jnp.cos(far), jnp.sin(far)

    def by_document(values):
        docs = document.reshape(5, count, 1)
        return jnp.where(docs == 0, values[:, None, 0], jnp.where(
            docs == 1, values[:, None, 1], values[:, None, 2]))

    far_cos, far_sin = by_document(far_cos), by_document(far_sin)
    cosine = (far_cos * near_cos - far_sin * near_sin).reshape(5 * count, 128)
    sine = ((far_sin * near_cos + far_cos * near_sin) * sign).reshape(5 * count, 128)
    row_index = index[:count]
    columns = jnp.arange(384, dtype=jnp.int32)[None, :]
    key_document = jnp.where(index >= 0, document, -1)

    held, cosine, sine, document, index, key_document, row_index = lax.optimization_barrier(
        (held, cosine, sine, document, index, key_document, row_index))
    picked = jnp.stack([lax.dynamic_index_in_dim(held, prompt_adapter[0, p], 0, False)
                        for p in range(3)]).reshape(48, width)
    turn = [picked] + [lax.ppermute(picked, "seq", [(s, (s + d) % 8) for s in range(8)])
                       for d in (2, 6, 4)]
    base = base_projections(tok, attention_gain[None], query_weight, key_weight, value_weight)
    rel = jnp.array([0, 3, 1, 2], jnp.int32)
    first, second = jnp.where(me % 2 == 0, grp % 4, grp // 4), jnp.where(
        me % 2 == 0, grp // 4, grp % 4)
    first, second = (first + rel[None, :]) % 4, (second + rel[:, None]) % 4
    source = jnp.where(me % 2 == 0, second * 4 + first, first * 4 + second).reshape(16)
    order = (source[:, None] == jnp.arange(16, dtype=jnp.int32)[None, :]).astype(F32)
    route_in = jnp.dot(order, held[:, 14, :].astype(F32), precision=lax.Precision.HIGHEST)
    route_in = (route_in[:, :3 * count] + route_in[:, 3 * count:6 * count]).reshape(8, 2, 3, count)
    route_in = jnp.concatenate([route_in, jnp.zeros((8, 2, 5, count), F32)], axis=2)
    route_in = route_in.transpose(0, 2, 1, 3).reshape(8, 8, 2 * count)
    odd = (grp % 2).astype(jnp.int32)[None]
    weights = (gate_weight, up_weight, down_weight)

    shares = {pair: jnp.stack([route_in[k] for k in pair])
              for pair in ((0, 1), (2, 5), (3, 4), (6, 7))}
    turn, base, shares = lax.optimization_barrier((turn, base, shares))
    adapt = turn + [partner(piece) for piece in turn]

    tables = [expert_gain[None], cosine, sine, key_document[None], index[None],
              document[:, None], row_index[:, None], columns // 16 % 3, columns % 16]
    mixed, moe_in = attention(adapt, own, tables, base, output_weight)

    def share(pieces, which):
        return experts(pieces, odd, shares[which], *weights)

    line = lax.optimization_barrier(
        [shift(moe_in, 0, 1), shift(moe_in, 0, -1), shift(moe_in, 0, 2)])
    own_lo, own_hi = jnp.stack([moe_in, line[0]]), jnp.stack([line[1], line[2]])
    minus_lo, plus_hi = shift(own_lo, 1, 1), shift(own_hi, 1, -1)
    minus_hi, plus_lo = shift(own_hi, 1, 1), shift(own_lo, 1, -1)
    own_lo, own_hi = share([own_lo, own_hi], (0, 1))
    minus_lo, plus_hi, own_lo, own_hi = lax.optimization_barrier(
        (minus_lo, plus_hi, own_lo, own_hi))
    first_lo, first_hi = share([minus_lo, plus_hi], (2, 5))
    minus_lo, plus_hi, minus_hi, plus_lo, first_lo, first_hi = lax.optimization_barrier(
        (minus_lo, plus_hi, minus_hi, plus_lo, first_lo, first_hi))
    far_lo, far_hi = shift(minus_lo, 1, 1), shift(plus_hi, 1, -1)
    minus_hi, plus_lo = share([minus_hi, plus_lo], (3, 4))
    minus_lo, plus_hi, minus_hi, plus_lo, far_lo, far_hi = lax.optimization_barrier(
        (first_lo, first_hi, minus_hi, plus_lo, far_lo, far_hi))

    minus_lo, plus_hi = shift(minus_lo, 1, -1), shift(plus_hi, 1, 1)
    far_lo, far_hi = share([far_lo, far_hi], (6, 7))
    far_lo, far_hi = lax.optimization_barrier((shift(far_lo, 1, 1), shift(far_hi, 1, -1)))
    plus_lo = shift((wide(plus_lo) + wide(far_lo)).astype(BF), 1, 1)
    minus_hi = shift((wide(minus_hi) + wide(far_hi)).astype(BF), 1, -1)
    minus_lo, plus_hi, minus_hi, plus_lo = lax.optimization_barrier(
        (minus_lo, plus_hi, minus_hi, plus_lo))
    own_lo = wide(own_lo) + wide(plus_lo) + wide(minus_lo)
    own_hi = wide(own_hi) + wide(plus_hi) + wide(minus_hi)
    line = lax.optimization_barrier(
        [shift(own_hi[0].astype(BF), 0, 1), shift(own_lo[1].astype(BF), 0, -1),
         shift(own_hi[1].astype(BF), 0, 2)])
    combined = own_lo[0] + wide(line[0]) + wide(line[1]) + wide(line[2])
    hidden_out = (mixed.astype(F32) + combined).astype(BF)

    selector = (ends[:, None] - 1 == row_index[None, :]).astype(BF)
    last = jnp.dot(selector, hidden_out, preferred_element_type=F32)
    last = rms_scaled(last, closing_gain)
    part = width // 8
    split = last.reshape(3, 8, part).transpose(1, 0, 2)
    mine = lax.all_to_all(split, "seq", 0, 0, tiled=True)
    mine = jnp.sum(mine.astype(F32), axis=0).astype(BF)
    everyone = lax.all_to_all(jnp.broadcast_to(mine[None], (128, 3, part)), WHOLE, 0, 0,
                              tiled=True)
    final_rows = everyone.reshape(8, 48, part).transpose(1, 0, 2).reshape(48, width)
    logits = jnp.dot(final_rows, vocab_projection, preferred_element_type=F32)
    top = jnp.max(logits, axis=1)
    mass = jnp.sum(jnp.exp(logits - top[:, None]), axis=1)
    stats = jnp.concatenate([top, mass, jnp.zeros((32,), F32)])
    stats = lax.all_to_all(jnp.broadcast_to(stats[None], (128, 128)), WHOLE, 0, 0, tiled=True)
    tops = stats[:, :48]
    peak = jnp.max(tops, axis=0)
    total = jnp.sum(stats[:, 48:96] * jnp.exp(tops - peak[None]), axis=0)
    log_probs = logits - (peak + jnp.log(total))[:, None]
    return hidden_out[None], log_probs


def solution(mesh):
    placed = (
        P("grp", "seq", None), P("grp", None), P("grp", None), P("grp", "seq", None),
        P("grp", "seq", None), P(), P(), P(), P(), P(), P(None, "grp", None, None),
        P(None, "grp", None, None), P(None, "grp", None, None), P(), P("grp", None, None),
        P("grp", None, None), P("grp", None, None), P(), P(None, WHOLE),
    )
    return jax.shard_map(
        body,
        mesh=mesh,
        in_specs=placed,
        out_specs=(P("grp", "seq", None), P(None, WHOLE)),
        check_vma=False,
    )
```

```python
import jax
import jax.numpy as jnp
import numpy as np
from jax import lax
from jax.experimental import pallas as pl
from jax.experimental.pallas import tpu as pltpu
from jax.sharding import PartitionSpec as P

HEADS = 24
KV_HEADS = 8
HEAD = 64
EXPERTS = 40
TOP = 8
CAP = 40
ATTENTION_VMEM = 63 << 20
EPSILON = 1e-05
ROPE_BASE = 10000.0
MASKED = -1e30
SIDE = 4
BF = jnp.bfloat16
F32 = jnp.float32
WHOLE = ("seq", "grp")


def shift(rows, phase, step):
    pairs = []
    for s in range(8):
        for i in range(16):
            if s % 2 == phase:
                to = i // SIDE * SIDE + (i % SIDE + step) % SIDE
            else:
                to = (i // SIDE + step) % SIDE * SIDE + i % SIDE
            pairs.append((s * 16 + i, s * 16 + to))
    return lax.ppermute(rows, WHOLE, pairs)


def partner(rows):
    return lax.ppermute(rows, "seq", [(s, s ^ 1) for s in range(8)])


def wide(v):
    return v.astype(F32)


def dot_t(lhs, rhs):
    return lax.dot_general(lhs, rhs, (((1,), (1,)), ((), ())), preferred_element_type=F32)


def norm(rows, scale):
    inverse = lax.rsqrt(jnp.mean(rows * rows, axis=-1, keepdims=True) + EPSILON)
    return (rows * inverse * scale).astype(BF)


def attention_kernel(*refs):
    tok = refs[0:5]
    adapt = refs[5:13]
    (place, gain, gain_moe, cosine, sine, wq_hbm, wk_hbm, wv_hbm, wo_hbm, mixed_out, moe_out,
     wq, wk, wv, wo, xn, ad, qbuf, kbuf, vbuf, att, score, prob, sems) = refs[13:]
    loads = [pltpu.make_async_copy(src, dst, sems.at[i]) for i, (src, dst) in enumerate(
        [(wk_hbm, wk), (wv_hbm, wv), (wq_hbm, wq), (wo_hbm, wo)])]
    for load in loads:
        load.start()
    count = tok[0].shape[0]
    ends = [place[0], place[1], place[2]]
    me = place[3]

    def document(index):
        return sum((index >= end).astype(jnp.int32) for end in ends)

    def block_start(b):
        return (me - jnp.where(b < 3, 2 * b, 2 * b - 5)) * count

    for j in range(8):
        ad[48 * j:48 * j + 48, :] = adapt[j][...]
    for b in range(5):
        xn[b * count:(b + 1) * count, :] = norm(tok[b][...].astype(F32), gain[...])
    column = lax.broadcasted_iota(jnp.int32, (1, 384), 1)
    col_row = column & 15
    col_prompt = column >> 4
    col_prompt = col_prompt - 3 * ((col_prompt * 171) >> 9)

    def low(z, roll, first, docs):
        moved = pltpu.roll(z, roll, 1)
        keep = (docs == col_prompt) & (col_row >= first) & (col_row < first + 2)
        return jnp.where(keep, moved, 0.0).astype(BF)

    lane = lax.broadcasted_iota(jnp.int32, (count, 128), 1)
    lower = (lane & 63) < 32
    down_rows = lax.broadcasted_iota(jnp.int32, (count, 1), 0)

    def rope(u, cos_t, sin_t):
        turned = jnp.where(lower, pltpu.roll(u, 96, 1), pltpu.roll(u, 32, 1))
        return u * cos_t + turned * sin_t

    loads[0].wait()
    loads[1].wait()

    def key_block(b, carry):
        at = pl.ds(pl.multiple_of(b * count, count), count)
        docs = document(block_start(b) + down_rows)
        rows = xn[at, :]
        z = dot_t(rows, ad[...])
        keys = jnp.dot(rows, wk[...], preferred_element_type=F32) + jnp.dot(
            low(z, 10, 12, docs), ad[:, :512], preferred_element_type=F32)
        values = jnp.dot(rows, wv[...], preferred_element_type=F32) + jnp.dot(
            low(z, 8, 12, docs), ad[:, 512:1024], preferred_element_type=F32)
        vbuf[at, :] = values.astype(BF)
        cos_t = cosine[at, :]
        sin_t = sine[at, :]
        for c in range(4):
            kbuf[at, 128 * c:128 * c + 128] = rope(
                keys[:, 128 * c:128 * c + 128], cos_t, sin_t).astype(BF)
        return carry

    lax.fori_loop(0, 5, key_block, 0)
    own_index = me * count + down_rows
    docs = document(own_index)
    own = xn[0:count, :]
    zq = low(dot_t(own, ad[...]), 8, 8, docs)
    cos_t = cosine[0:count, :]
    sin_t = sine[0:count, :]
    low_half = lane < 64
    along = lax.broadcasted_iota(jnp.int32, (1, count), 1)
    key_index = jnp.concatenate([block_start(b) + along for b in range(5)], axis=1)
    allowed = ((docs == document(key_index)) & (key_index <= own_index) & (key_index >= 0))
    bias = jnp.where(allowed, 0.0, MASKED)
    loads[2].wait()

    def query_block(c, carry):
        at = pl.multiple_of(c * 384, 128)
        u = jnp.dot(own, wq[:, pl.ds(at, 384)], preferred_element_type=F32) + jnp.dot(
            zq, ad[:, pl.ds(at, 384)], preferred_element_type=F32)
        for t in range(3):
            q = rope(u[:, 128 * t:128 * t + 128], cos_t, sin_t).astype(BF).astype(F32)
            q = q * (HEAD ** -0.5)
            turned = pltpu.roll(q, 64, 1)
            for own_low in (True, False):
                h = 2 * t + (0 if own_low else 1)
                kv_low = h < 3
                rows = q if own_low == kv_low else turned
                keep = low_half if kv_low else ~low_half
                qbuf[c, count * h:count * h + count, :] = jnp.where(keep, rows, 0.0).astype(BF)
        return carry

    lax.fori_loop(0, 4, query_block, 0)

    def pair(j, carry):
        kv = pl.ds(pl.multiple_of(j * 128, 128), 128)
        score[...] = dot_t(qbuf[j], kbuf[:, kv])
        totals = []
        for h in range(6):
            at = slice(count * h, count * h + count)
            s = score[at, :] + bias
            top = jnp.max(s, axis=-1, keepdims=True)
            w = jnp.exp(s - top)
            totals.append(jnp.sum(w, axis=-1, keepdims=True))
            prob[at, :] = w.astype(BF)
        out = jnp.dot(prob[...], vbuf[:, kv], preferred_element_type=F32)
        results = []
        for h in range(6):
            o = out[count * h:count * h + count] / totals[h]
            results.append(pltpu.roll(o, 64, 1) if (h % 2 == 0) != (h < 3) else o)
        for t in range(3):
            att[:, pl.ds(pl.multiple_of(j * 384 + 128 * t, 128), 128)] = jnp.where(
                low_half, results[2 * t], results[2 * t + 1]).astype(BF)
        return carry

    lax.fori_loop(0, 4, pair, 0)
    loads[3].wait()
    attended = att[...]
    zo = low(dot_t(attended, ad[...]), 4, 10, docs)
    mixed = (tok[0][...].astype(F32) + jnp.dot(attended, wo[...], preferred_element_type=F32)
             + jnp.dot(zo, ad[...], preferred_element_type=F32)).astype(BF)
    mixed_out[...] = mixed
    moe_out[...] = norm(mixed.astype(F32), gain_moe[...])


def attention(tok, adapt, place, gain, gain_moe, cosine, sine, wq, wk, wv, wo):
    count, width = tok[0].shape
    vm = pl.BlockSpec(memory_space=pltpu.VMEM)
    anywhere = pl.BlockSpec(memory_space=pl.ANY)
    rows = jax.ShapeDtypeStruct((count, width), BF)
    return pl.pallas_call(
        attention_kernel,
        out_shape=(rows, rows),
        in_specs=[vm] * 13 + [pl.BlockSpec(memory_space=pltpu.SMEM)] + [vm] * 4
        + [anywhere] * 4,
        out_specs=(vm, vm),
        scratch_shapes=[
            pltpu.VMEM(wq.shape, BF), pltpu.VMEM(wk.shape, BF), pltpu.VMEM(wv.shape, BF),
            pltpu.VMEM(wo.shape, BF), pltpu.VMEM((5 * count, width), BF),
            pltpu.VMEM((384, width), BF), pltpu.VMEM((4, 6 * count, 128), BF),
            pltpu.VMEM((5 * count, 512), BF), pltpu.VMEM((5 * count, 512), BF),
            pltpu.VMEM((count, width), BF), pltpu.VMEM((6 * count, 5 * count), F32),
            pltpu.VMEM((6 * count, 5 * count), BF), pltpu.SemaphoreType.DMA((4,)),
        ],
        compiler_params=pltpu.CompilerParams(vmem_limit_bytes=ATTENTION_VMEM),
        cost_estimate=pl.CostEstimate(flops=8 << 30, transcendentals=0,
                                      bytes_accessed=20 << 20),
        name="attention_block",
    )(*tok, *adapt, place, gain, gain_moe, cosine, sine, wq, wk, wv, wo)


def expert_kernel(p0, p1, first, table, gate, up, down, out0, out1, xe, ho, scale):
    odd, part = first[0], first[1]
    row = lax.broadcasted_iota(jnp.int32, (256, 256), 0)
    col = lax.broadcasted_iota(jnp.int32, (256, 256), 1)
    before = ((row < col) & ((row < 128) == (col < 128))).astype(BF)
    slot = lax.broadcasted_iota(jnp.int32, (2 * CAP, 256), 0).astype(F32)
    base = jnp.where(lax.broadcasted_iota(jnp.int32, (8, 256), 1) < 128, 0.0, float(CAP))

    def places(i):
        named = table[part, i] > 0.0
        rank = jnp.dot(named.astype(F32).astype(BF), before, preferred_element_type=F32) + base
        rank = jnp.where(named, rank, -1.0)
        return [slot == rank[e:e + 1, :] for e in range(3)]

    hots = []
    for i, piece in enumerate((p0, p1)):
        spots = places(i)
        hot = jnp.concatenate([jnp.where(p, 1.0, 0.0) for p in spots]).astype(BF)
        hots.append(hot)
        rows = jnp.dot(hot, piece[...], preferred_element_type=F32).astype(BF)
        given = table[part, i]
        for e in range(3):
            at = slice(i * 2 * CAP, (i + 1) * 2 * CAP)
            xe[e, at, :] = rows[e * 2 * CAP:(e + 1) * 2 * CAP]
            scale[e, at, :] = jnp.sum(jnp.where(spots[e], given[e:e + 1, :], 0.0), axis=1,
                                      keepdims=True)

    def ffn(e, half, count):
        rows = xe[e]
        hidden = []
        for h in range(count):
            g = jnp.dot(rows, gate[half + h], preferred_element_type=F32)
            u = jnp.dot(rows, up[half + h], preferred_element_type=F32)
            hidden.append((g / (1.0 + jnp.exp(-g)) * u).astype(BF))
        hidden = jnp.concatenate(hidden, axis=1)
        maps = down[pl.ds(pl.multiple_of(256 * half, 256), 256 * count), :]
        out = jnp.dot(hidden, maps, preferred_element_type=F32)
        ho[e] = (out * scale[e]).astype(BF)

    def whole(e, carry):
        ffn(e, odd + 2 * e, 2)
        return carry

    lax.fori_loop(0, 2, whole, 0)
    ffn(2, 4 - 4 * odd, 1)
    for i, out in enumerate((out0, out1)):
        rows = jnp.concatenate([ho[e, i * 2 * CAP:(i + 1) * 2 * CAP, :] for e in range(3)])
        out[...] = lax.dot_general(hots[i], rows, (((0,), (0,)), ((), ())),
                                   preferred_element_type=F32).astype(BF)


def experts(pieces, first, table, gate, up, down):
    width = gate.shape[1]
    shape = pieces[0].shape
    vm = pl.BlockSpec(memory_space=pltpu.VMEM)
    piece = jax.ShapeDtypeStruct((256, width), BF)
    outs = pl.pallas_call(
        expert_kernel,
        out_shape=(piece, piece),
        in_specs=[vm, vm, pl.BlockSpec(memory_space=pltpu.SMEM), vm, vm, vm, vm],
        out_specs=(vm, vm),
        scratch_shapes=[
            pltpu.VMEM((3, 4 * CAP, width), BF), pltpu.VMEM((3, 4 * CAP, width), BF),
            pltpu.VMEM((3, 4 * CAP, 1), F32),
        ],
        compiler_params=pltpu.CompilerParams(vmem_limit_bytes=24 << 20),
        cost_estimate=pl.CostEstimate(flops=7 << 30, transcendentals=0,
                                      bytes_accessed=12 << 20),
        name="expert_block",
    )(*[rows.reshape(256, width) for rows in pieces], first, table, gate, up,
      down.reshape(5 * 256, width))
    return [rows.reshape(shape) for rows in outs]


def rms_scaled(features, scales):
    features = features.astype(F32)
    inverse = lax.rsqrt(jnp.mean(features * features, axis=-1, keepdims=True) + EPSILON)
    return (features * inverse * scales).astype(BF)


def body(tokens, lengths, prompt_adapter, routes, routing_weight, attention_gain, query_weight,
         key_weight, value_weight, output_weight, adapter_down_maps, adapter_up_query_output,
         adapter_up_key_value, expert_gain, gate_weight, up_weight, down_weight, closing_gain,
         vocab_projection):
    own = tokens[0]
    count, width = own.shape
    me, grp = lax.axis_index("seq"), lax.axis_index("grp")

    listing = np.concatenate([np.array([0, 1, 2] if g % 2 == 0 else [1, 2, 0]) + 5 * g // 2
                              for g in range(16)]).astype(np.int32)
    ids, given = routes[0], routing_weight[0]
    table = jnp.sum(jnp.where(ids.T[None] == jnp.asarray(listing)[:, None, None],
                              given.T[None], 0.0), axis=1).reshape(16, 3 * count)
    high = lax.reduce_precision(table, 8, 7)
    low = table - high
    route_rows = jnp.concatenate(
        [high, low, jnp.zeros((16, width - 6 * count), F32)], axis=1).astype(BF)

    ranks = (jnp.arange(16, dtype=jnp.int32)[:, None]
             == 2 * me + jnp.arange(2, dtype=jnp.int32)[None, :]).astype(BF)
    downs = jnp.einsum("rk,pdr->pkd", ranks, adapter_down_maps[:, 0],
                       preferred_element_type=F32).astype(BF).reshape(8, width)
    ups = lax.dynamic_slice_in_dim(adapter_up_query_output[:, 0], 2 * me, 2, 1).reshape(4, width)
    thin = lax.dynamic_slice_in_dim(adapter_up_key_value[:, 0], 2 * me, 2, 1)
    thin = jnp.concatenate([thin[0], thin[1], jnp.zeros((2, width - 1024), BF)], axis=1)
    maps = jnp.concatenate([downs, ups, thin], axis=0)
    payload = jnp.concatenate(
        [jnp.broadcast_to(maps[None], (16, 14, width)), route_rows[:, None, :],
         jnp.zeros((16, 1, width), BF)], axis=1)
    payload, own = lax.optimization_barrier((payload, own))
    held = lax.all_to_all(payload, "grp", 0, 0, tiled=True)
    back1 = lax.ppermute(own, "seq", [(s, s + 2) for s in range(6)])
    back2 = lax.ppermute(own, "seq", [(s, s + 4) for s in range(4)])
    odd_core = me % 2 == 1
    tok = [own, back1, back2, partner(jnp.where(odd_core, back1, own)),
           partner(jnp.where(odd_core, back2, back1))]

    lens = lengths[0]
    ends = jnp.cumsum(lens)
    starts = ends - lens
    blocks = me - jnp.array([0, 2, 4, 1, 3], jnp.int32)
    row = jnp.arange(count, dtype=jnp.int32)
    index = (blocks[:, None] * count + row[None, :]).reshape(-1)
    document = jnp.sum((index[:, None] >= ends[None, :]).astype(jnp.int32), axis=1)
    half = HEAD // 2
    frequency = ROPE_BASE ** (-(jnp.arange(128, dtype=jnp.int32) % half).astype(F32) / half)
    sign = jnp.where(jnp.arange(128) % HEAD < half, -1.0, 1.0).astype(F32)
    near = row.astype(F32)[:, None] * frequency[None, :]
    far = (blocks[:, None] * count - starts[None, :]).astype(F32)[:, :, None] * frequency
    near_cos, near_sin = jnp.cos(near)[None], jnp.sin(near)[None]
    far_cos, far_sin = jnp.cos(far), jnp.sin(far)

    def by_document(values):
        docs = document.reshape(5, count, 1)
        return jnp.where(docs == 0, values[:, None, 0], jnp.where(
            docs == 1, values[:, None, 1], values[:, None, 2]))

    far_cos, far_sin = by_document(far_cos), by_document(far_sin)
    cosine = (far_cos * near_cos - far_sin * near_sin).reshape(5 * count, 128)
    sine = ((far_sin * near_cos + far_cos * near_sin) * sign).reshape(5 * count, 128)
    row_index = index[:count]
    place = jnp.concatenate([ends, me[None]]).astype(jnp.int32)
    gain, gain_moe = attention_gain[None], expert_gain[None]
    held, cosine, sine, place, gain, gain_moe = lax.optimization_barrier(
        (held, cosine, sine, place, gain, gain_moe))
    picked = jnp.stack([lax.dynamic_index_in_dim(held, prompt_adapter[0, p], 0, False)
                        for p in range(3)]).reshape(48, width)
    turn = [picked] + [lax.ppermute(picked, "seq", [(s, (s + d) % 8) for s in range(8)])
                       for d in (2, 6, 4)]
    rel = jnp.array([0, 3, 1, 2], jnp.int32)
    first, second = jnp.where(me % 2 == 0, grp % 4, grp // 4), jnp.where(
        me % 2 == 0, grp // 4, grp % 4)
    first, second = (first + rel[None, :]) % 4, (second + rel[:, None]) % 4
    source = jnp.where(me % 2 == 0, second * 4 + first, first * 4 + second).reshape(8, 2)
    source = jnp.concatenate([source[:3], source[5:6], source[3:5], source[6:]]).reshape(16)
    order = (source[:, None] == jnp.arange(16, dtype=jnp.int32)[None, :]).astype(F32)
    route_in = jnp.dot(order, held[:, 14, :].astype(F32), precision=lax.Precision.HIGHEST)
    route_in = (route_in[:, :3 * count] + route_in[:, 3 * count:6 * count]).reshape(8, 2, 3, count)
    route_in = jnp.concatenate([route_in, jnp.zeros((8, 2, 5, count), F32)], axis=2)
    route_in = route_in.transpose(0, 2, 1, 3).reshape(4, 2, 8, 2 * count)
    odd = (grp % 2).astype(jnp.int32)
    weights = (gate_weight, up_weight, down_weight)

    turn, route_in = lax.optimization_barrier((turn, route_in))
    adapt = turn + [partner(piece) for piece in turn]
    mixed, moe_in = attention(tok, adapt, place, gain, gain_moe, cosine, sine, query_weight,
                              key_weight, value_weight, output_weight)

    def share(pieces, which):
        return experts(pieces, jnp.stack([odd, jnp.int32(which)]), route_in, *weights)

    line = lax.optimization_barrier(
        [shift(moe_in, 0, 1), shift(moe_in, 0, -1), shift(moe_in, 0, 2)])
    own_lo, own_hi = jnp.stack([moe_in, line[0]]), jnp.stack([line[1], line[2]])
    minus_lo, plus_hi = shift(own_lo, 1, 1), shift(own_hi, 1, -1)
    minus_hi, plus_lo = shift(own_hi, 1, 1), shift(own_lo, 1, -1)
    own_lo, own_hi = share([own_lo, own_hi], 0)
    minus_lo, plus_hi, own_lo, own_hi = lax.optimization_barrier(
        (minus_lo, plus_hi, own_lo, own_hi))
    first_lo, first_hi = share([minus_lo, plus_hi], 1)
    minus_lo, plus_hi, minus_hi, plus_lo, first_lo, first_hi = lax.optimization_barrier(
        (minus_lo, plus_hi, minus_hi, plus_lo, first_lo, first_hi))
    far_lo, far_hi = shift(minus_lo, 1, 1), shift(plus_hi, 1, -1)
    minus_hi, plus_lo = share([minus_hi, plus_lo], 2)
    minus_lo, plus_hi, minus_hi, plus_lo, far_lo, far_hi = lax.optimization_barrier(
        (first_lo, first_hi, minus_hi, plus_lo, far_lo, far_hi))

    minus_lo, plus_hi = shift(minus_lo, 1, -1), shift(plus_hi, 1, 1)
    far_lo, far_hi = share([far_lo, far_hi], 3)
    far_lo, far_hi = lax.optimization_barrier((shift(far_lo, 1, 1), shift(far_hi, 1, -1)))
    plus_lo = shift((wide(plus_lo) + wide(far_lo)).astype(BF), 1, 1)
    minus_hi = shift((wide(minus_hi) + wide(far_hi)).astype(BF), 1, -1)
    minus_lo, plus_hi, minus_hi, plus_lo = lax.optimization_barrier(
        (minus_lo, plus_hi, minus_hi, plus_lo))
    own_lo = wide(own_lo) + wide(plus_lo) + wide(minus_lo)
    own_hi = wide(own_hi) + wide(plus_hi) + wide(minus_hi)
    line = lax.optimization_barrier(
        [shift(own_hi[0].astype(BF), 0, 1), shift(own_lo[1].astype(BF), 0, -1),
         shift(own_hi[1].astype(BF), 0, 2)])
    combined = own_lo[0] + wide(line[0]) + wide(line[1]) + wide(line[2])
    hidden_out = (mixed.astype(F32) + combined).astype(BF)

    selector = (ends[:, None] - 1 == row_index[None, :]).astype(BF)
    last = jnp.dot(selector, hidden_out, preferred_element_type=F32)
    last = rms_scaled(last, closing_gain)
    part = width // 8
    split = last.reshape(3, 8, part).transpose(1, 0, 2)
    mine = lax.all_to_all(split, "seq", 0, 0, tiled=True)
    mine = jnp.sum(mine.astype(F32), axis=0).astype(BF)
    everyone = lax.all_to_all(jnp.broadcast_to(mine[None], (128, 3, part)), WHOLE, 0, 0,
                              tiled=True)
    final_rows = everyone.reshape(8, 48, part).transpose(1, 0, 2).reshape(48, width)
    logits = jnp.dot(final_rows, vocab_projection, preferred_element_type=F32)
    top = jnp.max(logits, axis=1)
    mass = jnp.sum(jnp.exp(logits - top[:, None]), axis=1)
    stats = jnp.concatenate([top, mass, jnp.zeros((32,), F32)])
    stats = lax.all_to_all(jnp.broadcast_to(stats[None], (128, 128)), WHOLE, 0, 0, tiled=True)
    tops = stats[:, :48]
    peak = jnp.max(tops, axis=0)
    total = jnp.sum(stats[:, 48:96] * jnp.exp(tops - peak[None]), axis=0)
    log_probs = logits - (peak + jnp.log(total))[:, None]
    return hidden_out[None], log_probs


def solution(mesh):
    placed = (
        P("grp", "seq", None), P("grp", None), P("grp", None), P("grp", "seq", None),
        P("grp", "seq", None), P(), P(), P(), P(), P(), P(None, "grp", None, None),
        P(None, "grp", None, None), P(None, "grp", None, None), P(), P("grp", None, None),
        P("grp", None, None), P("grp", None, None), P(), P(None, WHOLE),
    )
    return jax.shard_map(
        body,
        mesh=mesh,
        in_specs=placed,
        out_specs=(P("grp", "seq", None), P(None, WHOLE)),
        check_vma=False,
    )
```

```python
import jax
import jax.numpy as jnp
import numpy as np
from jax import lax
from jax.experimental import pallas as pl
from jax.experimental.pallas import tpu as pltpu
from jax.sharding import PartitionSpec as P

HEADS = 24
KV_HEADS = 8
HEAD = 64
EXPERTS = 40
TOP = 8
CAP = 40
ATTENTION_VMEM = 63 << 20
EPSILON = 1e-05
ROPE_BASE = 10000.0
MASKED = -1e30
SIDE = 4
BF = jnp.bfloat16
F32 = jnp.float32
WHOLE = ("seq", "grp")


def shift(rows, phase, step):
    pairs = []
    for s in range(8):
        for i in range(16):
            if s % 2 == phase:
                to = i // SIDE * SIDE + (i % SIDE + step) % SIDE
            else:
                to = (i // SIDE + step) % SIDE * SIDE + i % SIDE
            pairs.append((s * 16 + i, s * 16 + to))
    return lax.ppermute(rows, WHOLE, pairs)


def partner(rows):
    return lax.ppermute(rows, "seq", [(s, s ^ 1) for s in range(8)])


def wide(v):
    return v.astype(F32)


def dot_t(lhs, rhs):
    return lax.dot_general(lhs, rhs, (((1,), (1,)), ((), ())), preferred_element_type=F32)


def norm(rows, scale):
    inverse = lax.rsqrt(jnp.mean(rows * rows, axis=-1, keepdims=True) + EPSILON)
    return (rows * inverse * scale).astype(BF)


def attention_kernel(*refs):
    tok = refs[0:5]
    adapt = refs[5:13]
    (place, gain, gain_moe, cosine, sine, wq_hbm, wk_hbm, wv_hbm, wo_hbm, mixed_out, moe_out,
     wq, wk, wv, wo, xn, ad, qbuf, kbuf, vbuf, att, score, prob, sems) = refs[13:]
    loads = [pltpu.make_async_copy(src, dst, sems.at[i]) for i, (src, dst) in enumerate(
        [(wk_hbm, wk), (wv_hbm, wv), (wq_hbm, wq), (wo_hbm, wo)])]
    for load in loads:
        load.start()
    count = tok[0].shape[0]
    ends = [place[0], place[1], place[2]]
    me = place[3]

    def document(index):
        return sum((index >= end).astype(jnp.int32) for end in ends)

    def block_start(b):
        return (me - jnp.where(b < 3, 2 * b, 2 * b - 5)) * count

    for j in range(8):
        ad[48 * j:48 * j + 48, :] = adapt[j][...]
    for b in range(5):
        xn[b * count:(b + 1) * count, :] = norm(tok[b][...].astype(F32), gain[...])
    column = lax.broadcasted_iota(jnp.int32, (1, 384), 1)
    col_row = column & 15
    col_prompt = column >> 4
    col_prompt = col_prompt - 3 * ((col_prompt * 171) >> 9)

    def low(z, roll, first, docs):
        moved = pltpu.roll(z, roll, 1)
        keep = (docs == col_prompt) & (col_row >= first) & (col_row < first + 2)
        return jnp.where(keep, moved, 0.0).astype(BF)

    lane = lax.broadcasted_iota(jnp.int32, (count, 128), 1)
    down_rows = lax.broadcasted_iota(jnp.int32, (count, 1), 0)

    def rope(u, cos_t, sin_t):
        lower = (lax.broadcasted_iota(jnp.int32, u.shape, 1) & 63) < 32
        turned = jnp.where(lower, pltpu.roll(u, 96, 1), pltpu.roll(u, 32, 1))
        return u * cos_t + turned * sin_t

    loads[0].wait()
    loads[1].wait()

    def key_block(b, carry):
        size = 5 * count // 2
        at = pl.ds(pl.multiple_of(b * size, 16), size)
        row = b * size + lax.broadcasted_iota(jnp.int32, (size, 1), 0)
        docs = document(block_start(row >> 7) + (row & 127))
        rows = xn[at, :]
        z = dot_t(rows, ad[...])
        keys = jnp.dot(rows, wk[...], preferred_element_type=F32) + jnp.dot(
            low(z, 10, 12, docs), ad[:, :512], preferred_element_type=F32)
        values = jnp.dot(rows, wv[...], preferred_element_type=F32) + jnp.dot(
            low(z, 8, 12, docs), ad[:, 512:1024], preferred_element_type=F32)
        vbuf[at, :] = values.astype(BF)
        cos_t = cosine[at, :]
        sin_t = sine[at, :]
        for c in range(4):
            kbuf[at, 128 * c:128 * c + 128] = rope(
                keys[:, 128 * c:128 * c + 128], cos_t, sin_t).astype(BF)
        return carry

    lax.fori_loop(0, 2, key_block, 0)
    own_index = me * count + down_rows
    docs = document(own_index)
    own = xn[0:count, :]
    zq = low(dot_t(own, ad[...]), 8, 8, docs)
    cos_t = cosine[0:count, :]
    sin_t = sine[0:count, :]
    low_half = lane < 64
    along = lax.broadcasted_iota(jnp.int32, (1, count), 1)
    key_index = jnp.concatenate([block_start(b) + along for b in range(5)], axis=1)
    allowed = ((docs == document(key_index)) & (key_index <= own_index) & (key_index >= 0))
    bias = jnp.where(allowed, 0.0, MASKED)
    loads[2].wait()

    def query_block(c, carry):
        at = pl.multiple_of(c * 384, 128)
        u = jnp.dot(own, wq[:, pl.ds(at, 384)], preferred_element_type=F32) + jnp.dot(
            zq, ad[:, pl.ds(at, 384)], preferred_element_type=F32)
        for t in range(3):
            q = rope(u[:, 128 * t:128 * t + 128], cos_t, sin_t).astype(BF).astype(F32)
            q = q * (HEAD ** -0.5)
            turned = pltpu.roll(q, 64, 1)
            for own_low in (True, False):
                h = 2 * t + (0 if own_low else 1)
                kv_low = h < 3
                rows = q if own_low == kv_low else turned
                keep = low_half if kv_low else ~low_half
                qbuf[c, count * h:count * h + count, :] = jnp.where(keep, rows, 0.0).astype(BF)
        return carry

    lax.fori_loop(0, 4, query_block, 0)

    def pair(j, carry):
        kv = pl.ds(pl.multiple_of(j * 128, 128), 128)
        score[...] = dot_t(qbuf[j], kbuf[:, kv])
        totals = []
        for h in range(6):
            at = slice(count * h, count * h + count)
            s = score[at, :] + bias
            top = jnp.max(s, axis=-1, keepdims=True)
            w = jnp.exp(s - top)
            totals.append(jnp.sum(w, axis=-1, keepdims=True))
            prob[at, :] = w.astype(BF)
        out = jnp.dot(prob[...], vbuf[:, kv], preferred_element_type=F32)
        results = []
        for h in range(6):
            o = out[count * h:count * h + count] / totals[h]
            results.append(pltpu.roll(o, 64, 1) if (h % 2 == 0) != (h < 3) else o)
        for t in range(3):
            att[:, pl.ds(pl.multiple_of(j * 384 + 128 * t, 128), 128)] = jnp.where(
                low_half, results[2 * t], results[2 * t + 1]).astype(BF)
        return carry

    lax.fori_loop(0, 4, pair, 0)
    loads[3].wait()
    attended = att[...]
    zo = low(dot_t(attended, ad[...]), 4, 10, docs)

    def out_block(c, carry):
        at = pl.ds(pl.multiple_of(c * 512, 512), 512)
        mixed_out[:, at] = (
            tok[0][:, at].astype(F32)
            + jnp.dot(attended, wo[:, at], preferred_element_type=F32)
            + jnp.dot(zo, ad[:, at], preferred_element_type=F32)).astype(BF)
        return carry

    lax.fori_loop(0, 3, out_block, 0)
    moe_out[...] = norm(mixed_out[...].astype(F32), gain_moe[...])


def attention(tok, adapt, place, gain, gain_moe, cosine, sine, wq, wk, wv, wo):
    count, width = tok[0].shape
    vm = pl.BlockSpec(memory_space=pltpu.VMEM)
    anywhere = pl.BlockSpec(memory_space=pl.ANY)
    rows = jax.ShapeDtypeStruct((count, width), BF)
    return pl.pallas_call(
        attention_kernel,
        out_shape=(rows, rows),
        in_specs=[vm] * 13 + [pl.BlockSpec(memory_space=pltpu.SMEM)] + [vm] * 4
        + [anywhere] * 4,
        out_specs=(vm, vm),
        scratch_shapes=[
            pltpu.VMEM(wq.shape, BF), pltpu.VMEM(wk.shape, BF), pltpu.VMEM(wv.shape, BF),
            pltpu.VMEM(wo.shape, BF), pltpu.VMEM((5 * count, width), BF),
            pltpu.VMEM((384, width), BF), pltpu.VMEM((4, 6 * count, 128), BF),
            pltpu.VMEM((5 * count, 512), BF), pltpu.VMEM((5 * count, 512), BF),
            pltpu.VMEM((count, width), BF), pltpu.VMEM((6 * count, 5 * count), F32),
            pltpu.VMEM((6 * count, 5 * count), BF), pltpu.SemaphoreType.DMA((4,)),
        ],
        compiler_params=pltpu.CompilerParams(vmem_limit_bytes=ATTENTION_VMEM),
        cost_estimate=pl.CostEstimate(flops=8 << 30, transcendentals=0,
                                      bytes_accessed=20 << 20),
        name="attention_block",
    )(*tok, *adapt, place, gain, gain_moe, cosine, sine, wq, wk, wv, wo)


def expert_kernel(p0, p1, first, table, gate, up, down, out0, out1, last, xe, ho, scale):
    odd, part = first[0], first[1]
    row = lax.broadcasted_iota(jnp.int32, (256, 256), 0)
    col = lax.broadcasted_iota(jnp.int32, (256, 256), 1)
    before = ((row < col) & ((row < 128) == (col < 128))).astype(BF)
    slot = lax.broadcasted_iota(jnp.int32, (2 * CAP, 256), 0).astype(F32)
    base = jnp.where(lax.broadcasted_iota(jnp.int32, (8, 256), 1) < 128, 0.0, float(CAP))

    def places(i):
        named = table[part, i] > 0.0
        rank = jnp.dot(named.astype(F32).astype(BF), before, preferred_element_type=F32) + base
        rank = jnp.where(named, rank, -1.0)
        return [slot == rank[e:e + 1, :] for e in range(3)]

    hots = []
    for i, piece in enumerate((p0, p1)):
        spots = places(i)
        hot = jnp.concatenate([jnp.where(p, 1.0, 0.0) for p in spots]).astype(BF)
        hots.append(hot)
        rows = jnp.dot(hot, piece[...], preferred_element_type=F32).astype(BF)
        given = table[part, i]
        for e in range(3):
            at = slice(i * 2 * CAP, (i + 1) * 2 * CAP)
            xe[e, at, :] = rows[e * 2 * CAP:(e + 1) * 2 * CAP]
            scale[e, at, :] = jnp.sum(jnp.where(spots[e], given[e:e + 1, :], 0.0), axis=1,
                                      keepdims=True)

    def ffn(e, half, count):
        rows = xe[e]
        hidden = []
        for h in range(count):
            g = jnp.dot(rows, gate[half + h], preferred_element_type=F32)
            u = jnp.dot(rows, up[half + h], preferred_element_type=F32)
            hidden.append((g / (1.0 + jnp.exp(-g)) * u).astype(BF))
        hidden = jnp.concatenate(hidden, axis=1)
        maps = down[pl.ds(pl.multiple_of(256 * half, 256), 256 * count), :]
        out = jnp.dot(hidden, maps, preferred_element_type=F32)
        ho[e] = (out * scale[e]).astype(BF)

    def whole(e, carry):
        ffn(e, odd + 2 * e, 2)
        return carry

    lax.fori_loop(0, 2, whole, 0)
    ffn(2, 4 - 4 * odd, 1)
    for i, out in enumerate((out0, out1)):
        rows = jnp.concatenate([ho[e, i * 2 * CAP:(i + 1) * 2 * CAP, :] for e in range(3)])
        total = lax.dot_general(hots[i], rows, (((0,), (0,)), ((), ())),
                                preferred_element_type=F32).astype(BF)
        out[...] = total
        marks = table[part, i][3:6]
        left = lax.broadcasted_iota(jnp.int32, marks.shape, 1) < 128
        marks = jnp.concatenate([jnp.where(left, marks, 0.0), jnp.where(left, 0.0, marks),
                                 jnp.zeros((2, 256), F32)]).astype(BF)
        last[i] = jnp.dot(marks, total, preferred_element_type=F32).astype(BF)


def experts(pieces, first, table, gate, up, down):
    width = gate.shape[1]
    shape = pieces[0].shape
    vm = pl.BlockSpec(memory_space=pltpu.VMEM)
    piece = jax.ShapeDtypeStruct((256, width), BF)
    first_out, second_out, last = pl.pallas_call(
        expert_kernel,
        out_shape=(piece, piece, jax.ShapeDtypeStruct((2, 8, width), BF)),
        in_specs=[vm, vm, pl.BlockSpec(memory_space=pltpu.SMEM), vm, vm, vm, vm],
        out_specs=(vm, vm, vm),
        scratch_shapes=[
            pltpu.VMEM((3, 4 * CAP, width), BF), pltpu.VMEM((3, 4 * CAP, width), BF),
            pltpu.VMEM((3, 4 * CAP, 1), F32),
        ],
        compiler_params=pltpu.CompilerParams(vmem_limit_bytes=24 << 20),
        cost_estimate=pl.CostEstimate(flops=7 << 30, transcendentals=0,
                                      bytes_accessed=12 << 20),
        name="expert_block",
    )(*[rows.reshape(256, width) for rows in pieces], first, table, gate, up,
      down.reshape(5 * 256, width))
    return first_out.reshape(shape), second_out.reshape(shape), last


def rms_scaled(features, scales):
    features = features.astype(F32)
    inverse = lax.rsqrt(jnp.mean(features * features, axis=-1, keepdims=True) + EPSILON)
    return (features * inverse * scales).astype(BF)


def body(tokens, lengths, prompt_adapter, routes, routing_weight, attention_gain, query_weight,
         key_weight, value_weight, output_weight, adapter_down_maps, adapter_up_query_output,
         adapter_up_key_value, expert_gain, gate_weight, up_weight, down_weight, closing_gain,
         vocab_projection):
    own = tokens[0]
    count, width = own.shape
    me, grp = lax.axis_index("seq"), lax.axis_index("grp")

    listing = np.concatenate([np.array([0, 1, 2] if g % 2 == 0 else [1, 2, 0]) + 5 * g // 2
                              for g in range(16)]).astype(np.int32)
    ids, given = routes[0], routing_weight[0]
    table = jnp.sum(jnp.where(ids.T[None] == jnp.asarray(listing)[:, None, None],
                              given.T[None], 0.0), axis=1).reshape(16, 3 * count)
    high = lax.reduce_precision(table, 8, 7)
    low = table - high
    route_rows = jnp.concatenate(
        [high, low, jnp.zeros((16, width - 6 * count), F32)], axis=1).astype(BF)

    ranks = (jnp.arange(16, dtype=jnp.int32)[:, None]
             == 2 * me + jnp.arange(2, dtype=jnp.int32)[None, :]).astype(BF)
    downs = jnp.einsum("rk,pdr->pkd", ranks, adapter_down_maps[:, 0],
                       preferred_element_type=F32).astype(BF).reshape(8, width)
    ups = lax.dynamic_slice_in_dim(adapter_up_query_output[:, 0], 2 * me, 2, 1).reshape(4, width)
    thin = lax.dynamic_slice_in_dim(adapter_up_key_value[:, 0], 2 * me, 2, 1)
    thin = jnp.concatenate([thin[0], thin[1], jnp.zeros((2, width - 1024), BF)], axis=1)
    maps = jnp.concatenate([downs, ups, thin], axis=0)
    ends = jnp.cumsum(lengths[0])
    marks = (ends[:, None] - 1 == me * count + jnp.arange(count, dtype=jnp.int32)[None, :])
    mark_row = jnp.concatenate([marks.reshape(1, 3 * count).astype(BF),
                                jnp.zeros((1, width - 3 * count), BF)], axis=1)
    payload = jnp.concatenate(
        [jnp.broadcast_to(maps[None], (16, 14, width)), route_rows[:, None, :],
         jnp.broadcast_to(mark_row[None], (16, 1, width))], axis=1)
    payload, own = lax.optimization_barrier((payload, own))
    held = lax.all_to_all(payload, "grp", 0, 0, tiled=True)
    back1 = lax.ppermute(own, "seq", [(s, s + 2) for s in range(6)])
    back2 = lax.ppermute(own, "seq", [(s, s + 4) for s in range(4)])
    odd_core = me % 2 == 1
    tok = [own, back1, back2, partner(jnp.where(odd_core, back1, own)),
           partner(jnp.where(odd_core, back2, back1))]

    lens = lengths[0]
    starts = ends - lens
    blocks = me - jnp.array([0, 2, 4, 1, 3], jnp.int32)
    row = jnp.arange(count, dtype=jnp.int32)
    index = (blocks[:, None] * count + row[None, :]).reshape(-1)
    document = jnp.sum((index[:, None] >= ends[None, :]).astype(jnp.int32), axis=1)
    half = HEAD // 2
    frequency = ROPE_BASE ** (-(jnp.arange(128, dtype=jnp.int32) % half).astype(F32) / half)
    sign = jnp.where(jnp.arange(128) % HEAD < half, -1.0, 1.0).astype(F32)
    near = row.astype(F32)[:, None] * frequency[None, :]
    far = (blocks[:, None] * count - starts[None, :]).astype(F32)[:, :, None] * frequency
    near_cos, near_sin = jnp.cos(near)[None], jnp.sin(near)[None]
    far_cos, far_sin = jnp.cos(far), jnp.sin(far)

    def by_document(values):
        docs = document.reshape(5, count, 1)
        return jnp.where(docs == 0, values[:, None, 0], jnp.where(
            docs == 1, values[:, None, 1], values[:, None, 2]))

    far_cos, far_sin = by_document(far_cos), by_document(far_sin)
    cosine = (far_cos * near_cos - far_sin * near_sin).reshape(5 * count, 128)
    sine = ((far_sin * near_cos + far_cos * near_sin) * sign).reshape(5 * count, 128)
    row_index = index[:count]
    place = jnp.concatenate([ends, me[None]]).astype(jnp.int32)
    gain, gain_moe = attention_gain[None], expert_gain[None]
    held, cosine, sine, place, gain, gain_moe = lax.optimization_barrier(
        (held, cosine, sine, place, gain, gain_moe))
    picked = jnp.stack([lax.dynamic_index_in_dim(held, prompt_adapter[0, p], 0, False)
                        for p in range(3)]).reshape(48, width)
    turn = [picked] + [lax.ppermute(picked, "seq", [(s, (s + d) % 8) for s in range(8)])
                       for d in (2, 6, 4)]
    rel = jnp.array([0, 3, 1, 2], jnp.int32)
    first, second = jnp.where(me % 2 == 0, grp % 4, grp // 4), jnp.where(
        me % 2 == 0, grp // 4, grp % 4)
    first, second = (first + rel[None, :]) % 4, (second + rel[:, None]) % 4
    source = jnp.where(me % 2 == 0, second * 4 + first, first * 4 + second).reshape(8, 2)
    source = jnp.concatenate([source[:3], source[5:6], source[3:5], source[6:]]).reshape(16)
    order = (source[:, None] == jnp.arange(16, dtype=jnp.int32)[None, :]).astype(F32)
    route_in = jnp.concatenate(
        [held[:, 14, :3 * count].astype(F32) + held[:, 14, 3 * count:6 * count].astype(F32),
         held[:, 15, :3 * count].astype(F32)], axis=1)
    route_in = jnp.dot(order, route_in, precision=lax.Precision.HIGHEST)
    route_in = route_in.reshape(8, 2, 6, count)
    route_in = jnp.concatenate([route_in, jnp.zeros((8, 2, 2, count), F32)], axis=2)
    route_in = route_in.transpose(0, 2, 1, 3).reshape(4, 2, 8, 2 * count)
    odd = (grp % 2).astype(jnp.int32)
    weights = (gate_weight, up_weight, down_weight)

    turn, route_in = lax.optimization_barrier((turn, route_in))
    adapt = turn + [partner(piece) for piece in turn]
    mixed, moe_in = attention(tok, adapt, place, gain, gain_moe, cosine, sine, query_weight,
                              key_weight, value_weight, output_weight)

    def share(pieces, which):
        return experts(pieces, jnp.stack([odd, jnp.int32(which)]), route_in, *weights)

    line = lax.optimization_barrier(
        [shift(moe_in, 0, 1), shift(moe_in, 0, -1), shift(moe_in, 0, 2)])
    own_lo, own_hi = jnp.stack([moe_in, line[0]]), jnp.stack([line[1], line[2]])
    minus_lo, plus_hi = shift(own_lo, 1, 1), shift(own_hi, 1, -1)
    minus_hi, plus_lo = shift(own_hi, 1, 1), shift(own_lo, 1, -1)
    own_lo, own_hi, last_own = share([own_lo, own_hi], 0)
    minus_lo, plus_hi, own_lo, own_hi = lax.optimization_barrier(
        (minus_lo, plus_hi, own_lo, own_hi))
    far_lo, far_hi = shift(minus_lo, 1, 1), shift(plus_hi, 1, -1)
    first_lo, first_hi, last_first = share([minus_lo, plus_hi], 1)
    minus_hi, plus_lo, first_lo, first_hi = lax.optimization_barrier(
        (minus_hi, plus_lo, first_lo, first_hi))
    minus_hi, plus_lo, last_second = share([minus_hi, plus_lo], 2)
    minus_lo, plus_hi, minus_hi, plus_lo, far_lo, far_hi = lax.optimization_barrier(
        (first_lo, first_hi, minus_hi, plus_lo, far_lo, far_hi))

    minus_lo, plus_hi = shift(minus_lo, 1, -1), shift(plus_hi, 1, 1)
    far_lo, far_hi, last_far = share([far_lo, far_hi], 3)
    far_lo, far_hi = lax.optimization_barrier((shift(far_lo, 1, 1), shift(far_hi, 1, -1)))
    plus_lo = shift((wide(plus_lo) + wide(far_lo)).astype(BF), 1, 1)
    minus_hi = shift((wide(minus_hi) + wide(far_hi)).astype(BF), 1, -1)
    minus_lo, plus_hi, minus_hi, plus_lo = lax.optimization_barrier(
        (minus_lo, plus_hi, minus_hi, plus_lo))
    own_lo = wide(own_lo) + wide(plus_lo) + wide(minus_lo)
    own_hi = wide(own_hi) + wide(plus_hi) + wide(minus_hi)
    line = lax.optimization_barrier(
        [shift(own_hi[0].astype(BF), 0, 1), shift(own_lo[1].astype(BF), 0, -1),
         shift(own_hi[1].astype(BF), 0, 2)])
    combined = own_lo[0] + wide(line[0]) + wide(line[1]) + wide(line[2])
    hidden_out = (mixed.astype(F32) + combined).astype(BF)

    last = jnp.stack([last_own, last_first, last_second, last_far])[:, :, :6]
    last = jnp.einsum("jg,jr->gr", order.astype(BF), last.reshape(16, 3 * width),
                      preferred_element_type=F32).astype(BF)
    last = lax.all_to_all(last.reshape(16, 3, width), "grp", 0, 0, tiled=True)
    last = jnp.sum(last.astype(F32), axis=0) + jnp.dot(
        marks.astype(BF), mixed, preferred_element_type=F32)
    last = rms_scaled(last.astype(BF), closing_gain)
    part = width // 8
    split = last.reshape(3, 8, part).transpose(1, 0, 2)
    mine = lax.all_to_all(split, "seq", 0, 0, tiled=True)
    mine = jnp.sum(mine.astype(F32), axis=0).astype(BF)
    everyone = lax.all_to_all(jnp.broadcast_to(mine[None], (128, 3, part)), WHOLE, 0, 0,
                              tiled=True)
    final_rows = everyone.reshape(8, 48, part).transpose(1, 0, 2).reshape(48, width)
    logits = jnp.dot(final_rows, vocab_projection, preferred_element_type=F32)
    top = jnp.max(logits, axis=1)
    mass = jnp.sum(jnp.exp(logits - top[:, None]), axis=1)
    stats = jnp.concatenate([top, mass, jnp.zeros((32,), F32)])
    stats = lax.all_to_all(jnp.broadcast_to(stats[None], (128, 128)), WHOLE, 0, 0, tiled=True)
    tops = stats[:, :48]
    peak = jnp.max(tops, axis=0)
    total = jnp.sum(stats[:, 48:96] * jnp.exp(tops - peak[None]), axis=0)
    log_probs = logits - (peak + jnp.log(total))[:, None]
    return hidden_out[None], log_probs


def solution(mesh):
    placed = (
        P("grp", "seq", None), P("grp", None), P("grp", None), P("grp", "seq", None),
        P("grp", "seq", None), P(), P(), P(), P(), P(), P(None, "grp", None, None),
        P(None, "grp", None, None), P(None, "grp", None, None), P(), P("grp", None, None),
        P("grp", None, None), P("grp", None, None), P(), P(None, WHOLE),
    )
    return jax.shard_map(
        body,
        mesh=mesh,
        in_specs=placed,
        out_specs=(P("grp", "seq", None), P(None, WHOLE)),
        check_vma=False,
    )
```

```python
import jax
import jax.numpy as jnp
import numpy as np
from jax import lax
from jax.experimental import pallas as pl
from jax.experimental.pallas import tpu as pltpu
from jax.sharding import PartitionSpec as P

HEADS = 24
KV_HEADS = 8
HEAD = 64
EXPERTS = 40
TOP = 8
CAP = 40
ATTENTION_VMEM = 63 << 20
EPSILON = 1e-05
ROPE_BASE = 10000.0
MASKED = -1e30
SIDE = 4
BF = jnp.bfloat16
F32 = jnp.float32
WHOLE = ("seq", "grp")


def shift(rows, phase, step):
    pairs = []
    for s in range(8):
        for i in range(16):
            if s % 2 == phase:
                to = i // SIDE * SIDE + (i % SIDE + step) % SIDE
            else:
                to = (i // SIDE + step) % SIDE * SIDE + i % SIDE
            pairs.append((s * 16 + i, s * 16 + to))
    return lax.ppermute(rows, WHOLE, pairs)


def partner(rows):
    return lax.ppermute(rows, "seq", [(s, s ^ 1) for s in range(8)])


def wide(v):
    return v.astype(F32)


def dot_t(lhs, rhs):
    return lax.dot_general(lhs, rhs, (((1,), (1,)), ((), ())), preferred_element_type=F32)


def norm(rows, scale):
    inverse = lax.rsqrt(jnp.mean(rows * rows, axis=-1, keepdims=True) + EPSILON)
    return (rows * inverse * scale).astype(BF)


def attention_kernel(*refs):
    tok = refs[0:5]
    adapt = refs[5:13]
    (place, gain, gain_moe, cosine, sine, wq_hbm, wk_hbm, wv_hbm, wo_hbm, mixed_out, moe_out,
     wq, wk, wv, wo, xn, ad, qbuf, kbuf, vbuf, att, score, prob, total, sems) = refs[13:]
    loads = [pltpu.make_async_copy(src, dst, sems.at[i]) for i, (src, dst) in enumerate(
        [(wk_hbm, wk), (wv_hbm, wv), (wq_hbm, wq), (wo_hbm, wo)])]
    for load in loads:
        load.start()
    count = tok[0].shape[0]
    ends = [place[0], place[1], place[2]]
    me = place[3]

    def document(index):
        return sum((index >= end).astype(jnp.int32) for end in ends)

    def block_start(b):
        return (me - jnp.where(b < 3, 2 * b, 2 * b - 5)) * count

    for j in range(8):
        ad[48 * j:48 * j + 48, :] = adapt[j][...]
    for b in range(5):
        xn[b * count:(b + 1) * count, :] = norm(tok[b][...].astype(F32), gain[...])
    column = lax.broadcasted_iota(jnp.int32, (1, 384), 1)
    col_row = column & 15
    col_prompt = column >> 4
    col_prompt = col_prompt - 3 * ((col_prompt * 171) >> 9)

    def low(z, roll, first, docs):
        moved = pltpu.roll(z, roll, 1)
        keep = (docs == col_prompt) & (col_row >= first) & (col_row < first + 2)
        return jnp.where(keep, moved, 0.0).astype(BF)

    lane = lax.broadcasted_iota(jnp.int32, (count, 128), 1)
    down_rows = lax.broadcasted_iota(jnp.int32, (count, 1), 0)

    def rope(u, cos_t, sin_t):
        lower = (lax.broadcasted_iota(jnp.int32, u.shape, 1) & 63) < 32
        turned = jnp.where(lower, pltpu.roll(u, 96, 1), pltpu.roll(u, 32, 1))
        return u * cos_t + turned * sin_t

    loads[0].wait()
    loads[1].wait()

    def key_block(b, carry):
        size = 5 * count // 2
        at = pl.ds(pl.multiple_of(b * size, 16), size)
        row = b * size + lax.broadcasted_iota(jnp.int32, (size, 1), 0)
        docs = document(block_start(row >> 7) + (row & 127))
        rows = xn[at, :]
        z = dot_t(rows, ad[...])
        keys = jnp.dot(rows, wk[...], preferred_element_type=F32) + jnp.dot(
            low(z, 10, 12, docs), ad[:, :512], preferred_element_type=F32)
        values = jnp.dot(rows, wv[...], preferred_element_type=F32) + jnp.dot(
            low(z, 8, 12, docs), ad[:, 512:1024], preferred_element_type=F32)
        vbuf[at, :] = values.astype(BF)
        cos_t = cosine[at, :]
        sin_t = sine[at, :]
        for c in range(4):
            kbuf[at, 128 * c:128 * c + 128] = rope(
                keys[:, 128 * c:128 * c + 128], cos_t, sin_t).astype(BF)
        return carry

    lax.fori_loop(0, 2, key_block, 0)
    own_index = me * count + down_rows
    docs = document(own_index)
    own = xn[0:count, :]
    zq = low(dot_t(own, ad[...]), 8, 8, docs)
    cos_t = cosine[0:count, :]
    sin_t = sine[0:count, :]
    low_half = lane < 64
    along = lax.broadcasted_iota(jnp.int32, (1, count), 1)
    key_index = jnp.concatenate([block_start(b) + along for b in range(5)], axis=1)
    allowed = ((docs == document(key_index)) & (key_index <= own_index) & (key_index >= 0))
    bias = jnp.where(allowed, 0.0, MASKED)
    loads[2].wait()

    def query_block(c, carry):
        at = pl.multiple_of(c * 384, 128)
        u = jnp.dot(own, wq[:, pl.ds(at, 384)], preferred_element_type=F32) + jnp.dot(
            zq, ad[:, pl.ds(at, 384)], preferred_element_type=F32)
        for t in range(3):
            q = rope(u[:, 128 * t:128 * t + 128], cos_t, sin_t).astype(BF).astype(F32)
            q = q * (HEAD ** -0.5)
            turned = pltpu.roll(q, 64, 1)
            for own_low in (True, False):
                h = 2 * t + (0 if own_low else 1)
                kv_low = h < 3
                rows = q if own_low == kv_low else turned
                keep = low_half if kv_low else ~low_half
                qbuf[c, count * h:count * h + count, :] = jnp.where(keep, rows, 0.0).astype(BF)
        return carry

    lax.fori_loop(0, 4, query_block, 0)

    def pair(j, carry):
        kv = pl.ds(pl.multiple_of(j * 128, 128), 128)
        score[...] = dot_t(qbuf[j], kbuf[:, kv])

        def soften(h, carry):
            at = pl.ds(pl.multiple_of(h * count, count), count)
            s = score[at, :] + bias
            top = jnp.max(s, axis=-1, keepdims=True)
            w = jnp.exp(s - top)
            total[at, :] = jnp.sum(w, axis=-1, keepdims=True)
            prob[at, :] = w.astype(BF)
            return carry

        lax.fori_loop(0, 6, soften, 0)
        out = jnp.dot(prob[...], vbuf[:, kv], preferred_element_type=F32) / total[...]
        results = []
        for h in range(6):
            o = out[count * h:count * h + count]
            results.append(pltpu.roll(o, 64, 1) if (h % 2 == 0) != (h < 3) else o)
        for t in range(3):
            att[:, pl.ds(pl.multiple_of(j * 384 + 128 * t, 128), 128)] = jnp.where(
                low_half, results[2 * t], results[2 * t + 1]).astype(BF)
        return carry

    lax.fori_loop(0, 4, pair, 0)
    loads[3].wait()
    attended = att[...]
    zo = low(dot_t(attended, ad[...]), 4, 10, docs)

    def out_block(c, carry):
        at = pl.ds(pl.multiple_of(c * 512, 512), 512)
        mixed_out[:, at] = (
            tok[0][:, at].astype(F32)
            + jnp.dot(attended, wo[:, at], preferred_element_type=F32)
            + jnp.dot(zo, ad[:, at], preferred_element_type=F32)).astype(BF)
        return carry

    lax.fori_loop(0, 3, out_block, 0)
    moe_out[...] = norm(mixed_out[...].astype(F32), gain_moe[...])


def attention(tok, adapt, place, gain, gain_moe, cosine, sine, wq, wk, wv, wo):
    count, width = tok[0].shape
    vm = pl.BlockSpec(memory_space=pltpu.VMEM)
    anywhere = pl.BlockSpec(memory_space=pl.ANY)
    rows = jax.ShapeDtypeStruct((count, width), BF)
    return pl.pallas_call(
        attention_kernel,
        out_shape=(rows, rows),
        in_specs=[vm] * 13 + [pl.BlockSpec(memory_space=pltpu.SMEM)] + [vm] * 4
        + [anywhere] * 4,
        out_specs=(vm, vm),
        scratch_shapes=[
            pltpu.VMEM(wq.shape, BF), pltpu.VMEM(wk.shape, BF), pltpu.VMEM(wv.shape, BF),
            pltpu.VMEM(wo.shape, BF), pltpu.VMEM((5 * count, width), BF),
            pltpu.VMEM((384, width), BF), pltpu.VMEM((4, 6 * count, 128), BF),
            pltpu.VMEM((5 * count, 512), BF), pltpu.VMEM((5 * count, 512), BF),
            pltpu.VMEM((count, width), BF), pltpu.VMEM((6 * count, 5 * count), F32),
            pltpu.VMEM((6 * count, 5 * count), BF), pltpu.VMEM((6 * count, 1), F32),
            pltpu.SemaphoreType.DMA((4,)),
        ],
        compiler_params=pltpu.CompilerParams(vmem_limit_bytes=ATTENTION_VMEM),
        cost_estimate=pl.CostEstimate(flops=8 << 30, transcendentals=0,
                                      bytes_accessed=20 << 20),
        name="attention_block",
    )(*tok, *adapt, place, gain, gain_moe, cosine, sine, wq, wk, wv, wo)


def expert_kernel(p0, p1, first, table, gate, up, down, out0, out1, last, xe, ho, scale):
    odd, part = first[0], first[1]
    row = lax.broadcasted_iota(jnp.int32, (256, 256), 0)
    col = lax.broadcasted_iota(jnp.int32, (256, 256), 1)
    before = ((row < col) & ((row < 128) == (col < 128))).astype(BF)
    slot = lax.broadcasted_iota(jnp.int32, (2 * CAP, 256), 0).astype(F32)
    base = jnp.where(lax.broadcasted_iota(jnp.int32, (8, 256), 1) < 128, 0.0, float(CAP))

    def places(i):
        named = table[part, i] > 0.0
        rank = jnp.dot(named.astype(F32).astype(BF), before, preferred_element_type=F32) + base
        rank = jnp.where(named, rank, -1.0)
        return [slot == rank[e:e + 1, :] for e in range(3)]

    hots = []
    for i, piece in enumerate((p0, p1)):
        spots = places(i)
        hot = jnp.concatenate([jnp.where(p, 1.0, 0.0) for p in spots]).astype(BF)
        hots.append(hot)
        rows = jnp.dot(hot, piece[...], preferred_element_type=F32).astype(BF)
        given = table[part, i]
        for e in range(3):
            at = slice(i * 2 * CAP, (i + 1) * 2 * CAP)
            xe[e, at, :] = rows[e * 2 * CAP:(e + 1) * 2 * CAP]
            scale[e, at, :] = jnp.sum(jnp.where(spots[e], given[e:e + 1, :], 0.0), axis=1,
                                      keepdims=True)

    def ffn(e, half, count):
        rows = xe[e]
        hidden = []
        for h in range(count):
            g = jnp.dot(rows, gate[half + h], preferred_element_type=F32)
            u = jnp.dot(rows, up[half + h], preferred_element_type=F32)
            hidden.append((g / (1.0 + jnp.exp(-g)) * u).astype(BF))
        hidden = jnp.concatenate(hidden, axis=1)
        depth = pl.ds(pl.multiple_of(256 * half, 256), 256 * count)
        given = scale[e]

        def columns(c, carry):
            at = pl.ds(pl.multiple_of(c * 512, 512), 512)
            out = jnp.dot(hidden, down[depth, at], preferred_element_type=F32)
            ho[e, :, at] = (out * given).astype(BF)
            return carry

        lax.fori_loop(0, 3, columns, 0)

    def whole(e, carry):
        ffn(e, odd + 2 * e, 2)
        return carry

    lax.fori_loop(0, 2, whole, 0)
    ffn(2, 4 - 4 * odd, 1)
    for i, out in enumerate((out0, out1)):
        rows = jnp.concatenate([ho[e, i * 2 * CAP:(i + 1) * 2 * CAP, :] for e in range(3)])
        total = lax.dot_general(hots[i], rows, (((0,), (0,)), ((), ())),
                                preferred_element_type=F32).astype(BF)
        out[...] = total
        marks = table[part, i][3:6]
        left = lax.broadcasted_iota(jnp.int32, marks.shape, 1) < 128
        marks = jnp.concatenate([jnp.where(left, marks, 0.0), jnp.where(left, 0.0, marks),
                                 jnp.zeros((2, 256), F32)]).astype(BF)
        last[i] = jnp.dot(marks, total, preferred_element_type=F32).astype(BF)


def experts(pieces, first, table, gate, up, down):
    width = gate.shape[1]
    shape = pieces[0].shape
    vm = pl.BlockSpec(memory_space=pltpu.VMEM)
    piece = jax.ShapeDtypeStruct((256, width), BF)
    first_out, second_out, last = pl.pallas_call(
        expert_kernel,
        out_shape=(piece, piece, jax.ShapeDtypeStruct((2, 8, width), BF)),
        in_specs=[vm, vm, pl.BlockSpec(memory_space=pltpu.SMEM), vm, vm, vm, vm],
        out_specs=(vm, vm, vm),
        scratch_shapes=[
            pltpu.VMEM((3, 4 * CAP, width), BF), pltpu.VMEM((3, 4 * CAP, width), BF),
            pltpu.VMEM((3, 4 * CAP, 1), F32),
        ],
        compiler_params=pltpu.CompilerParams(vmem_limit_bytes=24 << 20),
        cost_estimate=pl.CostEstimate(flops=7 << 30, transcendentals=0,
                                      bytes_accessed=12 << 20),
        name="expert_block",
    )(*[rows.reshape(256, width) for rows in pieces], first, table, gate, up,
      down.reshape(5 * 256, width))
    return first_out.reshape(shape), second_out.reshape(shape), last


def rms_scaled(features, scales):
    features = features.astype(F32)
    inverse = lax.rsqrt(jnp.mean(features * features, axis=-1, keepdims=True) + EPSILON)
    return (features * inverse * scales).astype(BF)


def body(tokens, lengths, prompt_adapter, routes, routing_weight, attention_gain, query_weight,
         key_weight, value_weight, output_weight, adapter_down_maps, adapter_up_query_output,
         adapter_up_key_value, expert_gain, gate_weight, up_weight, down_weight, closing_gain,
         vocab_projection):
    own = tokens[0]
    count, width = own.shape
    me, grp = lax.axis_index("seq"), lax.axis_index("grp")

    listing = np.concatenate([np.array([0, 1, 2] if g % 2 == 0 else [1, 2, 0]) + 5 * g // 2
                              for g in range(16)]).astype(np.int32)
    ids, given = routes[0], routing_weight[0]
    table = jnp.sum(jnp.where(ids.T[None] == jnp.asarray(listing)[:, None, None],
                              given.T[None], 0.0), axis=1).reshape(16, 3 * count)
    high = lax.reduce_precision(table, 8, 7)
    low = table - high
    route_rows = jnp.concatenate(
        [high, low, jnp.zeros((16, width - 6 * count), F32)], axis=1).astype(BF)

    ranks = (jnp.arange(16, dtype=jnp.int32)[:, None]
             == 2 * me + jnp.arange(2, dtype=jnp.int32)[None, :]).astype(BF)
    downs = jnp.einsum("rk,pdr->pkd", ranks, adapter_down_maps[:, 0],
                       preferred_element_type=F32).astype(BF).reshape(8, width)
    ups = lax.dynamic_slice_in_dim(adapter_up_query_output[:, 0], 2 * me, 2, 1).reshape(4, width)
    thin = lax.dynamic_slice_in_dim(adapter_up_key_value[:, 0], 2 * me, 2, 1)
    thin = jnp.concatenate([thin[0], thin[1], jnp.zeros((2, width - 1024), BF)], axis=1)
    maps = jnp.concatenate([downs, ups, thin], axis=0)
    ends = jnp.cumsum(lengths[0])
    marks = (ends[:, None] - 1 == me * count + jnp.arange(count, dtype=jnp.int32)[None, :])
    mark_row = jnp.concatenate([marks.reshape(1, 3 * count).astype(BF),
                                jnp.zeros((1, width - 3 * count), BF)], axis=1)
    payload = jnp.concatenate(
        [jnp.broadcast_to(maps[None], (16, 14, width)), route_rows[:, None, :],
         jnp.broadcast_to(mark_row[None], (16, 1, width))], axis=1)
    payload, own = lax.optimization_barrier((payload, own))
    held = lax.all_to_all(payload, "grp", 0, 0, tiled=True)
    back1 = lax.ppermute(own, "seq", [(s, s + 2) for s in range(6)])
    back2 = lax.ppermute(own, "seq", [(s, s + 4) for s in range(4)])
    odd_core = me % 2 == 1
    tok = [own, back1, back2, partner(jnp.where(odd_core, back1, own)),
           partner(jnp.where(odd_core, back2, back1))]

    lens = lengths[0]
    starts = ends - lens
    blocks = me - jnp.array([0, 2, 4, 1, 3], jnp.int32)
    row = jnp.arange(count, dtype=jnp.int32)
    index = (blocks[:, None] * count + row[None, :]).reshape(-1)
    document = jnp.sum((index[:, None] >= ends[None, :]).astype(jnp.int32), axis=1)
    half = HEAD // 2
    frequency = ROPE_BASE ** (-(jnp.arange(128, dtype=jnp.int32) % half).astype(F32) / half)
    sign = jnp.where(jnp.arange(128) % HEAD < half, -1.0, 1.0).astype(F32)
    near = row.astype(F32)[:, None] * frequency[None, :]
    far = (blocks[:, None] * count - starts[None, :]).astype(F32)[:, :, None] * frequency
    near_cos, near_sin = jnp.cos(near)[None], jnp.sin(near)[None]
    far_cos, far_sin = jnp.cos(far), jnp.sin(far)

    def by_document(values):
        docs = document.reshape(5, count, 1)
        return jnp.where(docs == 0, values[:, None, 0], jnp.where(
            docs == 1, values[:, None, 1], values[:, None, 2]))

    far_cos, far_sin = by_document(far_cos), by_document(far_sin)
    cosine = (far_cos * near_cos - far_sin * near_sin).reshape(5 * count, 128)
    sine = ((far_sin * near_cos + far_cos * near_sin) * sign).reshape(5 * count, 128)
    row_index = index[:count]
    place = jnp.concatenate([ends, me[None]]).astype(jnp.int32)
    gain, gain_moe = attention_gain[None], expert_gain[None]
    held, cosine, sine, place, gain, gain_moe = lax.optimization_barrier(
        (held, cosine, sine, place, gain, gain_moe))
    picked = jnp.stack([lax.dynamic_index_in_dim(held, prompt_adapter[0, p], 0, False)
                        for p in range(3)]).reshape(48, width)
    turn = [picked] + [lax.ppermute(picked, "seq", [(s, (s + d) % 8) for s in range(8)])
                       for d in (2, 6, 4)]
    rel = jnp.array([0, 3, 1, 2], jnp.int32)
    first, second = jnp.where(me % 2 == 0, grp % 4, grp // 4), jnp.where(
        me % 2 == 0, grp // 4, grp % 4)
    first, second = (first + rel[None, :]) % 4, (second + rel[:, None]) % 4
    source = jnp.where(me % 2 == 0, second * 4 + first, first * 4 + second).reshape(8, 2)
    source = jnp.concatenate([source[:3], source[5:6], source[3:5], source[6:]]).reshape(16)
    order = (source[:, None] == jnp.arange(16, dtype=jnp.int32)[None, :]).astype(F32)
    route_in = jnp.concatenate(
        [held[:, 14, :3 * count].astype(F32) + held[:, 14, 3 * count:6 * count].astype(F32),
         held[:, 15, :3 * count].astype(F32)], axis=1)
    route_in = jnp.dot(order, route_in, precision=lax.Precision.HIGHEST)
    route_in = route_in.reshape(8, 2, 6, count)
    route_in = jnp.concatenate([route_in, jnp.zeros((8, 2, 2, count), F32)], axis=2)
    route_in = route_in.transpose(0, 2, 1, 3).reshape(4, 2, 8, 2 * count)
    odd = (grp % 2).astype(jnp.int32)
    weights = (gate_weight, up_weight, down_weight)

    turn, route_in = lax.optimization_barrier((turn, route_in))
    adapt = turn + [partner(piece) for piece in turn]
    mixed, moe_in = attention(tok, adapt, place, gain, gain_moe, cosine, sine, query_weight,
                              key_weight, value_weight, output_weight)

    def share(pieces, which):
        return experts(pieces, jnp.stack([odd, jnp.int32(which)]), route_in, *weights)

    line = lax.optimization_barrier(
        [shift(moe_in, 0, 1), shift(moe_in, 0, -1), shift(moe_in, 0, 2)])
    own_lo, own_hi = jnp.stack([moe_in, line[0]]), jnp.stack([line[1], line[2]])
    minus_lo, plus_hi = shift(own_lo, 1, 1), shift(own_hi, 1, -1)
    minus_hi, plus_lo = shift(own_hi, 1, 1), shift(own_lo, 1, -1)
    own_lo, own_hi, last_own = share([own_lo, own_hi], 0)
    minus_lo, plus_hi, own_lo, own_hi = lax.optimization_barrier(
        (minus_lo, plus_hi, own_lo, own_hi))
    far_lo, far_hi = shift(minus_lo, 1, 1), shift(plus_hi, 1, -1)
    first_lo, first_hi, last_first = share([minus_lo, plus_hi], 1)
    minus_hi, plus_lo, first_lo, first_hi = lax.optimization_barrier(
        (minus_hi, plus_lo, first_lo, first_hi))
    minus_hi, plus_lo, last_second = share([minus_hi, plus_lo], 2)
    minus_lo, plus_hi, minus_hi, plus_lo, far_lo, far_hi = lax.optimization_barrier(
        (first_lo, first_hi, minus_hi, plus_lo, far_lo, far_hi))

    minus_lo, plus_hi = shift(minus_lo, 1, -1), shift(plus_hi, 1, 1)
    far_lo, far_hi, last_far = share([far_lo, far_hi], 3)
    columns = width // 8
    last = jnp.stack([last_own, last_first, last_second, last_far])[:, :, :6]
    last = jnp.einsum("jg,jr->gr", order.astype(BF), last.reshape(16, 3 * width),
                      preferred_element_type=F32).astype(BF)
    last = last.reshape(16, 3, 8, columns).transpose(2, 0, 1, 3)
    rows = jnp.dot(marks.astype(BF), mixed, preferred_element_type=F32).astype(BF)
    rows = rows.reshape(3, 8, columns).transpose(1, 0, 2)[:, None]
    here = (jnp.arange(16, dtype=jnp.int32) == grp)[None, :, None, None]
    shares = jnp.concatenate([last, jnp.where(here, rows, 0)], axis=2)
    shares = shares.reshape(128, 6, columns)
    far_lo, far_hi, shares = lax.optimization_barrier(
        (shift(far_lo, 1, 1), shift(far_hi, 1, -1), shares))
    plus_lo = shift((wide(plus_lo) + wide(far_lo)).astype(BF), 1, 1)
    minus_hi = shift((wide(minus_hi) + wide(far_hi)).astype(BF), 1, -1)
    minus_lo, plus_hi, minus_hi, plus_lo, shares = lax.optimization_barrier(
        (minus_lo, plus_hi, minus_hi, plus_lo, lax.all_to_all(shares, WHOLE, 0, 0, tiled=True)))
    own_lo = wide(own_lo) + wide(plus_lo) + wide(minus_lo)
    own_hi = wide(own_hi) + wide(plus_hi) + wide(minus_hi)
    line = [shift(own_hi[0].astype(BF), 0, 1), shift(own_lo[1].astype(BF), 0, -1),
            shift(own_hi[1].astype(BF), 0, 2)]

    mine = jnp.sum(shares.astype(F32), axis=0)
    mine = (mine[:3] + mine[3:]).astype(BF)
    everyone = lax.all_to_all(jnp.broadcast_to(mine[None], (128, 3, columns)), WHOLE, 0, 0,
                              tiled=True)
    final_rows = everyone.reshape(8, 48, columns).transpose(1, 0, 2).reshape(48, width)
    final_rows = rms_scaled(final_rows, closing_gain)
    logits = jnp.dot(final_rows, vocab_projection, preferred_element_type=F32)
    top = jnp.max(logits, axis=1)
    mass = jnp.sum(jnp.exp(logits - top[:, None]), axis=1)
    stats = jnp.concatenate([top, mass, jnp.zeros((32,), F32)])
    line, stats = lax.optimization_barrier((line, stats))
    combined = own_lo[0] + wide(line[0]) + wide(line[1]) + wide(line[2])
    hidden_out = (mixed.astype(F32) + combined).astype(BF)
    stats = lax.all_to_all(jnp.broadcast_to(stats[None], (128, 128)), WHOLE, 0, 0, tiled=True)
    tops = stats[:, :48]
    peak = jnp.max(tops, axis=0)
    total = jnp.sum(stats[:, 48:96] * jnp.exp(tops - peak[None]), axis=0)
    log_probs = logits - (peak + jnp.log(total))[:, None]
    return hidden_out[None], log_probs


def solution(mesh):
    placed = (
        P("grp", "seq", None), P("grp", None), P("grp", None), P("grp", "seq", None),
        P("grp", "seq", None), P(), P(), P(), P(), P(), P(None, "grp", None, None),
        P(None, "grp", None, None), P(None, "grp", None, None), P(), P("grp", None, None),
        P("grp", None, None), P("grp", None, None), P(), P(None, WHOLE),
    )
    return jax.shard_map(
        body,
        mesh=mesh,
        in_specs=placed,
        out_specs=(P("grp", "seq", None), P(None, WHOLE)),
        check_vma=False,
    )
```

```python
import jax
import jax.numpy as jnp
import numpy as np
from jax import lax
from jax.experimental import pallas as pl
from jax.experimental.pallas import tpu as pltpu
from jax.sharding import PartitionSpec as P

HEADS = 24
KV_HEADS = 8
HEAD = 64
EXPERTS = 40
TOP = 8
CAP = 40
ATTENTION_VMEM = 63 << 20
EPSILON = 1e-05
ROPE_BASE = 10000.0
MASKED = -1e30
SIDE = 4
BF = jnp.bfloat16
F32 = jnp.float32
WHOLE = ("seq", "grp")


def shift(rows, phase, step):
    pairs = []
    for s in range(8):
        for i in range(16):
            if s % 2 == phase:
                to = i // SIDE * SIDE + (i % SIDE + step) % SIDE
            else:
                to = (i // SIDE + step) % SIDE * SIDE + i % SIDE
            pairs.append((s * 16 + i, s * 16 + to))
    return lax.ppermute(rows, WHOLE, pairs)


def partner(rows):
    return lax.ppermute(rows, "seq", [(s, s ^ 1) for s in range(8)])


def wide(v):
    return v.astype(F32)


def dot_t(lhs, rhs):
    return lax.dot_general(lhs, rhs, (((1,), (1,)), ((), ())), preferred_element_type=F32)


def norm(rows, scale):
    inverse = lax.rsqrt(jnp.mean(rows * rows, axis=-1, keepdims=True) + EPSILON)
    return (rows * inverse * scale).astype(BF)


def attention_kernel(*refs):
    tok = refs[0:5]
    adapt = refs[5:13]
    (place, gain, gain_moe, cosine, sine, wq_hbm, wk_hbm, wv_hbm, wo_hbm, mixed_out, moe_out,
     wq, wk, wv, wo, xn, ad, qbuf, kbuf, vbuf, att, score, prob, sems) = refs[13:]
    loads = [pltpu.make_async_copy(src, dst, sems.at[i]) for i, (src, dst) in enumerate(
        [(wk_hbm, wk), (wv_hbm, wv), (wq_hbm, wq), (wo_hbm, wo)])]
    for load in loads:
        load.start()
    count = tok[0].shape[0]
    ends = [place[0], place[1], place[2]]
    me = place[3]

    def document(index):
        return sum((index >= end).astype(jnp.int32) for end in ends)

    def block_start(b):
        return (me - jnp.where(b < 3, 2 * b, 2 * b - 5)) * count

    for j in range(8):
        ad[48 * j:48 * j + 48, :] = adapt[j][...]
    for b in range(5):
        xn[b * count:(b + 1) * count, :] = norm(tok[b][...].astype(F32), gain[...])
    column = lax.broadcasted_iota(jnp.int32, (1, 384), 1)
    col_row = column & 15
    col_prompt = column >> 4
    col_prompt = col_prompt - 3 * ((col_prompt * 171) >> 9)

    def low(z, roll, first, docs):
        moved = pltpu.roll(z, roll, 1)
        keep = (docs == col_prompt) & (col_row >= first) & (col_row < first + 2)
        return jnp.where(keep, moved, 0.0).astype(BF)

    lane = lax.broadcasted_iota(jnp.int32, (count, 128), 1)
    down_rows = lax.broadcasted_iota(jnp.int32, (count, 1), 0)

    def rope(u, cos_t, sin_t):
        lower = (lax.broadcasted_iota(jnp.int32, u.shape, 1) & 63) < 32
        turned = jnp.where(lower, pltpu.roll(u, 96, 1), pltpu.roll(u, 32, 1))
        return u * cos_t + turned * sin_t

    loads[0].wait()
    loads[1].wait()

    def key_block(b, carry):
        size = 5 * count // 2
        at = pl.ds(pl.multiple_of(b * size, 16), size)
        row = b * size + lax.broadcasted_iota(jnp.int32, (size, 1), 0)
        docs = document(block_start(row >> 7) + (row & 127))
        rows = xn[at, :]
        z = dot_t(rows, ad[...])
        keys = jnp.dot(rows, wk[...], preferred_element_type=F32) + jnp.dot(
            low(z, 10, 12, docs), ad[:, :512], preferred_element_type=F32)
        values = jnp.dot(rows, wv[...], preferred_element_type=F32) + jnp.dot(
            low(z, 8, 12, docs), ad[:, 512:1024], preferred_element_type=F32)
        vbuf[at, :] = values.astype(BF)
        cos_t = cosine[at, :]
        sin_t = sine[at, :]
        for c in range(4):
            kbuf[at, 128 * c:128 * c + 128] = rope(
                keys[:, 128 * c:128 * c + 128], cos_t, sin_t).astype(BF)
        return carry

    lax.fori_loop(0, 2, key_block, 0)
    own_index = me * count + down_rows
    docs = document(own_index)
    own = xn[0:count, :]
    zq = low(dot_t(own, ad[...]), 8, 8, docs)
    cos_t = cosine[0:count, :]
    sin_t = sine[0:count, :]
    low_half = lane < 64
    along = lax.broadcasted_iota(jnp.int32, (1, count), 1)
    key_index = jnp.concatenate([block_start(b) + along for b in range(5)], axis=1)
    allowed = ((docs == document(key_index)) & (key_index <= own_index) & (key_index >= 0))
    bias = jnp.where(allowed, 0.0, MASKED)
    loads[2].wait()

    def query_block(c, carry):
        at = pl.multiple_of(c * 384, 128)
        u = jnp.dot(own, wq[:, pl.ds(at, 384)], preferred_element_type=F32) + jnp.dot(
            zq, ad[:, pl.ds(at, 384)], preferred_element_type=F32)
        for t in range(3):
            q = rope(u[:, 128 * t:128 * t + 128], cos_t, sin_t).astype(BF).astype(F32)
            q = q * (HEAD ** -0.5)
            turned = pltpu.roll(q, 64, 1)
            for own_low in (True, False):
                h = 2 * t + (0 if own_low else 1)
                kv_low = h < 3
                rows = q if own_low == kv_low else turned
                keep = low_half if kv_low else ~low_half
                qbuf[c, count * h:count * h + count, :] = jnp.where(keep, rows, 0.0).astype(BF)
        return carry

    lax.fori_loop(0, 4, query_block, 0)

    def pair(j, carry):
        kv = pl.ds(pl.multiple_of(j * 128, 128), 128)
        score[...] = dot_t(qbuf[j], kbuf[:, kv])
        totals = []
        for h in range(6):
            at = slice(count * h, count * h + count)
            s = score[at, :] + bias
            top = jnp.max(s, axis=-1, keepdims=True)
            w = jnp.exp(s - top)
            totals.append(jnp.sum(w, axis=-1, keepdims=True))
            prob[at, :] = w.astype(BF)
        out = jnp.dot(prob[...], vbuf[:, kv], preferred_element_type=F32)
        results = []
        for h in range(6):
            o = out[count * h:count * h + count] / totals[h]
            results.append(pltpu.roll(o, 64, 1) if (h % 2 == 0) != (h < 3) else o)
        for t in range(3):
            att[:, pl.ds(pl.multiple_of(j * 384 + 128 * t, 128), 128)] = jnp.where(
                low_half, results[2 * t], results[2 * t + 1]).astype(BF)
        return carry

    lax.fori_loop(0, 4, pair, 0)
    loads[3].wait()
    attended = att[...]
    zo = low(dot_t(attended, ad[...]), 4, 10, docs)

    def out_block(c, carry):
        at = pl.ds(pl.multiple_of(c * 512, 512), 512)
        mixed_out[:, at] = (
            tok[0][:, at].astype(F32)
            + jnp.dot(attended, wo[:, at], preferred_element_type=F32)
            + jnp.dot(zo, ad[:, at], preferred_element_type=F32)).astype(BF)
        return carry

    lax.fori_loop(0, 3, out_block, 0)
    moe_out[...] = norm(mixed_out[...].astype(F32), gain_moe[...])


def attention(tok, adapt, place, gain, gain_moe, cosine, sine, wq, wk, wv, wo):
    count, width = tok[0].shape
    vm = pl.BlockSpec(memory_space=pltpu.VMEM)
    anywhere = pl.BlockSpec(memory_space=pl.ANY)
    rows = jax.ShapeDtypeStruct((count, width), BF)
    return pl.pallas_call(
        attention_kernel,
        out_shape=(rows, rows),
        in_specs=[vm] * 13 + [pl.BlockSpec(memory_space=pltpu.SMEM)] + [vm] * 4
        + [anywhere] * 4,
        out_specs=(vm, vm),
        scratch_shapes=[
            pltpu.VMEM(wq.shape, BF), pltpu.VMEM(wk.shape, BF), pltpu.VMEM(wv.shape, BF),
            pltpu.VMEM(wo.shape, BF), pltpu.VMEM((5 * count, width), BF),
            pltpu.VMEM((384, width), BF), pltpu.VMEM((4, 6 * count, 128), BF),
            pltpu.VMEM((5 * count, 512), BF), pltpu.VMEM((5 * count, 512), BF),
            pltpu.VMEM((count, width), BF), pltpu.VMEM((6 * count, 5 * count), F32),
            pltpu.VMEM((6 * count, 5 * count), BF), pltpu.SemaphoreType.DMA((4,)),
        ],
        compiler_params=pltpu.CompilerParams(vmem_limit_bytes=ATTENTION_VMEM),
        cost_estimate=pl.CostEstimate(flops=8 << 30, transcendentals=0,
                                      bytes_accessed=20 << 20),
        name="attention_block",
    )(*tok, *adapt, place, gain, gain_moe, cosine, sine, wq, wk, wv, wo)


def expert_kernel(p0, p1, first, table, gate, up, down, out0, out1, last, xe, ho, scale):
    odd, part = first[0], first[1]
    row = lax.broadcasted_iota(jnp.int32, (256, 256), 0)
    col = lax.broadcasted_iota(jnp.int32, (256, 256), 1)
    before = ((row < col) & ((row < 128) == (col < 128))).astype(BF)
    slot = lax.broadcasted_iota(jnp.int32, (2 * CAP, 256), 0).astype(F32)
    base = jnp.where(lax.broadcasted_iota(jnp.int32, (8, 256), 1) < 128, 0.0, float(CAP))

    def places(i):
        named = table[part, i] > 0.0
        rank = jnp.dot(named.astype(F32).astype(BF), before, preferred_element_type=F32) + base
        rank = jnp.where(named, rank, -1.0)
        return [slot == rank[e:e + 1, :] for e in range(3)]

    hots = []
    for i, piece in enumerate((p0, p1)):
        spots = places(i)
        hot = jnp.concatenate([jnp.where(p, 1.0, 0.0) for p in spots]).astype(BF)
        hots.append(hot)
        rows = jnp.dot(hot, piece[...], preferred_element_type=F32).astype(BF)
        given = table[part, i]
        for e in range(3):
            at = slice(i * 2 * CAP, (i + 1) * 2 * CAP)
            xe[e, at, :] = rows[e * 2 * CAP:(e + 1) * 2 * CAP]
            scale[e, at, :] = jnp.sum(jnp.where(spots[e], given[e:e + 1, :], 0.0), axis=1,
                                      keepdims=True)

    def ffn(e, half, count):
        rows = xe[e]
        hidden = []
        for h in range(count):
            g = jnp.dot(rows, gate[half + h], preferred_element_type=F32)
            u = jnp.dot(rows, up[half + h], preferred_element_type=F32)
            hidden.append((g / (1.0 + jnp.exp(-g)) * u).astype(BF))
        hidden = jnp.concatenate(hidden, axis=1)
        maps = down[pl.ds(pl.multiple_of(256 * half, 256), 256 * count), :]
        out = jnp.dot(hidden, maps, preferred_element_type=F32)
        ho[e] = (out * scale[e]).astype(BF)

    def whole(e, carry):
        ffn(e, odd + 2 * e, 2)
        return carry

    lax.fori_loop(0, 2, whole, 0)
    ffn(2, 4 - 4 * odd, 1)
    for i, out in enumerate((out0, out1)):
        rows = jnp.concatenate([ho[e, i * 2 * CAP:(i + 1) * 2 * CAP, :] for e in range(3)])
        total = lax.dot_general(hots[i], rows, (((0,), (0,)), ((), ())),
                                preferred_element_type=F32).astype(BF)
        out[...] = total
        marks = table[part, i][3:6]
        left = lax.broadcasted_iota(jnp.int32, marks.shape, 1) < 128
        marks = jnp.concatenate([jnp.where(left, marks, 0.0), jnp.where(left, 0.0, marks),
                                 jnp.zeros((2, 256), F32)]).astype(BF)
        last[i] = jnp.dot(marks, total, preferred_element_type=F32).astype(BF)


def experts(pieces, first, table, gate, up, down):
    width = gate.shape[1]
    shape = pieces[0].shape
    vm = pl.BlockSpec(memory_space=pltpu.VMEM)
    piece = jax.ShapeDtypeStruct((256, width), BF)
    first_out, second_out, last = pl.pallas_call(
        expert_kernel,
        out_shape=(piece, piece, jax.ShapeDtypeStruct((2, 8, width), BF)),
        in_specs=[vm, vm, pl.BlockSpec(memory_space=pltpu.SMEM), vm, vm, vm, vm],
        out_specs=(vm, vm, vm),
        scratch_shapes=[
            pltpu.VMEM((3, 4 * CAP, width), BF), pltpu.VMEM((3, 4 * CAP, width), BF),
            pltpu.VMEM((3, 4 * CAP, 1), F32),
        ],
        compiler_params=pltpu.CompilerParams(vmem_limit_bytes=24 << 20),
        cost_estimate=pl.CostEstimate(flops=7 << 30, transcendentals=0,
                                      bytes_accessed=12 << 20),
        name="expert_block",
    )(*[rows.reshape(256, width) for rows in pieces], first, table, gate, up,
      down.reshape(5 * 256, width))
    return first_out.reshape(shape), second_out.reshape(shape), last


def rms_scaled(features, scales):
    features = features.astype(F32)
    inverse = lax.rsqrt(jnp.mean(features * features, axis=-1, keepdims=True) + EPSILON)
    return (features * inverse * scales).astype(BF)


def body(tokens, lengths, prompt_adapter, routes, routing_weight, attention_gain, query_weight,
         key_weight, value_weight, output_weight, adapter_down_maps, adapter_up_query_output,
         adapter_up_key_value, expert_gain, gate_weight, up_weight, down_weight, closing_gain,
         vocab_projection):
    own = tokens[0]
    count, width = own.shape
    me, grp = lax.axis_index("seq"), lax.axis_index("grp")

    listing = np.concatenate([np.array([0, 1, 2] if g % 2 == 0 else [1, 2, 0]) + 5 * g // 2
                              for g in range(16)]).astype(np.int32)
    ids, given = routes[0], routing_weight[0]
    table = jnp.sum(jnp.where(ids.T[None] == jnp.asarray(listing)[:, None, None],
                              given.T[None], 0.0), axis=1).reshape(16, 3 * count)
    high = lax.reduce_precision(table, 8, 7)
    low = table - high
    route_rows = jnp.concatenate(
        [high, low, jnp.zeros((16, width - 6 * count), F32)], axis=1).astype(BF)

    ranks = (jnp.arange(16, dtype=jnp.int32)[:, None]
             == 2 * me + jnp.arange(2, dtype=jnp.int32)[None, :]).astype(BF)
    downs = jnp.einsum("rk,pdr->pkd", ranks, adapter_down_maps[:, 0],
                       preferred_element_type=F32).astype(BF).reshape(8, width)
    ups = lax.dynamic_slice_in_dim(adapter_up_query_output[:, 0], 2 * me, 2, 1).reshape(4, width)
    thin = lax.dynamic_slice_in_dim(adapter_up_key_value[:, 0], 2 * me, 2, 1)
    thin = jnp.concatenate([thin[0], thin[1], jnp.zeros((2, width - 1024), BF)], axis=1)
    maps = jnp.concatenate([downs, ups, thin], axis=0)
    ends = jnp.cumsum(lengths[0])
    marks = (ends[:, None] - 1 == me * count + jnp.arange(count, dtype=jnp.int32)[None, :])
    mark_row = jnp.concatenate([marks.reshape(1, 3 * count).astype(BF),
                                jnp.zeros((1, width - 3 * count), BF)], axis=1)
    payload = jnp.concatenate(
        [jnp.broadcast_to(maps[None], (16, 14, width)), route_rows[:, None, :],
         jnp.broadcast_to(mark_row[None], (16, 1, width))], axis=1)
    payload, own = lax.optimization_barrier((payload, own))
    held = lax.all_to_all(payload, "grp", 0, 0, tiled=True)
    back1 = lax.ppermute(own, "seq", [(s, s + 2) for s in range(6)])
    back2 = lax.ppermute(own, "seq", [(s, s + 4) for s in range(4)])
    odd_core = me % 2 == 1
    tok = [own, back1, back2, partner(jnp.where(odd_core, back1, own)),
           partner(jnp.where(odd_core, back2, back1))]

    lens = lengths[0]
    starts = ends - lens
    blocks = me - jnp.array([0, 2, 4, 1, 3], jnp.int32)
    row = jnp.arange(count, dtype=jnp.int32)
    index = (blocks[:, None] * count + row[None, :]).reshape(-1)
    document = jnp.sum((index[:, None] >= ends[None, :]).astype(jnp.int32), axis=1)
    half = HEAD // 2
    frequency = ROPE_BASE ** (-(jnp.arange(128, dtype=jnp.int32) % half).astype(F32) / half)
    sign = jnp.where(jnp.arange(128) % HEAD < half, -1.0, 1.0).astype(F32)
    near = row.astype(F32)[:, None] * frequency[None, :]
    far = (blocks[:, None] * count - starts[None, :]).astype(F32)[:, :, None] * frequency
    near_cos, near_sin = jnp.cos(near)[None], jnp.sin(near)[None]
    far_cos, far_sin = jnp.cos(far), jnp.sin(far)

    def by_document(values):
        docs = document.reshape(5, count, 1)
        return jnp.where(docs == 0, values[:, None, 0], jnp.where(
            docs == 1, values[:, None, 1], values[:, None, 2]))

    far_cos, far_sin = by_document(far_cos), by_document(far_sin)
    cosine = (far_cos * near_cos - far_sin * near_sin).reshape(5 * count, 128)
    sine = ((far_sin * near_cos + far_cos * near_sin) * sign).reshape(5 * count, 128)
    row_index = index[:count]
    place = jnp.concatenate([ends, me[None]]).astype(jnp.int32)
    gain, gain_moe = attention_gain[None], expert_gain[None]
    held, cosine, sine, place, gain, gain_moe = lax.optimization_barrier(
        (held, cosine, sine, place, gain, gain_moe))
    picked = jnp.stack([lax.dynamic_index_in_dim(held, prompt_adapter[0, p], 0, False)
                        for p in range(3)]).reshape(48, width)
    turn = [picked] + [lax.ppermute(picked, "seq", [(s, (s + d) % 8) for s in range(8)])
                       for d in (2, 6, 4)]
    rel = jnp.array([0, 3, 1, 2], jnp.int32)
    first, second = jnp.where(me % 2 == 0, grp % 4, grp // 4), jnp.where(
        me % 2 == 0, grp // 4, grp % 4)
    first, second = (first + rel[None, :]) % 4, (second + rel[:, None]) % 4
    source = jnp.where(me % 2 == 0, second * 4 + first, first * 4 + second).reshape(8, 2)
    source = jnp.concatenate([source[:3], source[5:6], source[3:5], source[6:]]).reshape(16)
    order = (source[:, None] == jnp.arange(16, dtype=jnp.int32)[None, :]).astype(F32)
    route_in = jnp.concatenate(
        [held[:, 14, :3 * count].astype(F32) + held[:, 14, 3 * count:6 * count].astype(F32),
         held[:, 15, :3 * count].astype(F32)], axis=1)
    route_in = jnp.dot(order, route_in, precision=lax.Precision.HIGHEST)
    route_in = route_in.reshape(8, 2, 6, count)
    route_in = jnp.concatenate([route_in, jnp.zeros((8, 2, 2, count), F32)], axis=2)
    route_in = route_in.transpose(0, 2, 1, 3).reshape(4, 2, 8, 2 * count)
    odd = (grp % 2).astype(jnp.int32)
    weights = (gate_weight, up_weight, down_weight)

    turn, route_in = lax.optimization_barrier((turn, route_in))
    adapt = turn + [partner(piece) for piece in turn]
    mixed, moe_in = attention(tok, adapt, place, gain, gain_moe, cosine, sine, query_weight,
                              key_weight, value_weight, output_weight)

    def share(pieces, which):
        return experts(pieces, jnp.stack([odd, jnp.int32(which)]), route_in, *weights)

    line = lax.optimization_barrier(
        [shift(moe_in, 0, 1), shift(moe_in, 0, -1), shift(moe_in, 0, 2)])
    own_lo, own_hi = jnp.stack([moe_in, line[0]]), jnp.stack([line[1], line[2]])
    minus_lo, plus_hi = shift(own_lo, 1, 1), shift(own_hi, 1, -1)
    minus_hi, plus_lo = shift(own_hi, 1, 1), shift(own_lo, 1, -1)
    own_lo, own_hi, last_own = share([own_lo, own_hi], 0)
    minus_lo, plus_hi, own_lo, own_hi = lax.optimization_barrier(
        (minus_lo, plus_hi, own_lo, own_hi))
    far_lo, far_hi = shift(minus_lo, 1, 1), shift(plus_hi, 1, -1)
    first_lo, first_hi, last_first = share([minus_lo, plus_hi], 1)
    minus_hi, plus_lo, first_lo, first_hi = lax.optimization_barrier(
        (minus_hi, plus_lo, first_lo, first_hi))
    minus_hi, plus_lo, last_second = share([minus_hi, plus_lo], 2)
    minus_lo, plus_hi, minus_hi, plus_lo, far_lo, far_hi = lax.optimization_barrier(
        (first_lo, first_hi, minus_hi, plus_lo, far_lo, far_hi))

    minus_lo, plus_hi = shift(minus_lo, 1, -1), shift(plus_hi, 1, 1)
    far_lo, far_hi, last_far = share([far_lo, far_hi], 3)
    minus_lo, plus_hi, far_lo, far_hi, last_far = lax.optimization_barrier(
        (minus_lo, plus_hi, far_lo, far_hi, last_far))
    far_lo, far_hi = lax.optimization_barrier((shift(far_lo, 1, 1), shift(far_hi, 1, -1)))
    plus_lo = (wide(plus_lo) + wide(far_lo)).astype(BF)
    minus_hi = (wide(minus_hi) + wide(far_hi)).astype(BF)

    last = jnp.stack([last_own, last_first, last_second, last_far])[:, :, :6]
    last = jnp.einsum("jg,jr->gr", order.astype(BF), last.reshape(16, 3 * width),
                      preferred_element_type=F32).astype(BF)
    last = lax.all_to_all(last.reshape(16, 3, width), "grp", 0, 0, tiled=True)
    last = jnp.sum(last.astype(F32), axis=0) + jnp.dot(
        marks.astype(BF), mixed, preferred_element_type=F32)
    last = rms_scaled(last.astype(BF), closing_gain)
    part = width // 8
    split = last.reshape(3, 8, part).transpose(1, 0, 2)
    mine = lax.all_to_all(split, "seq", 0, 0, tiled=True)
    mine = jnp.sum(mine.astype(F32), axis=0).astype(BF)
    plus_lo, minus_hi, mine = lax.optimization_barrier((plus_lo, minus_hi, mine))
    everyone = lax.all_to_all(jnp.broadcast_to(mine[None], (128, 3, part)), WHOLE, 0, 0,
                              tiled=True)
    final_rows = everyone.reshape(8, 48, part).transpose(1, 0, 2).reshape(48, width)
    logits = jnp.dot(final_rows, vocab_projection, preferred_element_type=F32)
    top = jnp.max(logits, axis=1)
    mass = jnp.sum(jnp.exp(logits - top[:, None]), axis=1)
    stats = jnp.concatenate([top, mass, jnp.zeros((32,), F32)])
    plus_lo, minus_hi = shift(plus_lo, 1, 1), shift(minus_hi, 1, -1)
    own_lo = wide(own_lo) + wide(plus_lo) + wide(minus_lo)
    own_hi = wide(own_hi) + wide(plus_hi) + wide(minus_hi)
    line = [own_hi[0].astype(BF), own_lo[1].astype(BF), own_hi[1].astype(BF)]
    line, stats = lax.optimization_barrier((line, stats))
    line = lax.optimization_barrier(
        [shift(line[0], 0, 1), shift(line[1], 0, -1), shift(line[2], 0, 2)])
    combined = own_lo[0] + wide(line[0]) + wide(line[1]) + wide(line[2])
    hidden_out = (mixed.astype(F32) + combined).astype(BF)
    stats = lax.all_to_all(jnp.broadcast_to(stats[None], (128, 128)), WHOLE, 0, 0, tiled=True)
    tops = stats[:, :48]
    peak = jnp.max(tops, axis=0)
    total = jnp.sum(stats[:, 48:96] * jnp.exp(tops - peak[None]), axis=0)
    log_probs = logits - (peak + jnp.log(total))[:, None]
    return hidden_out[None], log_probs


def solution(mesh):
    placed = (
        P("grp", "seq", None), P("grp", None), P("grp", None), P("grp", "seq", None),
        P("grp", "seq", None), P(), P(), P(), P(), P(), P(None, "grp", None, None),
        P(None, "grp", None, None), P(None, "grp", None, None), P(), P("grp", None, None),
        P("grp", None, None), P("grp", None, None), P(), P(None, WHOLE),
    )
    return jax.shard_map(
        body,
        mesh=mesh,
        in_specs=placed,
        out_specs=(P("grp", "seq", None), P(None, WHOLE)),
        check_vma=False,
    )
```

```python
import jax
import jax.numpy as jnp
import numpy as np
from jax import lax
from jax.experimental import pallas as pl
from jax.experimental.pallas import tpu as pltpu
from jax.sharding import PartitionSpec as P

HEADS = 24
KV_HEADS = 8
HEAD = 64
EXPERTS = 40
TOP = 8
CAP = 40
ATTENTION_VMEM = 63 << 20
EPSILON = 1e-05
ROPE_BASE = 10000.0
MASKED = -1e30
SIDE = 4
BF = jnp.bfloat16
F32 = jnp.float32
WHOLE = ("seq", "grp")


def shift(rows, phase, step):
    pairs = []
    for s in range(8):
        for i in range(16):
            if s % 2 == phase:
                to = i // SIDE * SIDE + (i % SIDE + step) % SIDE
            else:
                to = (i // SIDE + step) % SIDE * SIDE + i % SIDE
            pairs.append((s * 16 + i, s * 16 + to))
    return lax.ppermute(rows, WHOLE, pairs)


def partner(rows):
    return lax.ppermute(rows, "seq", [(s, s ^ 1) for s in range(8)])


def wide(v):
    return v.astype(F32)


def dot_t(lhs, rhs):
    return lax.dot_general(lhs, rhs, (((1,), (1,)), ((), ())), preferred_element_type=F32)


def norm(rows, scale):
    inverse = lax.rsqrt(jnp.mean(rows * rows, axis=-1, keepdims=True) + EPSILON)
    return (rows * inverse * scale).astype(BF)


def attention_kernel(*refs):
    tok = refs[0:5]
    adapt = refs[5:13]
    (place, gain, gain_moe, cosine, sine, wq_hbm, wk_hbm, wv_hbm, wo_hbm, mixed_out, moe_out,
     wq, wk, wv, wo, xn, ad, qbuf, kbuf, vbuf, att, score, prob, sems) = refs[13:]
    loads = [pltpu.make_async_copy(src, dst, sems.at[i]) for i, (src, dst) in enumerate(
        [(wk_hbm, wk), (wv_hbm, wv), (wq_hbm, wq), (wo_hbm, wo)])]
    for load in loads:
        load.start()
    count = tok[0].shape[0]
    ends = [place[0], place[1], place[2]]
    me = place[3]

    def document(index):
        return sum((index >= end).astype(jnp.int32) for end in ends)

    def block_start(b):
        return (me - jnp.where(b < 3, 2 * b, 2 * b - 5)) * count

    for j in range(8):
        ad[48 * j:48 * j + 48, :] = adapt[j][...]
    for b in range(5):
        xn[b * count:(b + 1) * count, :] = norm(tok[b][...].astype(F32), gain[...])
    column = lax.broadcasted_iota(jnp.int32, (1, 384), 1)
    col_row = column & 15
    col_prompt = column >> 4
    col_prompt = col_prompt - 3 * ((col_prompt * 171) >> 9)

    def low(z, roll, first, docs):
        moved = pltpu.roll(z, roll, 1)
        keep = (docs == col_prompt) & (col_row >= first) & (col_row < first + 2)
        return jnp.where(keep, moved, 0.0).astype(BF)

    lane = lax.broadcasted_iota(jnp.int32, (count, 128), 1)
    down_rows = lax.broadcasted_iota(jnp.int32, (count, 1), 0)

    def rope(u, cos_t, sin_t):
        lower = (lax.broadcasted_iota(jnp.int32, u.shape, 1) & 63) < 32
        turned = jnp.where(lower, pltpu.roll(u, 96, 1), pltpu.roll(u, 32, 1))
        return u * cos_t + turned * sin_t

    loads[0].wait()
    loads[1].wait()

    def key_block(b, carry):
        size = 5 * count // 2
        at = pl.ds(pl.multiple_of(b * size, 16), size)
        row = b * size + lax.broadcasted_iota(jnp.int32, (size, 1), 0)
        docs = document(block_start(row >> 7) + (row & 127))
        rows = xn[at, :]
        z = dot_t(rows, ad[...])
        keys = jnp.dot(rows, wk[...], preferred_element_type=F32) + jnp.dot(
            low(z, 10, 12, docs), ad[:, :512], preferred_element_type=F32)
        values = jnp.dot(rows, wv[...], preferred_element_type=F32) + jnp.dot(
            low(z, 8, 12, docs), ad[:, 512:1024], preferred_element_type=F32)
        vbuf[at, :] = values.astype(BF)
        cos_t = cosine[at, :]
        sin_t = sine[at, :]
        for c in range(4):
            kbuf[at, 128 * c:128 * c + 128] = rope(
                keys[:, 128 * c:128 * c + 128], cos_t, sin_t).astype(BF)
        return carry

    lax.fori_loop(0, 2, key_block, 0)
    own_index = me * count + down_rows
    docs = document(own_index)
    own = xn[0:count, :]
    zq = low(dot_t(own, ad[...]), 8, 8, docs)
    cos_t = cosine[0:count, :]
    sin_t = sine[0:count, :]
    low_half = lane < 64
    along = lax.broadcasted_iota(jnp.int32, (1, count), 1)
    key_index = jnp.concatenate([block_start(b) + along for b in range(5)], axis=1)
    allowed = ((docs == document(key_index)) & (key_index <= own_index) & (key_index >= 0))
    bias = jnp.where(allowed, 0.0, MASKED)
    loads[2].wait()

    def query_block(c, carry):
        at = pl.multiple_of(c * 384, 128)
        u = jnp.dot(own, wq[:, pl.ds(at, 384)], preferred_element_type=F32) + jnp.dot(
            zq, ad[:, pl.ds(at, 384)], preferred_element_type=F32)
        for t in range(3):
            q = rope(u[:, 128 * t:128 * t + 128], cos_t, sin_t).astype(BF).astype(F32)
            q = q * (HEAD ** -0.5)
            turned = pltpu.roll(q, 64, 1)
            for own_low in (True, False):
                h = 2 * t + (0 if own_low else 1)
                kv_low = h < 3
                rows = q if own_low == kv_low else turned
                keep = low_half if kv_low else ~low_half
                qbuf[c, count * h:count * h + count, :] = jnp.where(keep, rows, 0.0).astype(BF)
        return carry

    lax.fori_loop(0, 4, query_block, 0)

    def pair(j, carry):
        kv = pl.ds(pl.multiple_of(j * 128, 128), 128)
        score[...] = dot_t(qbuf[j], kbuf[:, kv])
        totals = []
        for h in range(6):
            at = slice(count * h, count * h + count)
            s = score[at, :] + bias
            top = jnp.max(s, axis=-1, keepdims=True)
            w = jnp.exp(s - top)
            totals.append(jnp.sum(w, axis=-1, keepdims=True))
            prob[at, :] = w.astype(BF)
        out = jnp.dot(prob[...], vbuf[:, kv], preferred_element_type=F32)
        results = []
        for h in range(6):
            o = out[count * h:count * h + count] / totals[h]
            results.append(pltpu.roll(o, 64, 1) if (h % 2 == 0) != (h < 3) else o)
        for t in range(3):
            att[:, pl.ds(pl.multiple_of(j * 384 + 128 * t, 128), 128)] = jnp.where(
                low_half, results[2 * t], results[2 * t + 1]).astype(BF)
        return carry

    lax.fori_loop(0, 4, pair, 0)
    loads[3].wait()
    attended = att[...]
    zo = low(dot_t(attended, ad[...]), 4, 10, docs)

    def out_block(c, carry):
        at = pl.ds(pl.multiple_of(c * 512, 512), 512)
        mixed_out[:, at] = (
            tok[0][:, at].astype(F32)
            + jnp.dot(attended, wo[:, at], preferred_element_type=F32)
            + jnp.dot(zo, ad[:, at], preferred_element_type=F32)).astype(BF)
        return carry

    lax.fori_loop(0, 3, out_block, 0)
    moe_out[...] = norm(mixed_out[...].astype(F32), gain_moe[...])


def attention(tok, adapt, place, gain, gain_moe, cosine, sine, wq, wk, wv, wo):
    count, width = tok[0].shape
    vm = pl.BlockSpec(memory_space=pltpu.VMEM)
    anywhere = pl.BlockSpec(memory_space=pl.ANY)
    rows = jax.ShapeDtypeStruct((count, width), BF)
    return pl.pallas_call(
        attention_kernel,
        out_shape=(rows, rows),
        in_specs=[vm] * 13 + [pl.BlockSpec(memory_space=pltpu.SMEM)] + [vm] * 4
        + [anywhere] * 4,
        out_specs=(vm, vm),
        scratch_shapes=[
            pltpu.VMEM(wq.shape, BF), pltpu.VMEM(wk.shape, BF), pltpu.VMEM(wv.shape, BF),
            pltpu.VMEM(wo.shape, BF), pltpu.VMEM((5 * count, width), BF),
            pltpu.VMEM((384, width), BF), pltpu.VMEM((4, 6 * count, 128), BF),
            pltpu.VMEM((5 * count, 512), BF), pltpu.VMEM((5 * count, 512), BF),
            pltpu.VMEM((count, width), BF), pltpu.VMEM((6 * count, 5 * count), F32),
            pltpu.VMEM((6 * count, 5 * count), BF), pltpu.SemaphoreType.DMA((4,)),
        ],
        compiler_params=pltpu.CompilerParams(vmem_limit_bytes=ATTENTION_VMEM),
        cost_estimate=pl.CostEstimate(flops=8 << 30, transcendentals=0,
                                      bytes_accessed=20 << 20),
        name="attention_block",
    )(*tok, *adapt, place, gain, gain_moe, cosine, sine, wq, wk, wv, wo)


def expert_kernel(p0, p1, first, table, gate, up, down, out0, out1, last, xe, ho, scale):
    odd, part = first[0], first[1]
    row = lax.broadcasted_iota(jnp.int32, (256, 256), 0)
    col = lax.broadcasted_iota(jnp.int32, (256, 256), 1)
    before = ((row < col) & ((row < 128) == (col < 128))).astype(BF)
    slot = lax.broadcasted_iota(jnp.int32, (2 * CAP, 256), 0).astype(F32)
    base = jnp.where(lax.broadcasted_iota(jnp.int32, (8, 256), 1) < 128, 0.0, float(CAP))

    def places(i):
        named = table[part, i] > 0.0
        rank = jnp.dot(named.astype(F32).astype(BF), before, preferred_element_type=F32) + base
        rank = jnp.where(named, rank, -1.0)
        return [slot == rank[e:e + 1, :] for e in range(3)]

    hots = []
    for i, piece in enumerate((p0, p1)):
        spots = places(i)
        hot = jnp.concatenate([jnp.where(p, 1.0, 0.0) for p in spots]).astype(BF)
        hots.append(hot)
        rows = jnp.dot(hot, piece[...], preferred_element_type=F32).astype(BF)
        given = table[part, i]
        for e in range(3):
            at = slice(i * 2 * CAP, (i + 1) * 2 * CAP)
            xe[e, at, :] = rows[e * 2 * CAP:(e + 1) * 2 * CAP]
            scale[e, at, :] = jnp.sum(jnp.where(spots[e], given[e:e + 1, :], 0.0), axis=1,
                                      keepdims=True)

    def ffn(e, half, count):
        rows = xe[e]
        hidden = []
        for h in range(count):
            g = jnp.dot(rows, gate[half + h], preferred_element_type=F32)
            u = jnp.dot(rows, up[half + h], preferred_element_type=F32)
            hidden.append((g / (1.0 + jnp.exp(-g)) * u).astype(BF))
        hidden = jnp.concatenate(hidden, axis=1)
        maps = down[pl.ds(pl.multiple_of(256 * half, 256), 256 * count), :]
        out = jnp.dot(hidden, maps, preferred_element_type=F32)
        ho[e] = (out * scale[e]).astype(BF)

    def whole(e, carry):
        ffn(e, odd + 2 * e, 2)
        return carry

    lax.fori_loop(0, 2, whole, 0)
    ffn(2, 4 - 4 * odd, 1)
    for i, out in enumerate((out0, out1)):
        rows = jnp.concatenate([ho[e, i * 2 * CAP:(i + 1) * 2 * CAP, :] for e in range(3)])
        total = lax.dot_general(hots[i], rows, (((0,), (0,)), ((), ())),
                                preferred_element_type=F32).astype(BF)
        out[...] = total
        marks = table[part, i][3:6]
        left = lax.broadcasted_iota(jnp.int32, marks.shape, 1) < 128
        marks = jnp.concatenate([jnp.where(left, marks, 0.0), jnp.where(left, 0.0, marks),
                                 jnp.zeros((2, 256), F32)]).astype(BF)
        last[i] = jnp.dot(marks, total, preferred_element_type=F32).astype(BF)


def experts(pieces, first, table, gate, up, down):
    width = gate.shape[1]
    shape = pieces[0].shape
    vm = pl.BlockSpec(memory_space=pltpu.VMEM)
    piece = jax.ShapeDtypeStruct((256, width), BF)
    first_out, second_out, last = pl.pallas_call(
        expert_kernel,
        out_shape=(piece, piece, jax.ShapeDtypeStruct((2, 8, width), BF)),
        in_specs=[vm, vm, pl.BlockSpec(memory_space=pltpu.SMEM), vm, vm, vm, vm],
        out_specs=(vm, vm, vm),
        scratch_shapes=[
            pltpu.VMEM((3, 4 * CAP, width), BF), pltpu.VMEM((3, 4 * CAP, width), BF),
            pltpu.VMEM((3, 4 * CAP, 1), F32),
        ],
        compiler_params=pltpu.CompilerParams(vmem_limit_bytes=24 << 20),
        cost_estimate=pl.CostEstimate(flops=7 << 30, transcendentals=0,
                                      bytes_accessed=12 << 20),
        name="expert_block",
    )(*[rows.reshape(256, width) for rows in pieces], first, table, gate, up,
      down.reshape(5 * 256, width))
    return first_out.reshape(shape), second_out.reshape(shape), last


def rms_scaled(features, scales):
    features = features.astype(F32)
    inverse = lax.rsqrt(jnp.mean(features * features, axis=-1, keepdims=True) + EPSILON)
    return (features * inverse * scales).astype(BF)


def body(tokens, lengths, prompt_adapter, routes, routing_weight, attention_gain, query_weight,
         key_weight, value_weight, output_weight, adapter_down_maps, adapter_up_query_output,
         adapter_up_key_value, expert_gain, gate_weight, up_weight, down_weight, closing_gain,
         vocab_projection):
    own = tokens[0]
    count, width = own.shape
    me, grp = lax.axis_index("seq"), lax.axis_index("grp")

    listing = np.concatenate([np.array([0, 1, 2] if g % 2 == 0 else [1, 2, 0]) + 5 * g // 2
                              for g in range(16)]).astype(np.int32)
    ids, given = routes[0], routing_weight[0]
    table = jnp.sum(jnp.where(ids.T[None] == jnp.asarray(listing)[:, None, None],
                              given.T[None], 0.0), axis=1).reshape(16, 3 * count)
    high = lax.reduce_precision(table, 8, 7)
    low = table - high
    route_rows = jnp.concatenate(
        [high, low, jnp.zeros((16, width - 6 * count), F32)], axis=1).astype(BF)

    ranks = (jnp.arange(16, dtype=jnp.int32)[:, None]
             == 2 * me + jnp.arange(2, dtype=jnp.int32)[None, :]).astype(BF)
    downs = jnp.einsum("rk,pdr->pkd", ranks, adapter_down_maps[:, 0],
                       preferred_element_type=F32).astype(BF).reshape(8, width)
    ups = lax.dynamic_slice_in_dim(adapter_up_query_output[:, 0], 2 * me, 2, 1).reshape(4, width)
    thin = lax.dynamic_slice_in_dim(adapter_up_key_value[:, 0], 2 * me, 2, 1)
    thin = jnp.concatenate([thin[0], thin[1], jnp.zeros((2, width - 1024), BF)], axis=1)
    maps = jnp.concatenate([downs, ups, thin], axis=0)
    ends = jnp.cumsum(lengths[0])
    marks = (ends[:, None] - 1 == me * count + jnp.arange(count, dtype=jnp.int32)[None, :])
    mark_row = jnp.concatenate([marks.reshape(1, 3 * count).astype(BF),
                                jnp.zeros((1, width - 3 * count), BF)], axis=1)
    payload = jnp.concatenate(
        [jnp.broadcast_to(maps[None], (16, 14, width)), route_rows[:, None, :],
         jnp.broadcast_to(mark_row[None], (16, 1, width))], axis=1)
    payload, own = lax.optimization_barrier((payload, own))
    held = lax.all_to_all(payload, "grp", 0, 0, tiled=True)
    back1 = lax.ppermute(own, "seq", [(s, s + 2) for s in range(6)])
    back2 = lax.ppermute(own, "seq", [(s, s + 4) for s in range(4)])
    odd_core = me % 2 == 1
    tok = [own, back1, back2, partner(jnp.where(odd_core, back1, own)),
           partner(jnp.where(odd_core, back2, back1))]

    lens = lengths[0]
    starts = ends - lens
    blocks = me - jnp.array([0, 2, 4, 1, 3], jnp.int32)
    row = jnp.arange(count, dtype=jnp.int32)
    index = (blocks[:, None] * count + row[None, :]).reshape(-1)
    document = jnp.sum((index[:, None] >= ends[None, :]).astype(jnp.int32), axis=1)
    half = HEAD // 2
    frequency = ROPE_BASE ** (-(jnp.arange(128, dtype=jnp.int32) % half).astype(F32) / half)
    sign = jnp.where(jnp.arange(128) % HEAD < half, -1.0, 1.0).astype(F32)
    near = row.astype(F32)[:, None] * frequency[None, :]
    far = (blocks[:, None] * count - starts[None, :]).astype(F32)[:, :, None] * frequency
    near_cos, near_sin = jnp.cos(near)[None], jnp.sin(near)[None]
    far_cos, far_sin = jnp.cos(far), jnp.sin(far)

    def by_document(values):
        docs = document.reshape(5, count, 1)
        return jnp.where(docs == 0, values[:, None, 0], jnp.where(
            docs == 1, values[:, None, 1], values[:, None, 2]))

    far_cos, far_sin = by_document(far_cos), by_document(far_sin)
    cosine = (far_cos * near_cos - far_sin * near_sin).reshape(5 * count, 128)
    sine = ((far_sin * near_cos + far_cos * near_sin) * sign).reshape(5 * count, 128)
    row_index = index[:count]
    place = jnp.concatenate([ends, me[None]]).astype(jnp.int32)
    gain, gain_moe = attention_gain[None], expert_gain[None]
    held, cosine, sine, place, gain, gain_moe = lax.optimization_barrier(
        (held, cosine, sine, place, gain, gain_moe))
    picked = jnp.stack([lax.dynamic_index_in_dim(held, prompt_adapter[0, p], 0, False)
                        for p in range(3)]).reshape(48, width)
    turn = [picked] + [lax.ppermute(picked, "seq", [(s, (s + d) % 8) for s in range(8)])
                       for d in (2, 6, 4)]
    rel = jnp.array([0, 3, 1, 2], jnp.int32)
    first, second = jnp.where(me % 2 == 0, grp % 4, grp // 4), jnp.where(
        me % 2 == 0, grp // 4, grp % 4)
    first, second = (first + rel[None, :]) % 4, (second + rel[:, None]) % 4
    source = jnp.where(me % 2 == 0, second * 4 + first, first * 4 + second).reshape(8, 2)
    source = jnp.concatenate([source[:3], source[5:6], source[3:5], source[6:]]).reshape(16)
    order = (source[:, None] == jnp.arange(16, dtype=jnp.int32)[None, :]).astype(F32)
    route_in = jnp.concatenate(
        [held[:, 14, :3 * count].astype(F32) + held[:, 14, 3 * count:6 * count].astype(F32),
         held[:, 15, :3 * count].astype(F32)], axis=1)
    route_in = jnp.dot(order, route_in, precision=lax.Precision.HIGHEST)
    route_in = route_in.reshape(8, 2, 6, count)
    route_in = jnp.concatenate([route_in, jnp.zeros((8, 2, 2, count), F32)], axis=2)
    route_in = route_in.transpose(0, 2, 1, 3).reshape(4, 2, 8, 2 * count)
    odd = (grp % 2).astype(jnp.int32)
    slot = jnp.arange(8, dtype=jnp.int32)
    which = (slot[None, :] % 3 == jnp.arange(3, dtype=jnp.int32)[:, None]) & (slot[None, :] < 6)
    pairs = order.reshape(8, 2, 16)
    chosen = jnp.where((slot < 3)[None, None, :], pairs[:, 0].T[:, :, None],
                       pairs[:, 1].T[:, :, None])
    spread = jnp.where(which[None, :, None, :], chosen[:, None], 0.0)
    spread = spread.reshape(48, 64).astype(BF)
    weights = (gate_weight, up_weight, down_weight)

    turn, route_in, spread = lax.optimization_barrier((turn, route_in, spread))
    adapt = turn + [partner(piece) for piece in turn]
    mixed, moe_in = attention(tok, adapt, place, gain, gain_moe, cosine, sine, query_weight,
                              key_weight, value_weight, output_weight)

    def share(pieces, which):
        return experts(pieces, jnp.stack([odd, jnp.int32(which)]), route_in, *weights)

    line = lax.optimization_barrier(
        [shift(moe_in, 0, 1), shift(moe_in, 0, -1), shift(moe_in, 0, 2)])
    own_lo, own_hi = jnp.stack([moe_in, line[0]]), jnp.stack([line[1], line[2]])
    minus_lo, plus_hi = shift(own_lo, 1, 1), shift(own_hi, 1, -1)
    minus_hi, plus_lo = shift(own_hi, 1, 1), shift(own_lo, 1, -1)
    own_lo, own_hi, last_own = share([own_lo, own_hi], 0)
    minus_lo, plus_hi, own_lo, own_hi = lax.optimization_barrier(
        (minus_lo, plus_hi, own_lo, own_hi))
    far_lo, far_hi = shift(minus_lo, 1, 1), shift(plus_hi, 1, -1)
    first_lo, first_hi, last_first = share([minus_lo, plus_hi], 1)
    minus_hi, plus_lo, first_lo, first_hi = lax.optimization_barrier(
        (minus_hi, plus_lo, first_lo, first_hi))
    minus_hi, plus_lo, last_second = share([minus_hi, plus_lo], 2)
    minus_lo, plus_hi, minus_hi, plus_lo, far_lo, far_hi = lax.optimization_barrier(
        (first_lo, first_hi, minus_hi, plus_lo, far_lo, far_hi))

    minus_lo, plus_hi = shift(minus_lo, 1, -1), shift(plus_hi, 1, 1)
    far_lo, far_hi, last_far = share([far_lo, far_hi], 3)
    far_lo, far_hi = lax.optimization_barrier((shift(far_lo, 1, 1), shift(far_hi, 1, -1)))
    plus_lo = shift((wide(plus_lo) + wide(far_lo)).astype(BF), 1, 1)
    minus_hi = shift((wide(minus_hi) + wide(far_hi)).astype(BF), 1, -1)
    minus_lo, plus_hi, minus_hi, plus_lo = lax.optimization_barrier(
        (minus_lo, plus_hi, minus_hi, plus_lo))
    own_lo = wide(own_lo) + wide(plus_lo) + wide(minus_lo)
    own_hi = wide(own_hi) + wide(plus_hi) + wide(minus_hi)
    line = lax.optimization_barrier(
        [shift(own_hi[0].astype(BF), 0, 1), shift(own_lo[1].astype(BF), 0, -1),
         shift(own_hi[1].astype(BF), 0, 2)])
    combined = own_lo[0] + wide(line[0]) + wide(line[1]) + wide(line[2])
    hidden_out = (mixed.astype(F32) + combined).astype(BF)

    last = jnp.concatenate([piece.reshape(16, width) for piece in (
        last_own, last_first, last_second, last_far)])
    last = jnp.dot(spread, last, preferred_element_type=F32).astype(BF)
    last = lax.all_to_all(last.reshape(16, 3, width), "grp", 0, 0, tiled=True)
    last = jnp.sum(last.astype(F32), axis=0) + jnp.dot(
        marks.astype(BF), mixed, preferred_element_type=F32)
    last = rms_scaled(last.astype(BF), closing_gain)
    part = width // 8
    split = last.reshape(3, 8, part).transpose(1, 0, 2)
    mine = lax.all_to_all(split, "seq", 0, 0, tiled=True)
    mine = jnp.sum(mine.astype(F32), axis=0).astype(BF)
    everyone = lax.all_to_all(jnp.broadcast_to(mine[None], (128, 3, part)), WHOLE, 0, 0,
                              tiled=True)
    final_rows = everyone.reshape(8, 48, part).transpose(1, 0, 2).reshape(48, width)
    logits = jnp.dot(final_rows, vocab_projection, preferred_element_type=F32)
    top = jnp.max(logits, axis=1)
    mass = jnp.sum(jnp.exp(logits - top[:, None]), axis=1)
    stats = jnp.concatenate([top, mass, jnp.zeros((32,), F32)])
    stats = lax.all_to_all(jnp.broadcast_to(stats[None], (128, 128)), WHOLE, 0, 0, tiled=True)
    tops = stats[:, :48]
    peak = jnp.max(tops, axis=0)
    total = jnp.sum(stats[:, 48:96] * jnp.exp(tops - peak[None]), axis=0)
    log_probs = logits - (peak + jnp.log(total))[:, None]
    return hidden_out[None], log_probs


def solution(mesh):
    placed = (
        P("grp", "seq", None), P("grp", None), P("grp", None), P("grp", "seq", None),
        P("grp", "seq", None), P(), P(), P(), P(), P(), P(None, "grp", None, None),
        P(None, "grp", None, None), P(None, "grp", None, None), P(), P("grp", None, None),
        P("grp", None, None), P("grp", None, None), P(), P(None, WHOLE),
    )
    return jax.shard_map(
        body,
        mesh=mesh,
        in_specs=placed,
        out_specs=(P("grp", "seq", None), P(None, WHOLE)),
        check_vma=False,
    )
```

```python
import jax
import jax.numpy as jnp
import numpy as np
from jax import lax
from jax.experimental import pallas as pl
from jax.experimental.pallas import tpu as pltpu
from jax.sharding import PartitionSpec as P

HEADS = 24
KV_HEADS = 8
HEAD = 64
EXPERTS = 40
TOP = 8
CAP = 40
ATTENTION_VMEM = 63 << 20
EPSILON = 1e-05
ROPE_BASE = 10000.0
MASKED = -1e30
SIDE = 4
BF = jnp.bfloat16
F32 = jnp.float32
WHOLE = ("seq", "grp")


def shift(rows, phase, step):
    pairs = []
    for s in range(8):
        for i in range(16):
            if s % 2 == phase:
                to = i // SIDE * SIDE + (i % SIDE + step) % SIDE
            else:
                to = (i // SIDE + step) % SIDE * SIDE + i % SIDE
            pairs.append((s * 16 + i, s * 16 + to))
    return lax.ppermute(rows, WHOLE, pairs)


def partner(rows):
    return lax.ppermute(rows, "seq", [(s, s ^ 1) for s in range(8)])


def wide(v):
    return v.astype(F32)


def dot_t(lhs, rhs):
    return lax.dot_general(lhs, rhs, (((1,), (1,)), ((), ())), preferred_element_type=F32)


def norm(rows, scale):
    inverse = lax.rsqrt(jnp.mean(rows * rows, axis=-1, keepdims=True) + EPSILON)
    return (rows * inverse * scale).astype(BF)


def attention_kernel(*refs):
    tok = refs[0:5]
    adapt = refs[5:13]
    (place, gain, gain_moe, cosine, sine, wq_hbm, wk_hbm, wv_hbm, wo_hbm, mixed_out, moe_out,
     wq, wk, wv, wo, xn, ad, qbuf, kbuf, vbuf, att, score, prob, sems) = refs[13:]
    loads = [pltpu.make_async_copy(src, dst, sems.at[i]) for i, (src, dst) in enumerate(
        [(wk_hbm, wk), (wv_hbm, wv), (wq_hbm, wq), (wo_hbm, wo)])]
    for load in loads:
        load.start()
    count = tok[0].shape[0]
    ends = [place[0], place[1], place[2]]
    me = place[3]

    def document(index):
        return sum((index >= end).astype(jnp.int32) for end in ends)

    def block_start(b):
        return (me - jnp.where(b < 3, 2 * b, 2 * b - 5)) * count

    for j in range(8):
        ad[48 * j:48 * j + 48, :] = adapt[j][...]
    for b in range(5):
        xn[b * count:(b + 1) * count, :] = norm(tok[b][...].astype(F32), gain[...])
    column = lax.broadcasted_iota(jnp.int32, (1, 384), 1)
    col_row = column & 15
    col_prompt = column >> 4
    col_prompt = col_prompt - 3 * ((col_prompt * 171) >> 9)

    def low(z, roll, first, docs):
        moved = pltpu.roll(z, roll, 1)
        keep = (docs == col_prompt) & (col_row >= first) & (col_row < first + 2)
        return jnp.where(keep, moved, 0.0).astype(BF)

    lane = lax.broadcasted_iota(jnp.int32, (count, 128), 1)
    down_rows = lax.broadcasted_iota(jnp.int32, (count, 1), 0)

    def rope(u, cos_t, sin_t):
        lower = (lax.broadcasted_iota(jnp.int32, u.shape, 1) & 63) < 32
        turned = jnp.where(lower, pltpu.roll(u, 96, 1), pltpu.roll(u, 32, 1))
        return u * cos_t + turned * sin_t

    loads[0].wait()
    loads[1].wait()

    def key_block(b, carry):
        size = 5 * count // 2
        at = pl.ds(pl.multiple_of(b * size, 16), size)
        row = b * size + lax.broadcasted_iota(jnp.int32, (size, 1), 0)
        docs = document(block_start(row >> 7) + (row & 127))
        rows = xn[at, :]
        z = dot_t(rows, ad[...])
        keys = jnp.dot(rows, wk[...], preferred_element_type=F32) + jnp.dot(
            low(z, 10, 12, docs), ad[:, :512], preferred_element_type=F32)
        values = jnp.dot(rows, wv[...], preferred_element_type=F32) + jnp.dot(
            low(z, 8, 12, docs), ad[:, 512:1024], preferred_element_type=F32)
        vbuf[at, :] = values.astype(BF)
        cos_t = cosine[at, :]
        sin_t = sine[at, :]
        for c in range(4):
            kbuf[at, 128 * c:128 * c + 128] = rope(
                keys[:, 128 * c:128 * c + 128], cos_t, sin_t).astype(BF)
        return carry

    lax.fori_loop(0, 2, key_block, 0)
    own_index = me * count + down_rows
    docs = document(own_index)
    own = xn[0:count, :]
    zq = low(dot_t(own, ad[...]), 8, 8, docs)
    cos_t = cosine[0:count, :]
    sin_t = sine[0:count, :]
    low_half = lane < 64
    along = lax.broadcasted_iota(jnp.int32, (1, count), 1)
    key_index = jnp.concatenate([block_start(b) + along for b in range(5)], axis=1)
    allowed = ((docs == document(key_index)) & (key_index <= own_index) & (key_index >= 0))
    bias = jnp.where(allowed, 0.0, MASKED)
    loads[2].wait()

    def query_block(c, carry):
        at = pl.multiple_of(c * 384, 128)
        u = jnp.dot(own, wq[:, pl.ds(at, 384)], preferred_element_type=F32) + jnp.dot(
            zq, ad[:, pl.ds(at, 384)], preferred_element_type=F32)
        for t in range(3):
            q = rope(u[:, 128 * t:128 * t + 128], cos_t, sin_t).astype(BF).astype(F32)
            q = q * (HEAD ** -0.5)
            turned = pltpu.roll(q, 64, 1)
            for own_low in (True, False):
                h = 2 * t + (0 if own_low else 1)
                kv_low = h < 3
                rows = q if own_low == kv_low else turned
                keep = low_half if kv_low else ~low_half
                qbuf[c, count * h:count * h + count, :] = jnp.where(keep, rows, 0.0).astype(BF)
        return carry

    lax.fori_loop(0, 4, query_block, 0)

    def pair(j, carry):
        kv = pl.ds(pl.multiple_of(j * 128, 128), 128)
        score[...] = dot_t(qbuf[j], kbuf[:, kv])
        totals = []
        for h in range(6):
            at = slice(count * h, count * h + count)
            s = score[at, :] + bias
            top = jnp.max(s, axis=-1, keepdims=True)
            w = jnp.exp(s - top)
            totals.append(jnp.sum(w, axis=-1, keepdims=True))
            prob[at, :] = w.astype(BF)
        out = jnp.dot(prob[...], vbuf[:, kv], preferred_element_type=F32)
        results = []
        for h in range(6):
            o = out[count * h:count * h + count] / totals[h]
            results.append(pltpu.roll(o, 64, 1) if (h % 2 == 0) != (h < 3) else o)
        for t in range(3):
            att[:, pl.ds(pl.multiple_of(j * 384 + 128 * t, 128), 128)] = jnp.where(
                low_half, results[2 * t], results[2 * t + 1]).astype(BF)
        return carry

    lax.fori_loop(0, 4, pair, 0)
    loads[3].wait()
    attended = att[...]
    zo = low(dot_t(attended, ad[...]), 4, 10, docs)

    def out_block(c, carry):
        at = pl.ds(pl.multiple_of(c * 512, 512), 512)
        mixed_out[:, at] = (
            tok[0][:, at].astype(F32)
            + jnp.dot(attended, wo[:, at], preferred_element_type=F32)
            + jnp.dot(zo, ad[:, at], preferred_element_type=F32)).astype(BF)
        return carry

    lax.fori_loop(0, 3, out_block, 0)
    moe_out[...] = norm(mixed_out[...].astype(F32), gain_moe[...])


def attention(tok, adapt, place, gain, gain_moe, cosine, sine, wq, wk, wv, wo):
    count, width = tok[0].shape
    vm = pl.BlockSpec(memory_space=pltpu.VMEM)
    anywhere = pl.BlockSpec(memory_space=pl.ANY)
    rows = jax.ShapeDtypeStruct((count, width), BF)
    return pl.pallas_call(
        attention_kernel,
        out_shape=(rows, rows),
        in_specs=[vm] * 13 + [pl.BlockSpec(memory_space=pltpu.SMEM)] + [vm] * 4
        + [anywhere] * 4,
        out_specs=(vm, vm),
        scratch_shapes=[
            pltpu.VMEM(wq.shape, BF), pltpu.VMEM(wk.shape, BF), pltpu.VMEM(wv.shape, BF),
            pltpu.VMEM(wo.shape, BF), pltpu.VMEM((5 * count, width), BF),
            pltpu.VMEM((384, width), BF), pltpu.VMEM((4, 6 * count, 128), BF),
            pltpu.VMEM((5 * count, 512), BF), pltpu.VMEM((5 * count, 512), BF),
            pltpu.VMEM((count, width), BF), pltpu.VMEM((6 * count, 5 * count), F32),
            pltpu.VMEM((6 * count, 5 * count), BF), pltpu.SemaphoreType.DMA((4,)),
        ],
        compiler_params=pltpu.CompilerParams(vmem_limit_bytes=ATTENTION_VMEM),
        cost_estimate=pl.CostEstimate(flops=8 << 30, transcendentals=0,
                                      bytes_accessed=20 << 20),
        name="attention_block",
    )(*tok, *adapt, place, gain, gain_moe, cosine, sine, wq, wk, wv, wo)


def expert_kernel(p0, p1, first, table, gate, up, down, out0, out1, last, xe, ho, scale):
    odd, part = first[0], first[1]
    row = lax.broadcasted_iota(jnp.int32, (256, 256), 0)
    col = lax.broadcasted_iota(jnp.int32, (256, 256), 1)
    before = ((row < col) & ((row < 128) == (col < 128))).astype(BF)
    slot = lax.broadcasted_iota(jnp.int32, (2 * CAP, 256), 0).astype(F32)
    base = jnp.where(lax.broadcasted_iota(jnp.int32, (8, 256), 1) < 128, 0.0, float(CAP))

    def places(i):
        named = table[part, i] > 0.0
        rank = jnp.dot(named.astype(F32).astype(BF), before, preferred_element_type=F32) + base
        rank = jnp.where(named, rank, -1.0)
        return [slot == rank[e:e + 1, :] for e in range(3)]

    hots = []
    for i, piece in enumerate((p0, p1)):
        spots = places(i)
        hot = jnp.concatenate([jnp.where(p, 1.0, 0.0) for p in spots]).astype(BF)
        hots.append(hot)
        rows = jnp.dot(hot, piece[...], preferred_element_type=F32).astype(BF)
        given = table[part, i]
        for e in range(3):
            at = slice(i * 2 * CAP, (i + 1) * 2 * CAP)
            xe[e, at, :] = rows[e * 2 * CAP:(e + 1) * 2 * CAP]
            scale[e, at, :] = jnp.sum(jnp.where(spots[e], given[e:e + 1, :], 0.0), axis=1,
                                      keepdims=True)

    def ffn(e, half, count):
        rows = xe[e]
        hidden = []
        for h in range(count):
            g = jnp.dot(rows, gate[half + h], preferred_element_type=F32)
            u = jnp.dot(rows, up[half + h], preferred_element_type=F32)
            hidden.append((g / (1.0 + jnp.exp(-g)) * u).astype(BF))
        hidden = jnp.concatenate(hidden, axis=1)
        maps = down[pl.ds(pl.multiple_of(256 * half, 256), 256 * count), :]
        out = jnp.dot(hidden, maps, preferred_element_type=F32)
        ho[e] = (out * scale[e]).astype(BF)

    def whole(e, carry):
        ffn(e, odd + 2 * e, 2)
        return carry

    lax.fori_loop(0, 2, whole, 0)
    ffn(2, 4 - 4 * odd, 1)
    for i, out in enumerate((out0, out1)):
        rows = jnp.concatenate([ho[e, i * 2 * CAP:(i + 1) * 2 * CAP, :] for e in range(3)])
        total = lax.dot_general(hots[i], rows, (((0,), (0,)), ((), ())),
                                preferred_element_type=F32).astype(BF)
        out[...] = total
        marks = table[part, i][3:6]
        left = lax.broadcasted_iota(jnp.int32, marks.shape, 1) < 128
        marks = jnp.concatenate([jnp.where(left, marks, 0.0), jnp.where(left, 0.0, marks),
                                 jnp.zeros((2, 256), F32)]).astype(BF)
        last[i] = jnp.dot(marks, total, preferred_element_type=F32).astype(BF)


def experts(pieces, first, table, gate, up, down):
    width = gate.shape[1]
    shape = pieces[0].shape
    vm = pl.BlockSpec(memory_space=pltpu.VMEM)
    piece = jax.ShapeDtypeStruct((256, width), BF)
    first_out, second_out, last = pl.pallas_call(
        expert_kernel,
        out_shape=(piece, piece, jax.ShapeDtypeStruct((2, 8, width), BF)),
        in_specs=[vm, vm, pl.BlockSpec(memory_space=pltpu.SMEM), vm, vm, vm, vm],
        out_specs=(vm, vm, vm),
        scratch_shapes=[
            pltpu.VMEM((3, 4 * CAP, width), BF), pltpu.VMEM((3, 4 * CAP, width), BF),
            pltpu.VMEM((3, 4 * CAP, 1), F32),
        ],
        compiler_params=pltpu.CompilerParams(vmem_limit_bytes=24 << 20),
        cost_estimate=pl.CostEstimate(flops=7 << 30, transcendentals=0,
                                      bytes_accessed=12 << 20),
        name="expert_block",
    )(*[rows.reshape(256, width) for rows in pieces], first, table, gate, up,
      down.reshape(5 * 256, width))
    return first_out.reshape(shape), second_out.reshape(shape), last


def rms_scaled(features, scales):
    features = features.astype(F32)
    inverse = lax.rsqrt(jnp.mean(features * features, axis=-1, keepdims=True) + EPSILON)
    return (features * inverse * scales).astype(BF)


def body(tokens, lengths, prompt_adapter, routes, routing_weight, attention_gain, query_weight,
         key_weight, value_weight, output_weight, adapter_down_maps, adapter_up_query_output,
         adapter_up_key_value, expert_gain, gate_weight, up_weight, down_weight, closing_gain,
         vocab_projection):
    own = tokens[0]
    count, width = own.shape
    me, grp = lax.axis_index("seq"), lax.axis_index("grp")

    listing = np.concatenate([np.array([0, 1, 2] if g % 2 == 0 else [1, 2, 0]) + 5 * g // 2
                              for g in range(16)]).astype(np.int32)
    ids, given = routes[0], routing_weight[0]
    table = jnp.sum(jnp.where(ids.T[None] == jnp.asarray(listing)[:, None, None],
                              given.T[None], 0.0), axis=1).reshape(16, 3 * count)
    high = lax.reduce_precision(table, 8, 7)
    low = table - high
    route_rows = jnp.concatenate(
        [high, low, jnp.zeros((16, width - 6 * count), F32)], axis=1).astype(BF)

    ranks = (jnp.arange(16, dtype=jnp.int32)[:, None]
             == 2 * me + jnp.arange(2, dtype=jnp.int32)[None, :]).astype(BF)
    downs = jnp.einsum("rk,pdr->pkd", ranks, adapter_down_maps[:, 0],
                       preferred_element_type=F32).astype(BF).reshape(8, width)
    ups = lax.dynamic_slice_in_dim(adapter_up_query_output[:, 0], 2 * me, 2, 1).reshape(4, width)
    thin = lax.dynamic_slice_in_dim(adapter_up_key_value[:, 0], 2 * me, 2, 1)
    thin = jnp.concatenate([thin[0], thin[1], jnp.zeros((2, width - 1024), BF)], axis=1)
    maps = jnp.concatenate([downs, ups, thin], axis=0)
    ends = jnp.cumsum(lengths[0])
    marks = (ends[:, None] - 1 == me * count + jnp.arange(count, dtype=jnp.int32)[None, :])
    mark_row = jnp.concatenate([marks.reshape(1, 3 * count).astype(BF),
                                jnp.zeros((1, width - 3 * count), BF)], axis=1)
    payload = jnp.concatenate(
        [jnp.broadcast_to(maps[None], (16, 14, width)), route_rows[:, None, :],
         jnp.broadcast_to(mark_row[None], (16, 1, width))], axis=1)
    payload, own = lax.optimization_barrier((payload, own))
    held = lax.all_to_all(payload, "grp", 0, 0, tiled=True)
    back1 = lax.ppermute(own, "seq", [(s, s + 2) for s in range(6)])
    back2 = lax.ppermute(own, "seq", [(s, s + 4) for s in range(4)])
    odd_core = me % 2 == 1
    tok = [own, back1, back2, partner(jnp.where(odd_core, back1, own)),
           partner(jnp.where(odd_core, back2, back1))]

    lens = lengths[0]
    starts = ends - lens
    blocks = me - jnp.array([0, 2, 4, 1, 3], jnp.int32)
    row = jnp.arange(count, dtype=jnp.int32)
    index = (blocks[:, None] * count + row[None, :]).reshape(-1)
    document = jnp.sum((index[:, None] >= ends[None, :]).astype(jnp.int32), axis=1)
    half = HEAD // 2
    frequency = ROPE_BASE ** (-(jnp.arange(128, dtype=jnp.int32) % half).astype(F32) / half)
    sign = jnp.where(jnp.arange(128) % HEAD < half, -1.0, 1.0).astype(F32)
    near = row.astype(F32)[:, None] * frequency[None, :]
    far = (blocks[:, None] * count - starts[None, :]).astype(F32)[:, :, None] * frequency
    near_cos, near_sin = jnp.cos(near)[None], jnp.sin(near)[None]
    far_cos, far_sin = jnp.cos(far), jnp.sin(far)

    def by_document(values):
        docs = document.reshape(5, count, 1)
        return jnp.where(docs == 0, values[:, None, 0], jnp.where(
            docs == 1, values[:, None, 1], values[:, None, 2]))

    far_cos, far_sin = by_document(far_cos), by_document(far_sin)
    cosine = (far_cos * near_cos - far_sin * near_sin).reshape(5 * count, 128)
    sine = ((far_sin * near_cos + far_cos * near_sin) * sign).reshape(5 * count, 128)
    row_index = index[:count]
    place = jnp.concatenate([ends, me[None]]).astype(jnp.int32)
    gain, gain_moe = attention_gain[None], expert_gain[None]
    held, cosine, sine, place, gain, gain_moe = lax.optimization_barrier(
        (held, cosine, sine, place, gain, gain_moe))
    picked = jnp.stack([lax.dynamic_index_in_dim(held, prompt_adapter[0, p], 0, False)
                        for p in range(3)]).reshape(48, width)
    turn = [picked] + [lax.ppermute(picked, "seq", [(s, (s + d) % 8) for s in range(8)])
                       for d in (2, 6, 4)]
    rel = jnp.array([0, 3, 1, 2], jnp.int32)
    first, second = jnp.where(me % 2 == 0, grp % 4, grp // 4), jnp.where(
        me % 2 == 0, grp // 4, grp % 4)
    first, second = (first + rel[None, :]) % 4, (second + rel[:, None]) % 4
    source = jnp.where(me % 2 == 0, second * 4 + first, first * 4 + second).reshape(8, 2)
    source = jnp.concatenate([source[:3], source[5:6], source[3:5], source[6:]]).reshape(16)
    order = (source[:, None] == jnp.arange(16, dtype=jnp.int32)[None, :]).astype(F32)
    route_in = jnp.concatenate(
        [held[:, 14, :3 * count].astype(F32) + held[:, 14, 3 * count:6 * count].astype(F32),
         held[:, 15, :3 * count].astype(F32)], axis=1)
    route_in = jnp.dot(order, route_in, precision=lax.Precision.HIGHEST)
    route_in = route_in.reshape(8, 2, 6, count)
    route_in = jnp.concatenate([route_in, jnp.zeros((8, 2, 2, count), F32)], axis=2)
    route_in = route_in.transpose(0, 2, 1, 3).reshape(4, 2, 8, 2 * count)
    odd = (grp % 2).astype(jnp.int32)
    slot = jnp.arange(8, dtype=jnp.int32)
    which = (slot[None, :] % 3 == jnp.arange(3, dtype=jnp.int32)[:, None]) & (slot[None, :] < 6)
    pairs = order.reshape(8, 2, 16)
    chosen = jnp.where((slot < 3)[None, None, :], pairs[:, 0].T[:, :, None],
                       pairs[:, 1].T[:, :, None])
    spread = jnp.where(which[None, :, None, :], chosen[:, None], 0.0)
    spread = spread.reshape(48, 64).astype(BF)
    weights = (gate_weight, up_weight, down_weight)

    turn, route_in, spread = lax.optimization_barrier((turn, route_in, spread))
    adapt = turn + [partner(piece) for piece in turn]
    mixed, moe_in = attention(tok, adapt, place, gain, gain_moe, cosine, sine, query_weight,
                              key_weight, value_weight, output_weight)

    def share(pieces, which):
        return experts(pieces, jnp.stack([odd, jnp.int32(which)]), route_in, *weights)

    line = lax.optimization_barrier(
        [shift(moe_in, 0, 1), shift(moe_in, 0, -1), shift(moe_in, 0, 2)])
    own_lo = jnp.concatenate([moe_in, line[0]])
    own_hi = jnp.concatenate([line[1], line[2]])
    minus_lo, plus_hi = shift(own_lo, 1, 1), shift(own_hi, 1, -1)
    minus_hi, plus_lo = shift(own_hi, 1, 1), shift(own_lo, 1, -1)
    own_lo, own_hi, last_own = share([own_lo, own_hi], 0)
    minus_lo, plus_hi, own_lo, own_hi = lax.optimization_barrier(
        (minus_lo, plus_hi, own_lo, own_hi))
    far_lo, far_hi = shift(minus_lo, 1, 1), shift(plus_hi, 1, -1)
    first_lo, first_hi, last_first = share([minus_lo, plus_hi], 1)
    minus_hi, plus_lo, first_lo, first_hi = lax.optimization_barrier(
        (minus_hi, plus_lo, first_lo, first_hi))
    minus_hi, plus_lo, last_second = share([minus_hi, plus_lo], 2)
    minus_lo, plus_hi, minus_hi, plus_lo, far_lo, far_hi = lax.optimization_barrier(
        (first_lo, first_hi, minus_hi, plus_lo, far_lo, far_hi))

    minus_lo, plus_hi = shift(minus_lo, 1, -1), shift(plus_hi, 1, 1)
    far_lo, far_hi, last_far = share([far_lo, far_hi], 3)
    far_lo, far_hi = lax.optimization_barrier((shift(far_lo, 1, 1), shift(far_hi, 1, -1)))
    plus_lo = shift((wide(plus_lo) + wide(far_lo)).astype(BF), 1, 1)
    minus_hi = shift((wide(minus_hi) + wide(far_hi)).astype(BF), 1, -1)
    minus_lo, plus_hi, minus_hi, plus_lo = lax.optimization_barrier(
        (minus_lo, plus_hi, minus_hi, plus_lo))
    own_lo = wide(own_lo) + wide(plus_lo) + wide(minus_lo)
    own_hi = wide(own_hi) + wide(plus_hi) + wide(minus_hi)
    line = lax.optimization_barrier(
        [shift(own_hi[:count].astype(BF), 0, 1), shift(own_lo[count:].astype(BF), 0, -1),
         shift(own_hi[count:].astype(BF), 0, 2)])
    combined = own_lo[:count] + wide(line[0]) + wide(line[1]) + wide(line[2])
    hidden_out = (mixed.astype(F32) + combined).astype(BF)

    last = jnp.concatenate([piece.reshape(16, width) for piece in (
        last_own, last_first, last_second, last_far)])
    last = jnp.dot(spread, last, preferred_element_type=F32).astype(BF)
    last = lax.all_to_all(last.reshape(16, 3, width), "grp", 0, 0, tiled=True)
    last = jnp.sum(last.astype(F32), axis=0) + jnp.dot(
        marks.astype(BF), mixed, preferred_element_type=F32)
    last = rms_scaled(last.astype(BF), closing_gain)
    part = width // 8
    split = last.reshape(3, 8, part).transpose(1, 0, 2)
    mine = lax.all_to_all(split, "seq", 0, 0, tiled=True)
    mine = jnp.sum(mine.astype(F32), axis=0).astype(BF)
    everyone = lax.all_to_all(jnp.broadcast_to(mine[None], (128, 3, part)), WHOLE, 0, 0,
                              tiled=True)
    final_rows = everyone.reshape(8, 48, part).transpose(1, 0, 2).reshape(48, width)
    logits = jnp.dot(final_rows, vocab_projection, preferred_element_type=F32)
    top = jnp.max(logits, axis=1)
    mass = jnp.sum(jnp.exp(logits - top[:, None]), axis=1)
    stats = jnp.concatenate([top, mass, jnp.zeros((32,), F32)])
    stats = lax.all_to_all(jnp.broadcast_to(stats[None], (128, 128)), WHOLE, 0, 0, tiled=True)
    tops = stats[:, :48]
    peak = jnp.max(tops, axis=0)
    total = jnp.sum(stats[:, 48:96] * jnp.exp(tops - peak[None]), axis=0)
    log_probs = logits - (peak + jnp.log(total))[:, None]
    return hidden_out[None], log_probs


def solution(mesh):
    placed = (
        P("grp", "seq", None), P("grp", None), P("grp", None), P("grp", "seq", None),
        P("grp", "seq", None), P(), P(), P(), P(), P(), P(None, "grp", None, None),
        P(None, "grp", None, None), P(None, "grp", None, None), P(), P("grp", None, None),
        P("grp", None, None), P("grp", None, None), P(), P(None, WHOLE),
    )
    return jax.shard_map(
        body,
        mesh=mesh,
        in_specs=placed,
        out_specs=(P("grp", "seq", None), P(None, WHOLE)),
        check_vma=False,
    )
```
